256 devices in a mesh: row: 8 (over y, core), col: 32 (over x, z).
Axes of the slice: x: 4, y: 4, z: 8, core: 2. Of those that a mesh axis runs over, the one named last changes fastest.
Arguments:
- adjoint: bfloat16 [16384, 16384], P('row', 'col'), may hold values from -1 to 1, as said below
- taper: int32 [64, 64], replicated, may hold values from 0 to 1, as said below
- panel_two: bfloat16 [16384, 1024], P(('row', 'col')), may hold values from -6 to 6
- panel_one: bfloat16 [16384, 1024], P(('row', 'col')), may hold values from -6 to 6
- incoming: float32 [16384, 1024], P('col', 'row'), may hold values from -6 to 6
- inverse_factor: bfloat16 [1024, 1024], P('row'), may hold values from -1 to 1, as said below
Outputs:
- second_grad: float32 [16384, 1024], P('col', 'row')
- first_grad: float32 [16384, 1024], P('col', 'row')
The draws below stay inside these ranges and needn't reach their ends.
Inputs may be any that keep to these rules, and one draw needn't show every extreme that they name: `taper`: symmetric in its two indices; every entry with |a - b| <= 1 is 1. `adjoint`: symmetric. `inverse_factor`: lower triangular with a positive diagonal.
All inputs are finite; a program needn't handle non-finite values.
Results may differ from the reference program's by a relative error of at most 0.0025.
Values may be sent and summed in bfloat16 or wider, within the bound.
No kernel may reach another device: no remote copies, remote signals or barrier semaphores. Data moves between devices by JAX's collectives and lax.ppermute only.
A program may use at most 64 MiB of HBM per device.

```python
import math
import jax
import jax.numpy as jnp
from jax import lax

BLK = 256
W = 1024
RL = 2048
N = 16384
NT = 64
N_ROW = 8


def draw_adjoint(key, part):
    base_draw = jax.random.normal(jax.random.fold_in(key, 11), (N, N), jnp.float32)
    paired = (base_draw + base_draw.T) * 0.5 ** 0.5
    return jnp.clip(paired * N ** (-0.5), -1.0, 1.0).astype(jnp.bfloat16)


def draw_taper(key, part):
    region_count = 16
    region_level = jax.random.randint(jax.random.fold_in(key, 21), (region_count,), 0, 4)
    tile_index = jnp.arange(NT, dtype=jnp.int32)
    tile_region = tile_index * region_count // NT
    tile_level = region_level[tile_region]
    pair_level = tile_level[:, None] + tile_level[None, :]
    coin_toss = jax.random.randint(jax.random.fold_in(key, 22), (NT, NT), 0, 8)
    kept_tile = (coin_toss <= pair_level).astype(jnp.int32)
    upper_half = tile_index[:, None] <= tile_index[None, :]
    symmetric = jnp.where(upper_half, kept_tile, kept_tile.T)
    near_band = jnp.abs(tile_index[:, None] - tile_index[None, :]) <= 1
    return jnp.where(near_band, 1, symmetric).astype(jnp.int32)


def draw_inverse_factor(key, part):
    diag_scale = jnp.exp(jax.random.uniform(jax.random.fold_in(key, 31), (W,), jnp.float32, math.log(0.5), math.log(2.0)))
    off_part = jax.random.normal(jax.random.fold_in(key, 32), (W, W), jnp.float32)
    line_index = jnp.arange(W, dtype=jnp.int32)
    below = line_index[:, None] > line_index[None, :]
    on_diag = line_index[:, None] == line_index[None, :]
    lower_part = jnp.where(below, off_part / W, 0.0)
    return (lower_part + jnp.where(on_diag, diag_scale[:, None] * W ** (-0.5), 0.0)).astype(jnp.bfloat16)


def shard_levels(stream_key, shape, shards, low, top_value):
    def one(position, shards_of):
        draws = jax.random.uniform(jax.random.fold_in(jax.random.fold_in(stream_key, 6), position), (shards_of,), jnp.float32, low / len(shards), top_value / len(shards))
        return jnp.repeat(jnp.exp(draws), shape[position] // shards_of).reshape((-1,) + (1,) * (len(shape) - position - 1))

    level = one(*shards[0])
    for cut in shards[1:]:
        level = level * one(*cut)
    return level


def normal_values(stream_key, extent, deviation, bound, split=(), kind=jnp.bfloat16):
    values = deviation * jax.random.normal(stream_key, extent, jnp.float32)
    if split:
        values = values * shard_levels(stream_key, extent, split, -0.22, 0.18)
    return jnp.clip(values, -bound, bound).astype(kind)


def setup_inputs(seed: int = 0) -> dict:
    key_of = jax.random.split(jax.random.key(seed), 7)
    return {
        "adjoint": draw_adjoint(jax.random.fold_in(key_of[6], 71), 0),
        "taper": draw_taper(jax.random.fold_in(key_of[6], 71), 0),
        "panel_two": normal_values(key_of[2], (N, W), 1.0, 6.0, ((0, 256),)),
        "panel_one": normal_values(key_of[3], (N, W), 1.0, 6.0, ((0, 256),)),
        "incoming": normal_values(key_of[4], (N, W), 1.0, 6.0, ((0, 32), (1, 8)), jnp.float32),
        "inverse_factor": draw_inverse_factor(jax.random.fold_in(key_of[6], 71), 0),
    }


def reference(adjoint, taper, panel_two, panel_one, incoming, inverse_factor):
    panels = jnp.concatenate([panel_two, panel_one], axis=1).astype(jnp.float32)

    def one_group(group):
        row_start = group * RL
        slab_rows = lax.dynamic_slice_in_dim(adjoint, row_start, RL, 0)
        mask_rows = lax.dynamic_slice_in_dim(taper, group * (RL // BLK), RL // BLK, 0).astype(jnp.float32)
        shaped = slab_rows.reshape(RL // BLK, BLK, NT, BLK)
        masked_rows = (shaped.astype(jnp.float32) * mask_rows[:, None, :, None]).astype(jnp.bfloat16).reshape(RL, N)

        def one_block(block):
            cols = lax.dynamic_slice_in_dim(masked_rows, block * 512, 512, 1).astype(jnp.float32)
            rows = lax.dynamic_slice_in_dim(panels, block * 512, 512, 0)
            return jnp.dot(cols, rows, precision=lax.Precision.HIGHEST)

        def add_block(total, block):
            return total + one_block(block), None

        if N % 512 == 0:
            total, _ = lax.scan(add_block, jnp.zeros((RL, 2 * W), jnp.float32), jnp.arange(N // 512, dtype=jnp.int32))
            return total
        return jnp.dot(masked_rows.astype(jnp.float32), panels, precision=lax.Precision.HIGHEST)

    products = lax.map(one_group, jnp.arange(N_ROW, dtype=jnp.int32)).reshape(N, 2 * W)
    second_grad = incoming - 2.0 * products[:, :W]
    second_rounded = second_grad.astype(jnp.bfloat16)
    carried = jnp.dot(second_rounded, inverse_factor, preferred_element_type=jnp.float32)
    diagonal_rows = panel_one[:W].astype(jnp.float32)
    carried_term = jnp.dot(carried, diagonal_rows, precision=lax.Precision.HIGHEST)
    first_grad = -2.0 * products[:, W:] - carried_term
    return second_grad, first_grad
```

```python
import functools

import jax
import jax.numpy as jnp
from jax import lax
from jax.experimental import pallas as pl
from jax.experimental.pallas import tpu as pltpu
from jax.sharding import PartitionSpec as P

BLK = 256
NX, NZ, NY = 4, 8, 4
SUB = 64
XOFF = (0, -1, 1, 2)
ZOFF = (0, -1, 1, -2, 2, -3, 3, 4)
F32, BF16 = jnp.float32, jnp.bfloat16
VMEM = pl.BlockSpec(memory_space=pltpu.VMEM)
SMEM = pl.BlockSpec(memory_space=pltpu.SMEM)
BIG = pltpu.CompilerParams(vmem_limit_bytes=40 * 2**20)


def x_shift(value, dx):
    pairs = [(x * NZ + z, (x + dx) % NX * NZ + z) for x in range(NX) for z in range(NZ)]
    return lax.ppermute(value, "col", pairs)


def z_shift(value, dz):
    pairs = [(x * NZ + z, x * NZ + (z + dz) % NZ) for x in range(NX) for z in range(NZ)]
    return lax.ppermute(value, "col", pairs)


def y_shift(value, dy):
    pairs = [(y * 2 + k, (y + dy) % NY * 2 + k) for y in range(NY) for k in range(2)]
    return lax.ppermute(value, "row", pairs)


def core_swap(value):
    return lax.ppermute(value, "row", [(r, r ^ 1) for r in range(2 * NY)])


def x_all(value):
    return [value, x_shift(value, 1), x_shift(value, -1), x_shift(value, 2)]


def z_ring(value, turn):
    down1, up1 = z_shift(value, 1), z_shift(value, -1)
    down2, up2 = z_shift(down1, 1), z_shift(up1, -1)
    down3, up3 = z_shift(down2, 1), z_shift(up2, -1)
    far = z_shift(down3, 1) if turn > 0 else z_shift(up3, -1)
    return [value, down1, up1, down2, up2, down3, up3, far]


def gather_xz(part):
    return z_ring(jnp.concatenate(x_all(part), axis=0), 1)


def gather_zx(part):
    return x_all(jnp.concatenate(z_ring(part, -1), axis=0))


def piece_row(pos, i, j):
    x = (pos[0] + XOFF[i] + NX) % NX
    z = (pos[1] + ZOFF[j] + NZ) % NZ
    return x, z


def prepare_kernel(pos, taper, adjoint, by_z, by_x, rows_z, rows_x):
    lane = lax.broadcasted_iota(jnp.int32, (SUB, 2 * BLK), 1)
    first_tile = (pos[2] * 2 + pos[3]) * 8
    first_col = (pos[0] * NZ + pos[1]) * 2
    for j in range(NZ):
        for i in range(NX):
            x, z = piece_row(pos, i, j)
            tile = first_tile + x * 2 + z // 4
            left = taper[tile, first_col].astype(F32)
            right = taper[tile, first_col + 1].astype(F32)
            keep = jnp.where(lane < BLK, left, right)
            row = pl.multiple_of((x * NZ + z) * SUB, SUB)
            part = (adjoint[pl.ds(row, SUB), :].astype(F32) * keep).astype(BF16)
            rows_z[(j * NX + i) * SUB:(j * NX + i + 1) * SUB, :] = part
            rows_x[(i * NZ + j) * SUB:(i * NZ + j + 1) * SUB, :] = part
    for j in range(NZ):
        by_z[j] = rows_z[j * 256:(j + 1) * 256, :].T
    for i in range(NX):
        by_x[i] = rows_x[i * 512:(i + 1) * 512, :].T


def prepare(pos, taper, adjoint):
    return pl.pallas_call(
        prepare_kernel,
        out_shape=(
            jax.ShapeDtypeStruct((NZ, 512, 256), BF16),
            jax.ShapeDtypeStruct((NX, 512, 512), BF16),
        ),
        in_specs=[SMEM, SMEM, VMEM],
        out_specs=(VMEM, VMEM),
        scratch_shapes=[pltpu.VMEM((2048, 512), BF16), pltpu.VMEM((2048, 512), BF16)],
        compiler_params=BIG,
        name="prepare_adjoint",
    )(pos, taper, adjoint)


def product_kernel(pos, by_z, by_x, *refs):
    from_z, from_x, give, keep = refs[:NZ], refs[NZ:NZ + NX], refs[-2], refs[-1]
    first = pos[3] == 0
    for p in range(NY):
        if p < 2:
            total = sum(
                jnp.dot(by_z[j], from_z[j][:, p * 256:(p + 1) * 256], preferred_element_type=F32)
                for j in range(NZ)
            )
        else:
            q = p - 2
            total = sum(
                jnp.dot(by_x[i], from_x[i][:, q * 256:(q + 1) * 256], preferred_element_type=F32)
                for i in range(NX)
            )
        total = -2.0 * total
        left, right = total[:, :128], total[:, 128:]
        keep[p] = jnp.where(first, left, right)
        give[p] = jnp.where(first, right, left).astype(give.dtype)


def product(pos, by_z, by_x, from_z, from_x):
    return pl.pallas_call(
        product_kernel,
        out_shape=(
            jax.ShapeDtypeStruct((NY, 512, 128), F32),
            jax.ShapeDtypeStruct((NY, 512, 128), F32),
        ),
        in_specs=[SMEM] + [VMEM] * (2 + NZ + NX),
        out_specs=(VMEM, VMEM),
        compiler_params=BIG,
        name="masked_product",
    )(pos, by_z, by_x, *from_z, *from_x)


def split_kernel(pos, keep, other, own, one, two, three):
    y = pos[2]
    own[...] = keep[y] + other[y]
    for d, out in ((1, one), (2, two), (3, three)):
        t = (y + d) % NY
        out[...] = (keep[t] + other[t]).astype(out.dtype)


def split(pos, keep, other, kind):
    return pl.pallas_call(
        split_kernel,
        out_shape=(jax.ShapeDtypeStruct((512, 128), F32),) + (jax.ShapeDtypeStruct((512, 128), kind),) * 3,
        in_specs=[SMEM, VMEM, VMEM],
        out_specs=(VMEM,) * 4,
        compiler_params=BIG,
        name="split_by_y",
    )(pos, keep, other)


def reduce_rows(pos, give, keep, kind):
    own, one, two, three = split(pos, keep, core_swap(give), kind)
    return own, y_shift(one, 1), y_shift(two, 2), y_shift(three, 3)


def factor_kernel(pos, inverse, *refs):
    blocks, out, diagonal = refs[:NZ], refs[NZ], refs[NZ + 1]
    for j in range(NZ):
        for i in range(NX):
            x, z = piece_row(pos, i, j)
            row = pl.multiple_of((x * NZ + z) * SUB, SUB)
            diagonal[pl.ds(row, SUB), :] = blocks[j][i * SUB:(i + 1) * SUB, 512:640]
    value = jnp.dot(inverse[...], diagonal[:1024, :], preferred_element_type=F32)
    high = value.astype(BF16)
    out[:, :128] = high
    out[:, 128:] = (value - high.astype(F32)).astype(BF16)


def factor(pos, inverse, blocks):
    return pl.pallas_call(
        factor_kernel,
        out_shape=jax.ShapeDtypeStruct((1024, 256), BF16),
        in_specs=[SMEM] + [VMEM] * (1 + NZ),
        out_specs=VMEM,
        scratch_shapes=[pltpu.VMEM((2048, 128), BF16)],
        compiler_params=BIG,
        name="inverse_times_diagonal",
    )(pos, inverse, *blocks)


def carried_kernel(pos, mine, other, factors, out):
    first = pos[3] == 0
    total = None
    for d in range(NY):
        y = (pos[2] - d + NY) % NY
        a, b = mine[d], other[d]
        pair = jnp.concatenate([jnp.where(first, a, b), jnp.where(first, b, a)], axis=1)
        rows = pl.multiple_of(y * 256, 256)
        term = jnp.dot(pair, factors[pl.ds(rows, 256), :], preferred_element_type=F32)
        total = term if total is None else total + term
    out[...] = total[:, :128] + total[:, 128:]


def carried(pos, mine, other, factors):
    return pl.pallas_call(
        carried_kernel,
        out_shape=jax.ShapeDtypeStruct((512, 128), F32),
        in_specs=[SMEM] + [VMEM] * 3,
        out_specs=VMEM,
        compiler_params=BIG,
        name="carried_term",
    )(pos, mine, other, factors)


def local(adjoint, taper, panel_two, panel_one, incoming, inverse_factor):
    row, col = lax.axis_index("row"), lax.axis_index("col")
    pos = jnp.stack([col // NZ, col % NZ, row // 2, row % 2]).astype(jnp.int32)

    inverse = lax.all_gather(inverse_factor, "row", axis=0, tiled=True)
    diagonal = lax.all_to_all(panel_one.reshape(SUB, 8, 128), "row", 1, 0, tiled=True)
    diagonal = diagonal.reshape(8, SUB, 128)[0]

    two_z = gather_xz(panel_two[:, :512])
    two_x = gather_zx(panel_two[:, 512:])
    by_z, by_x = prepare(pos, taper, adjoint)
    one_z = gather_xz(jnp.concatenate([panel_one[:, :512], diagonal], axis=1))
    one_x = gather_zx(panel_one[:, 512:])

    give, keep = product(pos, by_z, by_x, two_z, two_x)
    own, r1, r2, r3 = reduce_rows(pos, give, keep, F32)
    second_grad = incoming + ((own + r1) + (r2 + r3))
    rounded = second_grad.astype(BF16)
    mine = jnp.stack([rounded, y_shift(rounded, 1), y_shift(rounded, 2), y_shift(rounded, 3)])
    other = core_swap(mine)

    factors = factor(pos, inverse, one_z)
    give, keep = product(pos, by_z, by_x, one_z, one_x)
    own, r1, r2, r3 = reduce_rows(pos, give, keep, BF16)
    term = carried(pos, mine, other, factors)
    first_grad = ((own + r1.astype(F32)) + (r2.astype(F32) + r3.astype(F32))) - term
    return second_grad, first_grad


def solution(mesh):
    in_specs = (
        P("row", "col"),
        P(),
        P(("row", "col"), None),
        P(("row", "col"), None),
        P("col", "row"),
        P("row", None),
    )
    out_specs = (P("col", "row"), P("col", "row"))
    return jax.shard_map(local, mesh=mesh, in_specs=in_specs, out_specs=out_specs, check_vma=False)
```

```python
import jax
import jax.numpy as jnp
from jax import lax
from jax.experimental import pallas as pl
from jax.experimental.pallas import tpu as pltpu
from jax.sharding import PartitionSpec as P

BLK = 256
NX, NZ, NY = 4, 8, 4
SUB = 64
PAIR = 2 * SUB
HALF = 512
F32, BF16 = jnp.float32, jnp.bfloat16
VMEM = pl.BlockSpec(memory_space=pltpu.VMEM)
SMEM = pl.BlockSpec(memory_space=pltpu.SMEM)
ANY = pl.BlockSpec(memory_space=pl.ANY)
BIG = pltpu.CompilerParams(vmem_limit_bytes=40 * 2**20)


def shift(value, core, dx, dz):
    pairs = []
    for y in range(NY):
        row = y * 2 + core
        for x in range(NX):
            for z in range(NZ):
                target = (x + dx) % NX * NZ + (z + dz) % NZ
                pairs.append((row * NX * NZ + x * NZ + z, row * NX * NZ + target))
    return lax.ppermute(value, ("row", "col"), pairs)


def y_shift(value, dy):
    pairs = [(y * 2 + k, (y + dy) % NY * 2 + k) for y in range(NY) for k in range(2)]
    return lax.ppermute(value, "row", pairs)


def core_swap(value):
    return lax.ppermute(value, "row", [(r, r ^ 1) for r in range(2 * NY)])


def x_all(value, core):
    return [value] + [shift(value, core, d, 0) for d in (1, -1, 2)]


def z_ring(value, core, turn):
    down1, up1 = shift(value, core, 0, 1), shift(value, core, 0, -1)
    down2, up2 = shift(down1, core, 0, 1), shift(up1, core, 0, -1)
    down3, up3 = shift(down2, core, 0, 1), shift(up2, core, 0, -1)
    far = shift(down3, core, 0, 1) if turn > 0 else shift(up3, core, 0, -1)
    return [value, down1, up1, down2, up2, down3, up3, far]


def offset(n):
    return ((n + 1) // 2) * (1 - 2 * (n % 2))


def source(pos, b, t):
    first = pos[3] == 0
    i = jnp.where(first, t, b // 2)
    j = jnp.where(first, b, b % 2 * 4 + t)
    return (pos[0] + offset(i) + NX) % NX, (pos[1] + offset(j) + NZ) % NZ


def pack_kernel(pos, two, one, own, give):
    first = pos[3] == 0
    for n, panel in enumerate((two, one)):
        for q in range(NY):
            left = panel[:, q * 256:q * 256 + 128]
            right = panel[:, q * 256 + 128:q * 256 + 256]
            at = slice(q * 128, q * 128 + 128)
            own[n, :, at] = jnp.where(first, left, right)
            give[n, :, at] = jnp.where(first, right, left)


def pack(pos, two, one):
    return pl.pallas_call(
        pack_kernel,
        out_shape=(jax.ShapeDtypeStruct((2, SUB, HALF), BF16),) * 2,
        in_specs=[SMEM, VMEM, VMEM],
        out_specs=(VMEM, VMEM),
        compiler_params=BIG,
        name="pack_columns",
    )(pos, two, one)


def diagonal_shard_kernel(pos, own, taken, gathered, out):
    out[:SUB] = own[1]
    out[SUB:PAIR] = taken[1]
    column = pl.multiple_of(pos[2] * 128, 128)
    for q in range(NY):
        out[PAIR:, q * 128:(q + 1) * 128] = gathered[q * 16:(q + 1) * 16, pl.ds(column, 128)]


def diagonal_shard(pos, own, taken, gathered):
    return pl.pallas_call(
        diagonal_shard_kernel,
        out_shape=jax.ShapeDtypeStruct((PAIR + 16, HALF), BF16),
        in_specs=[SMEM] + [VMEM] * 3,
        out_specs=VMEM,
        compiler_params=BIG,
        name="shard_with_diagonal",
    )(pos, own, taken, gathered)


def join(pos, parts, core, extra):
    count = len(parts)

    def kernel(pos, *refs):
        out, sems = refs[count], refs[count + 1]

        @pl.when(pos[3] == core)
        def _():
            copies = []
            for n in range(count):
                copies.append(pltpu.make_async_copy(
                    refs[n].at[:PAIR], out.at[pl.ds(n * PAIR, PAIR)], sems.at[n]))
                if extra:
                    copies.append(pltpu.make_async_copy(
                        refs[n].at[PAIR:], out.at[pl.ds(count * PAIR + n * 16, 16)], sems.at[count + n]))
            for copy in copies:
                copy.start()
            for copy in copies:
                copy.wait()

    rows = count * (PAIR + (16 if extra else 0))
    return pl.pallas_call(
        kernel,
        out_shape=jax.ShapeDtypeStruct((rows, HALF), BF16),
        in_specs=[SMEM] + [ANY] * count,
        out_specs=ANY,
        scratch_shapes=[pltpu.SemaphoreType.DMA((2 * count,))],
        name="join_parts",
    )(pos, *parts)


def gather(pos, shard, extra):
    by_z = z_ring(join(pos, x_all(shard, 0), 0, extra), 0, 1)
    by_x = x_all(join(pos, z_ring(shard, 1, -1), 1, extra), 1)
    return by_z + by_x


def prepare_kernel(pos, taper, mine, other, out, rows):
    lane = lax.broadcasted_iota(jnp.int32, (SUB, 2 * BLK), 1)
    first_col = (pos[0] * NZ + pos[1]) * 2

    def block(b, carry):
        for t in range(4):
            x, z = source(pos, b, t)
            row = pl.multiple_of((x * NZ + z) * SUB, SUB)
            for h, ref in enumerate((mine, other)):
                core = pos[3] if h == 0 else 1 - pos[3]
                tile = (pos[2] * 2 + core) * 8 + x * 2 + z // 4
                left = taper[tile, first_col].astype(F32)
                right = taper[tile, first_col + 1].astype(F32)
                keep = jnp.where(lane < BLK, left, right)
                at = t * PAIR + h * SUB
                rows[at:at + SUB, :] = (ref[pl.ds(row, SUB), :].astype(F32) * keep).astype(BF16)
        out[b] = rows[...].T
        return carry

    lax.fori_loop(0, 8, block, 0)


def prepare(pos, taper, mine, other):
    return pl.pallas_call(
        prepare_kernel,
        out_shape=jax.ShapeDtypeStruct((8, 512, 512), BF16),
        in_specs=[SMEM, SMEM, VMEM, VMEM],
        out_specs=VMEM,
        scratch_shapes=[pltpu.VMEM((512, 512), BF16)],
        compiler_params=BIG,
        name="prepare_adjoint",
    )(pos, taper, mine, other)


def block_refs(refs, core, first_row, rows, width):
    if core == 0:
        return [refs[b].at[pl.ds(first_row, rows)] for b in range(NZ)]
    return [
        refs[NZ + b // 2].at[pl.ds(2 * first_row + b % 2 * rows, rows)] for b in range(NZ)
    ]


def load_blocks(pos, refs, held, sems, first_row, rows):
    for core in range(2):
        @pl.when(pos[3] == core)
        def _(core=core):
            for b, ref in enumerate(block_refs(refs, core, first_row, rows, HALF)):
                pltpu.make_async_copy(ref, held.at[b], sems.at[b]).start()


def product_kernel(pos, adjoint, *refs):
    panels, outs, held, total, sems = refs[:12], refs[12:16], refs[16], refs[17], refs[18]
    load_blocks(pos, panels, held, sems, 0, 512)
    total[...] = jnp.zeros_like(total)

    def block(b, carry):
        pltpu.make_async_copy(held.at[b], held.at[b], sems.at[b]).wait()
        total[...] += jnp.dot(adjoint[b], held[b], preferred_element_type=F32)
        return carry

    lax.fori_loop(0, 8, block, 0)
    for d, out in enumerate(outs):
        column = pl.multiple_of((pos[2] + d) % NY * 128, 128)
        out[...] = (-2.0 * total[:, pl.ds(column, 128)]).astype(out.dtype)


def product(pos, adjoint, panels, kind):
    return pl.pallas_call(
        product_kernel,
        out_shape=(jax.ShapeDtypeStruct((512, 128), F32),) + (jax.ShapeDtypeStruct((512, 128), kind),) * 3,
        in_specs=[SMEM, VMEM] + [ANY] * 12,
        out_specs=(VMEM,) * 4,
        scratch_shapes=[
            pltpu.VMEM((8, 512, HALF), BF16),
            pltpu.VMEM((512, HALF), F32),
            pltpu.SemaphoreType.DMA((8,)),
        ],
        compiler_params=BIG,
        name="masked_product",
    )(pos, adjoint, *panels)


def factor_kernel(pos, inverse, *refs):
    panels, out, held, diagonal, sems = refs[:12], refs[12], refs[13], refs[14], refs[15]
    load_blocks(pos, panels, held, sems, 512, 64)

    def block(b, carry):
        pltpu.make_async_copy(held.at[b], held.at[b], sems.at[b]).wait()
        for t in range(4):
            x, z = source(pos, b, t)
            row = (x * NZ + z) * SUB
            for q in range(NY):
                at = pl.multiple_of(row + q * 16, 16)
                diagonal[pl.ds(at, 16), :] = held[b, t * 16:(t + 1) * 16, q * 128:(q + 1) * 128]
        return carry

    lax.fori_loop(0, 8, block, 0)
    value = jnp.dot(inverse[...], diagonal[:1024, :], preferred_element_type=F32)
    high = value.astype(BF16)
    out[:, :128] = high
    out[:, 128:] = (value - high.astype(F32)).astype(BF16)


def factor(pos, inverse, panels):
    return pl.pallas_call(
        factor_kernel,
        out_shape=jax.ShapeDtypeStruct((1024, 256), BF16),
        in_specs=[SMEM, VMEM] + [ANY] * 12,
        out_specs=VMEM,
        scratch_shapes=[
            pltpu.VMEM((8, 64, HALF), BF16),
            pltpu.VMEM((2048, 128), BF16),
            pltpu.SemaphoreType.DMA((8,)),
        ],
        compiler_params=BIG,
        name="inverse_times_diagonal",
    )(pos, inverse, *panels)


def carried_kernel(pos, mine, other, factors, out, total):
    first = pos[3] == 0
    total[...] = jnp.zeros_like(total)

    def block(d, carry):
        y = (pos[2] - d + NY) % NY
        a, b = mine[d], other[d]
        pair = jnp.concatenate([jnp.where(first, a, b), jnp.where(first, b, a)], axis=1)
        rows = pl.multiple_of(y * 256, 256)
        total[...] += jnp.dot(pair, factors[pl.ds(rows, 256), :], preferred_element_type=F32)
        return carry

    lax.fori_loop(0, NY, block, 0)
    out[...] = total[:, :128] + total[:, 128:]


def carried(pos, mine, other, factors):
    return pl.pallas_call(
        carried_kernel,
        out_shape=jax.ShapeDtypeStruct((512, 128), F32),
        in_specs=[SMEM] + [VMEM] * 3,
        out_specs=VMEM,
        scratch_shapes=[pltpu.VMEM((512, 256), F32)],
        compiler_params=BIG,
        name="carried_term",
    )(pos, mine, other, factors)


def after(value, *others):
    return lax.optimization_barrier((value,) + others)[0]


def local(adjoint, taper, panel_two, panel_one, incoming, inverse_factor):
    row, col = lax.axis_index("row"), lax.axis_index("col")
    pos = jnp.stack([col // NZ, col % NZ, row // 2, row % 2]).astype(jnp.int32)

    own, give = pack(pos, panel_two, panel_one)
    taken = core_swap(give)
    same_core = [[2 * y + k for y in range(NY)] for k in range(2)]
    top = jnp.where(pos[3] == 0, own[1], taken[1])
    diagonal = lax.all_gather(top, "row", axis_index_groups=same_core, axis=0, tiled=True)
    inverse = lax.all_gather(after(inverse_factor, diagonal), "row", axis=0, tiled=True)

    two = gather(pos, jnp.concatenate([own[0], taken[0]], axis=0), False)
    one = gather(pos, diagonal_shard(pos, own, taken, diagonal), True)
    masked = prepare(pos, taper, adjoint, core_swap(adjoint))

    mine, *sent = product(pos, masked, two, F32)
    r1, r2, r3 = [y_shift(part, d + 1) for d, part in enumerate(sent)]
    second_grad = incoming + ((mine + r1) + (r2 + r3))
    rounded = second_grad.astype(BF16)
    column = jnp.stack([rounded, y_shift(rounded, 1), y_shift(rounded, 2), y_shift(rounded, 3)])
    other = core_swap(column)

    factors = factor(pos, inverse, one)
    mine, *sent = product(pos, masked, one, BF16)
    r1, r2, r3 = [y_shift(part, d + 1) for d, part in enumerate(sent)]
    term = carried(pos, column, other, factors)
    first_grad = ((mine + r1.astype(F32)) + (r2.astype(F32) + r3.astype(F32))) - term
    return second_grad, first_grad


def solution(mesh):
    in_specs = (
        P("row", "col"),
        P(),
        P(("row", "col"), None),
        P(("row", "col"), None),
        P("col", "row"),
        P("row", None),
    )
    out_specs = (P("col", "row"), P("col", "row"))
    return jax.shard_map(local, mesh=mesh, in_specs=in_specs, out_specs=out_specs, check_vma=False)
```

```python
import functools

import jax
import jax.numpy as jnp
from jax import lax
from jax.experimental import pallas as pl
from jax.experimental.pallas import tpu as pltpu
from jax.sharding import PartitionSpec as P

BLK = 256
NX, NZ, NY = 4, 8, 4
SUB = 64
PAIR = 2 * SUB
HALF = 512
F32, BF16 = jnp.float32, jnp.bfloat16
VMEM = pl.BlockSpec(memory_space=pltpu.VMEM)
SMEM = pl.BlockSpec(memory_space=pltpu.SMEM)
ANY = pl.BlockSpec(memory_space=pl.ANY)
BIG = pltpu.CompilerParams(vmem_limit_bytes=40 * 2**20)


def x_shift(value, dx):
    pairs = [(x * NZ + z, (x + dx) % NX * NZ + z) for x in range(NX) for z in range(NZ)]
    return lax.ppermute(value, "col", pairs)


def z_shift(value, dz):
    pairs = [(x * NZ + z, x * NZ + (z + dz) % NZ) for x in range(NX) for z in range(NZ)]
    return lax.ppermute(value, "col", pairs)


def y_shift(value, dy):
    pairs = [(y * 2 + k, (y + dy) % NY * 2 + k) for y in range(NY) for k in range(2)]
    return lax.ppermute(value, "row", pairs)


def y_first(value, y):
    return lax.ppermute(value, "row", [(k, y * 2 + k) for k in range(2)])


def core_swap(value):
    return lax.ppermute(value, "row", [(r, r ^ 1) for r in range(2 * NY)])


def gather_xz(part):
    block = jnp.concatenate([part] + [x_shift(part, d) for d in (1, -1, 2)], axis=0)
    down1, up1 = z_shift(block, 1), z_shift(block, -1)
    down2, up2 = z_shift(down1, 1), z_shift(up1, -1)
    down3, up3 = z_shift(down2, 1), z_shift(up2, -1)
    return [block, down1, up1, down2, up2, down3, up3, z_shift(down3, 1)]


def after(value, *others):
    return lax.optimization_barrier((value,) + others)[0]


def gather_zx(part, earlier):
    same_x = [[x * NZ + z for z in range(NZ)] for x in range(NX)]
    block = lax.all_gather(part, "col", axis_index_groups=same_x, axis=0, tiled=True)
    block = after(block, earlier)
    down, up = x_shift(block, 1), x_shift(block, -1)
    return [block, down, up, x_shift(down[:HALF], 1), x_shift(up[HALF:], -1)]


def offset(n):
    return ((n + 1) // 2) * (1 - 2 * (n % 2))


def source_xz(pos, b, t):
    return (pos[0] + offset(t) + NX) % NX, (pos[1] + offset(b) + NZ) % NZ


def source_zx(pos, b, t):
    return (pos[0] + offset(b // 2) + NX) % NX, b % 2 * 4 + t


def pack_kernel(pos, two, one, own, give):
    first = pos[3] == 0
    for n, panel in enumerate((two, one)):
        for q in range(NY):
            left = panel[:, q * 256:q * 256 + 128]
            right = panel[:, q * 256 + 128:q * 256 + 256]
            at = slice(q * 128, q * 128 + 128)
            own[n, :, at] = jnp.where(first, left, right)
            give[n, :, at] = jnp.where(first, right, left)


def pack(pos, two, one):
    return pl.pallas_call(
        pack_kernel,
        out_shape=(jax.ShapeDtypeStruct((2, SUB, HALF), BF16),) * 2,
        in_specs=[SMEM, VMEM, VMEM],
        out_specs=(VMEM, VMEM),
        compiler_params=BIG,
        name="pack_columns",
    )(pos, two, one)


def prepare_kernel(pos, taper, mine, other, for_two, for_one, rows):
    lane = lax.broadcasted_iota(jnp.int32, (SUB, 2 * BLK), 1)
    first_col = (pos[0] * NZ + pos[1]) * 2

    for out, source in ((for_two, source_xz), (for_one, source_zx)):
        def block(b, carry, out=out, source=source):
            for t in range(4):
                x, z = source(pos, b, t)
                row = pl.multiple_of((x * NZ + z) * SUB, SUB)
                for h, ref in enumerate((mine, other)):
                    core = pos[3] if h == 0 else 1 - pos[3]
                    tile = (pos[2] * 2 + core) * 8 + x * 2 + z // 4
                    left = taper[tile, first_col].astype(F32)
                    right = taper[tile, first_col + 1].astype(F32)
                    keep = jnp.where(lane < BLK, left, right)
                    at = t * PAIR + h * SUB
                    rows[at:at + SUB, :] = (ref[pl.ds(row, SUB), :].astype(F32) * keep).astype(BF16)
            out[b] = rows[...].T
            return carry

        lax.fori_loop(0, 8, block, 0)


def prepare(pos, taper, mine, other):
    return pl.pallas_call(
        prepare_kernel,
        out_shape=(jax.ShapeDtypeStruct((8, 512, 512), BF16),) * 2,
        in_specs=[SMEM, SMEM, VMEM, VMEM],
        out_specs=(VMEM, VMEM),
        scratch_shapes=[pltpu.VMEM((512, 512), BF16)],
        compiler_params=BIG,
        name="prepare_adjoint",
    )(pos, taper, mine, other)


def windows(refs):
    if len(refs) == 8:
        return list(refs)
    halves = [ref.at[pl.ds(h * HALF, HALF)] for ref in refs[:3] for h in range(2)]
    return halves + list(refs[3:])


def product_kernel(count, pos, adjoint, *refs):
    panels, outs, held, total, sems = refs[:count], refs[count:count + 4], refs[-3], refs[-2], refs[-1]
    copies = [
        pltpu.make_async_copy(ref, held.at[b], sems.at[b]) for b, ref in enumerate(windows(panels))
    ]
    for copy in copies:
        copy.start()
    total[...] = jnp.zeros_like(total)

    def block(b, carry):
        pltpu.make_async_copy(held.at[b], held.at[b], sems.at[b]).wait()
        total[...] += jnp.dot(adjoint[b], held[b], preferred_element_type=F32)
        return carry

    lax.fori_loop(0, 8, block, 0)
    for d, out in enumerate(outs):
        column = pl.multiple_of((pos[2] + d) % NY * 128, 128)
        out[...] = (-2.0 * total[:, pl.ds(column, 128)]).astype(out.dtype)


def product(pos, adjoint, panels, kind):
    count = len(panels)
    return pl.pallas_call(
        functools.partial(product_kernel, count),
        out_shape=(jax.ShapeDtypeStruct((512, 128), F32),) + (jax.ShapeDtypeStruct((512, 128), kind),) * 3,
        in_specs=[SMEM, VMEM] + [ANY] * count,
        out_specs=(VMEM,) * 4,
        scratch_shapes=[
            pltpu.VMEM((8, 512, HALF), BF16),
            pltpu.VMEM((512, HALF), F32),
            pltpu.SemaphoreType.DMA((8,)),
        ],
        compiler_params=BIG,
        name="masked_product",
    )(pos, adjoint, *panels)


def diagonal_kernel(pos, block, down, up, far_low, far_high, own, one, two, three, held, sems):
    panels = (block, down, up, far_low, far_high)
    copies = [
        pltpu.make_async_copy(ref, held.at[b], sems.at[b]) for b, ref in enumerate(windows(panels))
    ]
    for copy in copies:
        copy.start()
    half = jnp.where(pos[3] == 0, 0, SUB)

    def fill(b, carry):
        pltpu.make_async_copy(held.at[b], held.at[b], sems.at[b]).wait()
        x, z = source_zx(pos, b, 0)

        @pl.when(x < 2)
        def _():
            for t in range(4):
                from_row = pl.multiple_of(half + t * PAIR, SUB)
                to_row = pl.multiple_of((x * NZ + z + t) * SUB, SUB)
                for d, out in enumerate((own, one, two, three)):
                    out[pl.ds(to_row, SUB), :] = held[b, pl.ds(from_row, SUB), d * 128:(d + 1) * 128]
        return carry

    lax.fori_loop(0, 8, fill, 0)


def diagonal(pos, panels):
    return pl.pallas_call(
        diagonal_kernel,
        out_shape=(jax.ShapeDtypeStruct((1024, 128), BF16),) * 4,
        in_specs=[SMEM] + [ANY] * 5,
        out_specs=(VMEM,) * 4,
        scratch_shapes=[pltpu.VMEM((8, 512, HALF), BF16), pltpu.SemaphoreType.DMA((8,))],
        compiler_params=BIG,
        name="diagonal_columns",
    )(pos, *panels)


def factor_kernel(pos, inverse, own, one, two, three, out):
    sent = (one[...] + two[...]) + three[...]
    columns = jnp.where(pos[2] == 0, own[...], sent)
    value = jnp.dot(inverse[...], columns, preferred_element_type=F32)
    high = value.astype(BF16)
    out[:, :128] = high
    out[:, 128:] = (value - high.astype(F32)).astype(BF16)


def factor(pos, inverse, parts):
    return pl.pallas_call(
        factor_kernel,
        out_shape=jax.ShapeDtypeStruct((1024, 256), BF16),
        in_specs=[SMEM] + [VMEM] * 5,
        out_specs=VMEM,
        compiler_params=BIG,
        name="inverse_times_diagonal",
    )(pos, inverse, *parts)


def carried_kernel(pos, mine, other, factors, out, total):
    first = pos[3] == 0
    total[...] = jnp.zeros_like(total)

    def block(d, carry):
        y = (pos[2] - d + NY) % NY
        a, b = mine[d], other[d]
        pair = jnp.concatenate([jnp.where(first, a, b), jnp.where(first, b, a)], axis=1)
        rows = pl.multiple_of(y * 256, 256)
        total[...] += jnp.dot(pair, factors[pl.ds(rows, 256), :], preferred_element_type=F32)
        return carry

    lax.fori_loop(0, NY, block, 0)
    out[...] = total[:, :128] + total[:, 128:]


def carried(pos, mine, other, factors):
    return pl.pallas_call(
        carried_kernel,
        out_shape=jax.ShapeDtypeStruct((512, 128), F32),
        in_specs=[SMEM] + [VMEM] * 3,
        out_specs=VMEM,
        scratch_shapes=[pltpu.VMEM((512, 256), F32)],
        compiler_params=BIG,
        name="carried_term",
    )(pos, mine, other, factors)


def local(adjoint, taper, panel_two, panel_one, incoming, inverse_factor):
    row, col = lax.axis_index("row"), lax.axis_index("col")
    pos = jnp.stack([col // NZ, col % NZ, row // 2, row % 2]).astype(jnp.int32)

    own, give = pack(pos, panel_two, panel_one)
    taken = core_swap(give)
    shards = jnp.concatenate([own, taken], axis=1)
    two = gather_xz(shards[0])
    one = gather_zx(shards[1], two[4])
    inverse = lax.all_gather(after(inverse_factor, two[4]), "row", axis=0, tiled=True)
    masked_two, masked_one = prepare(pos, taper, adjoint, core_swap(adjoint))

    mine, *sent = product(pos, masked_two, two, F32)
    r1, r2, r3 = [y_shift(part, d + 1) for d, part in enumerate(sent)]
    second_grad = incoming + ((mine + r1) + (r2 + r3))
    rounded = second_grad.astype(BF16)
    column = jnp.stack([rounded, y_shift(rounded, 1), y_shift(rounded, 2), y_shift(rounded, 3)])
    other = core_swap(column)

    mine, *sent = product(pos, masked_one, one, BF16)
    r1, r2, r3 = [y_shift(part, d + 1) for d, part in enumerate(sent)]
    first, *rest = diagonal(pos, one)
    factors = factor(pos, inverse, [first] + [y_first(part, d + 1) for d, part in enumerate(rest)])
    term = carried(pos, column, other, factors)
    first_grad = ((mine + r1.astype(F32)) + (r2.astype(F32) + r3.astype(F32))) - term
    return second_grad, first_grad


def solution(mesh):
    in_specs = (
        P("row", "col"),
        P(),
        P(("row", "col"), None),
        P(("row", "col"), None),
        P("col", "row"),
        P("row", None),
    )
    out_specs = (P("col", "row"), P("col", "row"))
    return jax.shard_map(local, mesh=mesh, in_specs=in_specs, out_specs=out_specs, check_vma=False)
```

```python
import functools

import jax
import jax.numpy as jnp
from jax import lax
from jax.experimental import pallas as pl
from jax.experimental.pallas import tpu as pltpu
from jax.sharding import PartitionSpec as P

BLK = 256
NX, NZ, NY = 4, 8, 4
SAME_CORE = [[2 * y + k for y in range(NY)] for k in range(2)]
SAME_X = [[x * NZ + z for z in range(NZ)] for x in range(NX)]
SUB = 64
PAIR = 2 * SUB
HALF = 512
F32, BF16 = jnp.float32, jnp.bfloat16
VMEM = pl.BlockSpec(memory_space=pltpu.VMEM)
SMEM = pl.BlockSpec(memory_space=pltpu.SMEM)
ANY = pl.BlockSpec(memory_space=pl.ANY)
BIG = pltpu.CompilerParams(vmem_limit_bytes=24 * 2**20)
SMALL = pltpu.CompilerParams(vmem_limit_bytes=12 * 2**20)


def x_shift(value, dx):
    pairs = [(x * NZ + z, (x + dx) % NX * NZ + z) for x in range(NX) for z in range(NZ)]
    return lax.ppermute(value, "col", pairs)


def z_shift(value, dz):
    pairs = [(x * NZ + z, x * NZ + (z + dz) % NZ) for x in range(NX) for z in range(NZ)]
    return lax.ppermute(value, "col", pairs)


def y_shift(value, dy):
    pairs = [(y * 2 + k, (y + dy) % NY * 2 + k) for y in range(NY) for k in range(2)]
    return lax.ppermute(value, "row", pairs)


def y_first(value, y):
    return lax.ppermute(value, "row", [(k, y * 2 + k) for k in range(2)])


def core_swap(value):
    return lax.ppermute(value, "row", [(r, r ^ 1) for r in range(2 * NY)])


def together(*values):
    return lax.optimization_barrier(values)


def y_exchange(value):
    return lax.all_to_all(value, "row", 0, 0, axis_index_groups=SAME_CORE, tiled=True)


def offset(n):
    return ((n + 1) // 2) * (1 - 2 * (n % 2))


def source_xz(pos, b, t):
    return (pos[0] + offset(t) + NX) % NX, (pos[1] + offset(b) + NZ) % NZ


def source_zx(pos, b, t):
    return (pos[0] + offset(b // 2) + NX) % NX, b % 2 * 4 + t


def pack_kernel(pos, two, one, own, give):
    first = pos[3] == 0
    for n, panel in enumerate((two, one)):
        for q in range(NY):
            left = panel[:, q * 256:q * 256 + 128]
            right = panel[:, q * 256 + 128:q * 256 + 256]
            at = slice(q * 128, q * 128 + 128)
            own[n, :, at] = jnp.where(first, left, right)
            give[n, :, at] = jnp.where(first, right, left)


def pack(pos, two, one):
    return pl.pallas_call(
        pack_kernel,
        out_shape=(jax.ShapeDtypeStruct((2, SUB, HALF), BF16),) * 2,
        in_specs=[SMEM, VMEM, VMEM],
        out_specs=(VMEM, VMEM),
        compiler_params=SMALL,
        name="pack_columns",
    )(pos, two, one)


def prepare_kernel(pos, taper, mine, other, for_two, for_one, rows):
    lane = lax.broadcasted_iota(jnp.int32, (SUB, 2 * BLK), 1)
    first_col = (pos[0] * NZ + pos[1]) * 2

    for out, source in ((for_two, source_xz), (for_one, source_zx)):
        def block(b, carry, out=out, source=source):
            for t in range(4):
                x, z = source(pos, b, t)
                row = pl.multiple_of((x * NZ + z) * SUB, SUB)
                for h, ref in enumerate((mine, other)):
                    core = pos[3] if h == 0 else 1 - pos[3]
                    tile = (pos[2] * 2 + core) * 8 + x * 2 + z // 4
                    left = taper[tile, first_col].astype(F32)
                    right = taper[tile, first_col + 1].astype(F32)
                    keep = jnp.where(lane < BLK, left, right)
                    at = t * PAIR + h * SUB
                    rows[at:at + SUB, :] = (ref[pl.ds(row, SUB), :].astype(F32) * keep).astype(BF16)
            out[b] = rows[...].T
            return carry

        lax.fori_loop(0, 8, block, 0)


def prepare(pos, taper, mine, other):
    return pl.pallas_call(
        prepare_kernel,
        out_shape=(jax.ShapeDtypeStruct((8, 512, 512), BF16),) * 2,
        in_specs=[SMEM, SMEM, VMEM, VMEM],
        out_specs=(VMEM, VMEM),
        scratch_shapes=[pltpu.VMEM((512, 512), BF16)],
        compiler_params=BIG,
        name="prepare_adjoint",
    )(pos, taper, mine, other)


def windows(refs):
    return [ref.at[pl.ds(h * HALF, HALF)] for ref in refs for h in range(ref.shape[0] // HALF)]


def product_kernel(count, first_block, scale, pos, adjoint, *refs):
    panels = refs[:count]
    held, sems = refs[-2], refs[-1]
    total = refs[-3]
    copies, rows = [], 0
    for n, ref in enumerate(panels):
        size = ref.shape[0]
        copies.append(pltpu.make_async_copy(ref, held.at[pl.ds(rows, size)], sems.at[n]))
        rows += size
    for copy in copies:
        copy.start()
    if first_block == 0:
        total[...] = jnp.zeros_like(total)
    else:
        total[...] = refs[count][...]
    for copy in copies:
        copy.wait()

    def block(b, carry):
        at = pl.multiple_of(b * HALF, HALF)
        total[...] += jnp.dot(
            adjoint[first_block + b], held[pl.ds(at, HALF), :], preferred_element_type=F32)
        return carry

    lax.fori_loop(0, rows // HALF, block, 0)
    if scale is not None:
        out = refs[count + 1]
        for t in range(NY):
            out[t] = (scale * total[:, t * 128:(t + 1) * 128]).astype(out.dtype)


def product(pos, adjoint, panels, first_block, before=None, kind=None):
    count = len(panels)
    rows = sum(panel.shape[0] for panel in panels)
    last = kind is not None
    scratch = [pltpu.VMEM((rows, HALF), BF16), pltpu.SemaphoreType.DMA((count,))]
    if last:
        scratch = [pltpu.VMEM((512, HALF), F32)] + scratch
        shape = jax.ShapeDtypeStruct((NY, 512, 128), kind)
    else:
        shape = jax.ShapeDtypeStruct((512, HALF), F32)
    extra = [] if before is None else [before]
    return pl.pallas_call(
        functools.partial(product_kernel, count, first_block, -2.0 if last else None),
        out_shape=shape,
        in_specs=[SMEM, VMEM] + [ANY] * count + [VMEM] * len(extra),
        out_specs=VMEM,
        scratch_shapes=scratch,
        compiler_params=SMALL,
        name="masked_product",
    )(pos, adjoint, *panels, *extra)


def diagonal_kernel(pos, block, down, up, far_low, far_high, own, one, two, three, held, sems):
    panels = (block, down, up, far_low, far_high)
    copies = [
        pltpu.make_async_copy(ref, held.at[b], sems.at[b]) for b, ref in enumerate(windows(panels))
    ]
    for copy in copies:
        copy.start()
    half = jnp.where(pos[3] == 0, 0, SUB)

    def fill(b, carry):
        pltpu.make_async_copy(held.at[b], held.at[b], sems.at[b]).wait()
        x, z = source_zx(pos, b, 0)

        @pl.when(x < 2)
        def _():
            for t in range(4):
                from_row = pl.multiple_of(half + t * PAIR, SUB)
                to_row = pl.multiple_of((x * NZ + z + t) * SUB, SUB)
                for d, out in enumerate((own, one, two, three)):
                    out[pl.ds(to_row, SUB), :] = held[b, pl.ds(from_row, SUB), d * 128:(d + 1) * 128]
        return carry

    lax.fori_loop(0, 8, fill, 0)


def diagonal(pos, panels):
    return pl.pallas_call(
        diagonal_kernel,
        out_shape=(jax.ShapeDtypeStruct((1024, 128), BF16),) * 4,
        in_specs=[SMEM] + [ANY] * 5,
        out_specs=(VMEM,) * 4,
        scratch_shapes=[pltpu.VMEM((8, 512, HALF), BF16), pltpu.SemaphoreType.DMA((8,))],
        compiler_params=SMALL,
        name="diagonal_columns",
    )(pos, *panels)


def factor_kernel(pos, inverse, own, one, two, three, out):
    sent = (one[...] + two[...]) + three[...]
    columns = jnp.where(pos[2] == 0, own[...], sent)
    value = jnp.dot(inverse[...], columns, preferred_element_type=F32)
    high = value.astype(BF16)
    out[:, :128] = high
    out[:, 128:] = (value - high.astype(F32)).astype(BF16)


def factor(pos, inverse, parts):
    return pl.pallas_call(
        factor_kernel,
        out_shape=jax.ShapeDtypeStruct((1024, 256), BF16),
        in_specs=[SMEM] + [VMEM] * 5,
        out_specs=VMEM,
        compiler_params=SMALL,
        name="inverse_times_diagonal",
    )(pos, inverse, *parts)


def carried_kernel(pos, mine, other, factors, out, total):
    first = pos[3] == 0
    total[...] = jnp.zeros_like(total)

    def block(y, carry):
        a, b = mine[y], other[y]
        pair = jnp.concatenate([jnp.where(first, a, b), jnp.where(first, b, a)], axis=1)
        rows = pl.multiple_of(y * 256, 256)
        total[...] += jnp.dot(pair, factors[pl.ds(rows, 256), :], preferred_element_type=F32)
        return carry

    lax.fori_loop(0, NY, block, 0)
    out[...] = total[:, :128] + total[:, 128:]


def carried(pos, mine, other, factors):
    return pl.pallas_call(
        carried_kernel,
        out_shape=jax.ShapeDtypeStruct((512, 128), F32),
        in_specs=[SMEM] + [VMEM] * 3,
        out_specs=VMEM,
        scratch_shapes=[pltpu.VMEM((512, 256), F32)],
        compiler_params=SMALL,
        name="carried_term",
    )(pos, mine, other, factors)


def local(adjoint, taper, panel_two, panel_one, incoming, inverse_factor):
    row, col = lax.axis_index("row"), lax.axis_index("col")
    pos = jnp.stack([col // NZ, col % NZ, row // 2, row % 2]).astype(jnp.int32)

    own, give = pack(pos, panel_two, panel_one)
    taken = core_swap(give)
    shard_two = jnp.concatenate([own[0], taken[0]], axis=0)
    shard_one = jnp.concatenate([own[1], taken[1]], axis=0)

    block = jnp.concatenate([shard_two] + [x_shift(shard_two, d) for d in (1, -1, 2)], axis=0)
    one = lax.all_gather(shard_one, "col", axis_index_groups=SAME_X, axis=0, tiled=True)
    down1, up1, swapped = together(z_shift(block, 1), z_shift(block, -1), core_swap(adjoint))
    for_two, for_one = prepare(pos, taper, adjoint, swapped)
    down2, up2, for_two, for_one = together(z_shift(down1, 1), z_shift(up1, -1), for_two, for_one)
    sum_two = product(pos, for_two, [block, down1, up1, down2, up2], 0)
    one, down2, up2 = together(one, down2, up2)
    down3, up3, sum_two = together(z_shift(down2, 1), z_shift(up2, -1), sum_two)
    far = [z_shift(down3[:256], 1), z_shift(up3[256:], -1)]
    sum_two = product(pos, for_two, [down3, up3], 5, sum_two)

    down, up = x_shift(one, 1), x_shift(one, -1)
    inverse = lax.all_gather(together(inverse_factor, up2)[0], "row", axis=0, tiled=True)
    far_one = [x_shift(down[:HALF], 1), x_shift(up[HALF:], -1)]
    sum_one = product(pos, for_one, [one, down, up], 0)

    sums = product(pos, for_two, far, 7, sum_two, F32)
    second_grad = incoming + jnp.sum(y_exchange(sums), axis=0)
    rounded = second_grad.astype(BF16)
    column = y_exchange(jnp.broadcast_to(rounded, (NY, 512, 128)))
    other = core_swap(column)

    first, *rest = diagonal(pos, [one, down, up] + far_one)
    factors = factor(pos, inverse, [first] + [y_first(part, d + 1) for d, part in enumerate(rest)])
    sums = product(pos, for_one, far_one, 6, sum_one, BF16)
    term = carried(pos, column, other, factors)
    first_grad = jnp.sum(y_exchange(sums).astype(F32), axis=0) - term
    return second_grad, first_grad


def solution(mesh):
    in_specs = (
        P("row", "col"),
        P(),
        P(("row", "col"), None),
        P(("row", "col"), None),
        P("col", "row"),
        P("row", None),
    )
    out_specs = (P("col", "row"), P("col", "row"))
    return jax.shard_map(local, mesh=mesh, in_specs=in_specs, out_specs=out_specs, check_vma=False)
```

```python
import functools

import jax
import jax.numpy as jnp
from jax import lax
from jax.experimental import pallas as pl
from jax.experimental.pallas import tpu as pltpu
from jax.sharding import PartitionSpec as P

BLK = 256
NX, NZ, NY = 4, 8, 4
SAME_X = [[x * NZ + z for z in range(NZ)] for x in range(NX)]
SUB = 64
PAIR = 2 * SUB
HALF = 512
WIDE = 384
F32, BF16 = jnp.float32, jnp.bfloat16
VMEM = pl.BlockSpec(memory_space=pltpu.VMEM)
SMEM = pl.BlockSpec(memory_space=pltpu.SMEM)
ANY = pl.BlockSpec(memory_space=pl.ANY)
BIG = pltpu.CompilerParams(vmem_limit_bytes=24 * 2**20)
SMALL = pltpu.CompilerParams(vmem_limit_bytes=16 * 2**20)


def x_shift(value, dx):
    pairs = [(x * NZ + z, (x + dx) % NX * NZ + z) for x in range(NX) for z in range(NZ)]
    return lax.ppermute(value, "col", pairs)


def z_shift(value, dz):
    pairs = [(x * NZ + z, x * NZ + (z + dz) % NZ) for x in range(NX) for z in range(NZ)]
    return lax.ppermute(value, "col", pairs)


def y_shift(value, dy):
    pairs = [(y * 2 + k, (y + dy) % NY * 2 + k) for y in range(NY) for k in range(2)]
    return lax.ppermute(value, "row", pairs)


def to_first(value):
    sent = [lax.ppermute(value, "row", [(y * 2 + k, k) for k in range(2)]) for y in range(1, NY)]
    return jnp.stack([value] + sent)


def swap_first(value):
    return lax.ppermute(value, "row", [(0, 1), (1, 0)])


def core_swap(value):
    return lax.ppermute(value, "row", [(r, r ^ 1) for r in range(2 * NY)])


def together(*values):
    return lax.optimization_barrier(values)


def offset(n):
    return ((n + 1) // 2) * (1 - 2 * (n % 2))


def source_xz(pos, b, t):
    return (pos[0] + offset(t) + NX) % NX, (pos[1] + offset(b) + NZ) % NZ


def source_zx(pos, b, t):
    return (pos[0] + offset(b // 2) + NX) % NX, b % 2 * 4 + t


def pack_kernel(pos, two, one, own, give):
    first = pos[3] == 0
    for q in range(NY):
        at = slice(q * 128, q * 128 + 128)
        for n, panel in enumerate((two, one) if q < 3 else (one, two)):
            left = panel[:, q * 256:q * 256 + 128]
            right = panel[:, q * 256 + 128:q * 256 + 256]
            own[n, :, at] = jnp.where(first, left, right)
            give[n, :, at] = jnp.where(first, right, left)


def pack(pos, two, one):
    return pl.pallas_call(
        pack_kernel,
        out_shape=(jax.ShapeDtypeStruct((2, SUB, HALF), BF16),) * 2,
        in_specs=[SMEM, VMEM, VMEM],
        out_specs=(VMEM, VMEM),
        compiler_params=SMALL,
        name="pack_columns",
    )(pos, two, one)


def join_kernel(own, down, up, far, main, rest):
    for n, part in enumerate((own, down, up, far)):
        main[n] = part[:, :WIDE]
        rest[n] = part[:, WIDE:]


def join(*parts):
    return pl.pallas_call(
        join_kernel,
        out_shape=(
            jax.ShapeDtypeStruct((NX, PAIR, WIDE), BF16),
            jax.ShapeDtypeStruct((NX, PAIR, HALF - WIDE), BF16),
        ),
        in_specs=[VMEM] * NX,
        out_specs=(VMEM, VMEM),
        compiler_params=SMALL,
        name="join_parts",
    )(*parts)


def prepare_kernel(pos, taper, mine, other, out_xz, out_zx, rows, held, sems):
    lane = lax.broadcasted_iota(jnp.int32, (SUB, 2 * BLK), 1)
    first_col = (pos[0] * NZ + pos[1]) * 2

    for out, source in ((out_xz, source_xz), (out_zx, source_zx)):
        def block(b, carry, out=out, source=source):
            for t in range(4):
                x, z = source(pos, b, t)
                row = pl.multiple_of((x * NZ + z) * SUB, SUB)
                for h, ref in enumerate((mine, other)):
                    core = pos[3] if h == 0 else 1 - pos[3]
                    tile = (pos[2] * 2 + core) * 8 + x * 2 + z // 4
                    left = taper[tile, first_col].astype(F32)
                    right = taper[tile, first_col + 1].astype(F32)
                    keep = jnp.where(lane < BLK, left, right)
                    at = t * PAIR + h * SUB
                    rows[at:at + SUB, :] = (ref[pl.ds(row, SUB), :].astype(F32) * keep).astype(BF16)
            held[b] = rows[...].T
            pltpu.make_async_copy(held.at[b], out.at[b], sems.at[b]).start()
            return carry

        lax.fori_loop(0, 8, block, 0)
        for b in range(8):
            pltpu.make_async_copy(held.at[b], out.at[b], sems.at[b]).wait()


def prepare(pos, taper, mine, other):
    return pl.pallas_call(
        prepare_kernel,
        out_shape=(jax.ShapeDtypeStruct((8, 512, 512), BF16),) * 2,
        in_specs=[SMEM, SMEM, VMEM, VMEM],
        out_specs=(pl.BlockSpec(memory_space=pltpu.HBM),) * 2,
        scratch_shapes=[
            pltpu.VMEM((512, 512), BF16),
            pltpu.VMEM((8, 512, 512), BF16),
            pltpu.SemaphoreType.DMA((8,)),
        ],
        compiler_params=BIG,
        name="prepare_adjoint",
    )(pos, taper, mine, other)


def product_kernel(count, wide, narrow, first, last, diagonal, pos, by_xz, by_zx, *refs):
    panels, refs = refs[:count], list(refs[count:])
    before = None if first else refs.pop(0)
    pieces = (refs.pop(0), refs.pop(0)) if diagonal else None
    outs = [refs.pop(0) for _ in range(NY)] if last else None
    total = refs.pop(0)
    left, main, rest, sems = refs[:4]
    items = list(wide) + list(narrow)
    for n, (which, b, parts) in enumerate(items):
        pltpu.make_async_copy((by_xz, by_zx)[which].at[b], left.at[n], sems.at[0, n]).start()
        held, at = (main, n) if n < len(wide) else (rest, n - len(wide))
        to = 0
        for index, start, size in parts:
            begin = start(pos) if callable(start) else start
            pltpu.make_async_copy(
                panels[index].at[pl.ds(begin, size)], held.at[at, pl.ds(to, size)], sems.at[1, n]
            ).start()
            to += size

    if diagonal:
        top, top_rest, top_sems = refs[4:7]
        half = jnp.where(pos[3] == 0, 0, SUB)

        @pl.when(pos[2] == 0)
        def _():
            for i in range(NX):
                x = (pos[0] + offset(i) + NX) % NX
                sources = ((panels[i], 0),) if i < 3 else ((panels[3], 0), (panels[4], 4))

                @pl.when(x < 2)
                def _(i=i, x=x, sources=sources):
                    for ref, z in sources:
                        pltpu.make_async_copy(
                            ref.at[:, pl.ds(half, SUB), :],
                            top.at[pl.ds(x * NZ + z, ref.shape[0])], top_sems.at[0]).start()
                    pltpu.make_async_copy(
                        panels[5].at[:, i, pl.ds(half, SUB), :],
                        top_rest.at[pl.ds(x * NZ, NZ)], top_sems.at[1]).start()

    if first:
        total[...] = jnp.zeros_like(total)
    else:
        total[...] = before[...]

    def step(n, held, at, columns):
        pltpu.make_async_copy(left.at[n], left.at[n], sems.at[0, n]).wait()
        pltpu.make_async_copy(held.at[at], held.at[at], sems.at[1, n]).wait()
        block = held[at].reshape(NX * PAIR, held.shape[-1])
        total[:, columns] += jnp.dot(left[n], block, preferred_element_type=F32)

    def wide_step(n, carry):
        step(n, main, n, slice(0, WIDE))
        return carry

    def narrow_step(n, carry):
        step(n + len(wide), rest, n, slice(WIDE, HALF))
        return carry

    if wide:
        lax.fori_loop(0, len(wide), wide_step, 0)
    if narrow:
        lax.fori_loop(0, len(narrow), narrow_step, 0)

    if diagonal:
        @pl.when(pos[2] == 0)
        def _():
            for n, (held, columns) in enumerate(((top, slice(0, WIDE)), (top_rest, slice(WIDE, HALF)))):
                pltpu.make_async_copy(held, held, top_sems.at[n]).wait()
                rows = held[...].reshape(2 * NZ * SUB, held.shape[-1])
                total[:, columns] += jnp.dot(pieces[0][...], rows, preferred_element_type=F32)
                total[:, columns] += jnp.dot(pieces[1][...], rows, preferred_element_type=F32)

    if last:
        for d, out in enumerate(outs):
            column = pl.multiple_of((pos[2] + d) % NY * 128, 128)
            out[...] = (-2.0 * total[:, pl.ds(column, 128)]).astype(out.dtype)


def product(pos, adjoint, panels, wide, narrow, before=None, pieces=(), kind=None):
    last = kind is not None
    column = jax.ShapeDtypeStruct((512, 128), F32)
    sums = jax.ShapeDtypeStruct((512, HALF), F32)
    count = len(wide) + len(narrow)
    scratch = [pltpu.VMEM((512, HALF), F32)] if last else []
    scratch += [
        pltpu.VMEM((max(count, 1), 512, 512), BF16),
        pltpu.VMEM((max(len(wide), 1), NX, PAIR, WIDE), BF16),
        pltpu.VMEM((max(len(narrow), 1), NX, PAIR, HALF - WIDE), BF16),
        pltpu.SemaphoreType.DMA((2, max(count, 1))),
    ]
    if pieces:
        scratch += [
            pltpu.VMEM((2 * NZ, SUB, WIDE), BF16),
            pltpu.VMEM((2 * NZ, SUB, HALF - WIDE), BF16),
            pltpu.SemaphoreType.DMA((2,)),
        ]
    extra = ([] if before is None else [before]) + list(pieces)
    kernel = functools.partial(
        product_kernel, len(panels), tuple(wide), tuple(narrow), before is None, last, bool(pieces))
    return pl.pallas_call(
        kernel,
        out_shape=(column,) + (jax.ShapeDtypeStruct((512, 128), kind),) * 3 if last else sums,
        in_specs=[SMEM, ANY, ANY] + [ANY] * len(panels) + [VMEM] * len(extra),
        out_specs=(VMEM,) * 4 if last else VMEM,
        scratch_shapes=scratch,
        compiler_params=SMALL,
        name="masked_product",
    )(pos, *adjoint, *panels, *extra)


def carried_kernel(pos, mine, other, factor, factor_other, high, low, total):
    @pl.when(pos[2] == 0)
    def _():
        total[...] = jnp.zeros_like(total)

        def block(y, carry):
            left = jnp.concatenate([mine[y], other[y]], axis=1)
            right = jnp.concatenate([factor[y], factor_other[y]], axis=0)
            total[...] += jnp.dot(left, right, preferred_element_type=F32)
            return carry

        lax.fori_loop(0, NY, block, 0)
        value = 0.5 * total[...]
        top = value.astype(BF16)
        high[...] = top
        low[...] = (value - top.astype(F32)).astype(BF16)


def carried(pos, mine, other, factor, factor_other):
    return pl.pallas_call(
        carried_kernel,
        out_shape=(jax.ShapeDtypeStruct((512, 1024), BF16),) * 2,
        in_specs=[SMEM] + [VMEM] * 4,
        out_specs=(VMEM, VMEM),
        scratch_shapes=[pltpu.VMEM((512, 1024), F32)],
        compiler_params=SMALL,
        name="carried_half",
    )(pos, mine, other, factor, factor_other)


def local(adjoint, taper, panel_two, panel_one, incoming, inverse_factor):
    row, col = lax.axis_index("row"), lax.axis_index("col")
    pos = jnp.stack([col // NZ, col % NZ, row // 2, row % 2]).astype(jnp.int32)

    own, give = pack(pos, panel_two, panel_one)
    taken = core_swap(give)
    x_first = jnp.concatenate([own[0], taken[0]], axis=0)
    z_first = jnp.concatenate([own[1], taken[1]], axis=0)

    over_z = lax.all_gather(z_first, "col", axis_index_groups=SAME_X, axis=0, tiled=True)
    block, rest_one = join(x_first, *[x_shift(x_first, d) for d in (1, -1, 2)])
    rest_one = lax.all_gather(rest_one, "col", axis_index_groups=SAME_X, axis=0)

    factor = to_first(inverse_factor)
    down1, up1, swapped, factor = together(
        z_shift(block, 1), z_shift(block, -1), core_swap(adjoint), factor)
    masked = prepare(pos, taper, adjoint, swapped)
    down2, up2, factor_other, *masked = together(
        z_shift(down1, 1), z_shift(up1, -1), swap_first(factor), *masked)
    sums = product(
        pos, masked, [block, down1, up1, down2, up2], [(0, b, [(b, 0, 4)]) for b in range(5)], [])
    over_z, down2, up2 = together(over_z, down2, up2)
    rest_two = over_z[:, WIDE:].reshape(NZ, PAIR, HALF - WIDE)
    rest_two = [rest_two] + [x_shift(rest_two, d) for d in (1, -1, 2)]
    down3, up3, sums = together(z_shift(down2, 1), z_shift(up2, -1), sums)
    far = [z_shift(down3[:2], 1), z_shift(up3[2:], -1)]

    main = over_z[:, :WIDE].reshape(NZ, PAIR, WIDE)
    main, *rest_two = together(main, *rest_two)
    down, up = x_shift(main, 1), x_shift(main, -1)
    sums = product(
        pos, masked, [down3, up3] + rest_two, [(0, 5 + b, [(b, 0, 4)]) for b in range(2)],
        [(1, b, [(2 + b // 2, b % 2 * 4, 4)]) for b in range(8)], sums)
    mine, *sent = product(
        pos, masked, far, [(0, 7, [(0, 0, 2), (1, 0, 2)])], [], sums, kind=F32)
    r1, r2, r3 = [y_shift(part, d + 1) for d, part in enumerate(sent)]
    far_one = [x_shift(down[:4], 1), x_shift(up[4:], -1)]
    second_grad = incoming + ((mine + r1) + (r2 + r3))
    rounded = to_first(second_grad.astype(BF16))
    rounded_other = swap_first(rounded)

    sums = product(
        pos, masked, [main, down, up], [(1, b, [(b // 2, b % 2 * 4, 4)]) for b in range(6)], [])
    pieces = carried(pos, rounded, rounded_other, factor, factor_other)

    def of_z(b):
        return lambda pos: source_xz(pos, b, 0)[1] * NX

    rest_flat = rest_one.reshape(NZ * NX, PAIR, HALF - WIDE)
    sums = product(
        pos, masked, far_one + [rest_flat], [(1, 6 + b, [(b, 0, 4)]) for b in range(2)],
        [(0, b, [(2, of_z(b), 4)]) for b in range(8)], sums)
    mine, *sent = product(
        pos, masked, [main, down, up] + far_one + [rest_one], [], [], sums, pieces, BF16)
    r1, r2, r3 = [y_shift(part, d + 1).astype(F32) for d, part in enumerate(sent)]
    return second_grad, (mine + r1) + (r2 + r3)


def solution(mesh):
    in_specs = (
        P("row", "col"),
        P(),
        P(("row", "col"), None),
        P(("row", "col"), None),
        P("col", "row"),
        P("row", None),
    )
    out_specs = (P("col", "row"), P("col", "row"))
    return jax.shard_map(local, mesh=mesh, in_specs=in_specs, out_specs=out_specs, check_vma=False)
```

```python
import functools

import jax
import jax.numpy as jnp
from jax import lax
from jax.experimental import pallas as pl
from jax.experimental.pallas import tpu as pltpu
from jax.sharding import PartitionSpec as P

BLK = 256
NX, NZ, NY = 4, 8, 4
SUB = 64
PAIR = 2 * SUB
HALF = 512
F32, BF16 = jnp.float32, jnp.bfloat16
VMEM = pl.BlockSpec(memory_space=pltpu.VMEM)
SMEM = pl.BlockSpec(memory_space=pltpu.SMEM)
ANY = pl.BlockSpec(memory_space=pl.ANY)
BIG = pltpu.CompilerParams(vmem_limit_bytes=24 * 2**20)
SMALL = pltpu.CompilerParams(vmem_limit_bytes=16 * 2**20)


def x_shift(value, dx):
    pairs = [(x * NZ + z, (x + dx) % NX * NZ + z) for x in range(NX) for z in range(NZ)]
    return lax.ppermute(value, "col", pairs)


def z_shift(value, dz):
    pairs = [(x * NZ + z, x * NZ + (z + dz) % NZ) for x in range(NX) for z in range(NZ)]
    return lax.ppermute(value, "col", pairs)


def y_shift(value, dy):
    pairs = [(y * 2 + k, (y + dy) % NY * 2 + k) for y in range(NY) for k in range(2)]
    return lax.ppermute(value, "row", pairs)


def y_first(value, y):
    return lax.ppermute(value, "row", [(k, y * 2 + k) for k in range(2)])


def y_all(value):
    return jnp.stack([value] + [y_shift(value, d) for d in range(1, NY)])


def core_swap(value):
    return lax.ppermute(value, "row", [(r, r ^ 1) for r in range(2 * NY)])


def together(*values):
    return lax.optimization_barrier(values)


def offset(n):
    return ((n + 1) // 2) * (1 - 2 * (n % 2))


def source(pos, i, j):
    return (pos[0] + offset(i) + NX) % NX, (pos[1] + offset(j) + NZ) % NZ


def pack_kernel(pos, two, one, own, give):
    first = pos[3] == 0
    for q in range(NY):
        at = slice(q * 128, q * 128 + 128)
        for n, panel in enumerate((two, one)):
            left = panel[:, q * 256:q * 256 + 128]
            right = panel[:, q * 256 + 128:q * 256 + 256]
            own[n, :, at] = jnp.where(first, left, right)
            give[n, :, at] = jnp.where(first, right, left)


def pack(pos, two, one):
    return pl.pallas_call(
        pack_kernel,
        out_shape=(jax.ShapeDtypeStruct((2, SUB, HALF), BF16),) * 2,
        in_specs=[SMEM, VMEM, VMEM],
        out_specs=(VMEM, VMEM),
        compiler_params=SMALL,
        name="pack_columns",
    )(pos, two, one)


def join_kernel(picks, *refs):
    for n, pick in enumerate(picks):
        refs[-1][n] = refs[n][...] if pick is None else refs[n][pick]


def join(parts, picks):
    return pl.pallas_call(
        functools.partial(join_kernel, picks),
        out_shape=jax.ShapeDtypeStruct((len(parts), PAIR, HALF), BF16),
        in_specs=[VMEM] * len(parts),
        out_specs=VMEM,
        compiler_params=SMALL,
        name="join_parts",
    )(*parts)


def prepare_kernel(pos, taper, mine, other, out, rows):
    lane = lax.broadcasted_iota(jnp.int32, (SUB, 2 * BLK), 1)
    first_col = (pos[0] * NZ + pos[1]) * 2

    def block(j, carry):
        for i in range(NX):
            x, z = source(pos, i, j)
            row = pl.multiple_of((x * NZ + z) * SUB, SUB)
            for h, ref in enumerate((mine, other)):
                core = pos[3] if h == 0 else 1 - pos[3]
                tile = (pos[2] * 2 + core) * 8 + x * 2 + z // 4
                left = taper[tile, first_col].astype(F32)
                right = taper[tile, first_col + 1].astype(F32)
                keep = jnp.where(lane < BLK, left, right)
                at = i * PAIR + h * SUB
                rows[at:at + SUB, :] = (ref[pl.ds(row, SUB), :].astype(F32) * keep).astype(BF16)
        out[j] = rows[...].T
        return carry

    lax.fori_loop(0, NZ, block, 0)


def prepare(pos, taper, mine, other):
    return pl.pallas_call(
        prepare_kernel,
        out_shape=jax.ShapeDtypeStruct((NZ, 512, 512), BF16),
        in_specs=[SMEM, SMEM, VMEM, VMEM],
        out_specs=VMEM,
        scratch_shapes=[pltpu.VMEM((512, 512), BF16)],
        compiler_params=SMALL,
        name="prepare_adjoint",
    )(pos, taper, mine, other)


def product_kernel(count, items, first, last, pos, adjoint, *refs):
    panels, refs = refs[:count], list(refs[count:])
    before = None if first else refs.pop(0)
    outs = [refs.pop(0) for _ in range(NY)] if last else None
    total, held, sems = refs
    for n, (_, parts) in enumerate(items):
        to = 0
        for index, start, size in parts:
            pltpu.make_async_copy(
                panels[index].at[pl.ds(start, size)], held.at[n, pl.ds(to, size)], sems.at[n]).start()
            to += size
    if first:
        total[...] = jnp.zeros_like(total)
    else:
        total[...] = before[...]
    begin = items[0][0]

    def step(n, carry):
        pltpu.make_async_copy(held.at[n], held.at[n], sems.at[n]).wait()
        total[...] += jnp.dot(
            adjoint[begin + n], held[n].reshape(NX * PAIR, HALF), preferred_element_type=F32)
        return carry

    lax.fori_loop(0, len(items), step, 0)
    if last:
        for d, out in enumerate(outs):
            column = pl.multiple_of((pos[2] + d) % NY * 128, 128)
            out[...] = (-2.0 * total[:, pl.ds(column, 128)]).astype(out.dtype)


def product(pos, adjoint, panels, items, before=None, kind=None):
    last = kind is not None
    column = jax.ShapeDtypeStruct((512, 128), F32)
    scratch = [pltpu.VMEM((512, HALF), F32)] if last else []
    scratch += [
        pltpu.VMEM((len(items), NX, PAIR, HALF), BF16),
        pltpu.SemaphoreType.DMA((len(items),)),
    ]
    extra = [] if before is None else [before]
    kernel = functools.partial(product_kernel, len(panels), tuple(items), before is None, last)
    return pl.pallas_call(
        kernel,
        out_shape=(column,) + (jax.ShapeDtypeStruct((512, 128), kind),) * 3
        if last else jax.ShapeDtypeStruct((512, HALF), F32),
        in_specs=[SMEM, VMEM] + [ANY] * len(panels) + [VMEM] * len(extra),
        out_specs=(VMEM,) * 4 if last else VMEM,
        scratch_shapes=scratch,
        compiler_params=SMALL,
        name="masked_product",
    )(pos, adjoint, *panels, *extra)


def diagonal_kernel(where, pos, *refs):
    panels, outs, held, sem = refs[:-6], refs[-6:-2], refs[-2], refs[-1]
    half = jnp.where(pos[3] == 0, 0, SUB)

    @pl.when(pos[2] == 0)
    def _():
        for i in range(NX):
            x = source(pos, i, 0)[0]

            @pl.when(x < 2)
            def _(i=i, x=x):
                for j in range(NZ):
                    index, at = where[i][j]
                    z = source(pos, i, j)[1]
                    pltpu.make_async_copy(
                        panels[index].at[at, pl.ds(half, SUB), :], held.at[x * NZ + z], sem.at[0]
                    ).start()

        pltpu.make_async_copy(held, held, sem.at[0]).wait()
        for d, out in enumerate(outs):
            out[...] = held[:, :, d * 128:(d + 1) * 128].reshape(2 * NZ * SUB, 128)


def diagonal(pos, panels, where):
    return pl.pallas_call(
        functools.partial(diagonal_kernel, where),
        out_shape=(jax.ShapeDtypeStruct((1024, 128), BF16),) * 4,
        in_specs=[SMEM] + [ANY] * len(panels),
        out_specs=(VMEM,) * 4,
        scratch_shapes=[pltpu.VMEM((2 * NZ, SUB, HALF), BF16), pltpu.SemaphoreType.DMA((1,))],
        compiler_params=SMALL,
        name="diagonal_columns",
    )(pos, *panels)


def factor_kernel(pos, inverse, inverse_other, own, one, two, three, out, out_other):
    sent = (one[...] + two[...]) + three[...]
    columns = jnp.where(pos[2] == 0, own[...], sent)
    for left, result in ((inverse, out), (inverse_other, out_other)):
        def block(d, carry, left=left, result=result):
            value = jnp.dot(left[d], columns, preferred_element_type=F32)
            high = value.astype(BF16)
            result[d, :, :128] = high
            result[d, :, 128:] = (value - high.astype(F32)).astype(BF16)
            return carry

        lax.fori_loop(0, NY, block, 0)


def factor(pos, inverse, inverse_other, parts):
    return pl.pallas_call(
        factor_kernel,
        out_shape=(jax.ShapeDtypeStruct((NY, 128, 256), BF16),) * 2,
        in_specs=[SMEM] + [VMEM] * 6,
        out_specs=(VMEM, VMEM),
        compiler_params=SMALL,
        name="inverse_times_diagonal",
    )(pos, inverse, inverse_other, *parts)


def carried_kernel(mine, other, factors, factors_other, out, total):
    total[...] = jnp.zeros_like(total)

    def block(d, carry):
        left = jnp.concatenate([mine[d], other[d]], axis=1)
        right = jnp.concatenate([factors[d], factors_other[d]], axis=0)
        total[...] += jnp.dot(left, right, preferred_element_type=F32)
        return carry

    lax.fori_loop(0, NY, block, 0)
    out[...] = total[:, :128] + total[:, 128:]


def carried(mine, other, factors, factors_other):
    return pl.pallas_call(
        carried_kernel,
        out_shape=jax.ShapeDtypeStruct((512, 128), F32),
        in_specs=[VMEM] * 4,
        out_specs=VMEM,
        scratch_shapes=[pltpu.VMEM((512, 256), F32)],
        compiler_params=SMALL,
        name="carried_term",
    )(mine, other, factors, factors_other)


def local(adjoint, taper, panel_two, panel_one, incoming, inverse_factor):
    row, col = lax.axis_index("row"), lax.axis_index("col")
    pos = jnp.stack([col // NZ, col % NZ, row // 2, row % 2]).astype(jnp.int32)

    own, give = pack(pos, panel_two, panel_one)
    taken = core_swap(give)
    shards = jnp.concatenate([own, taken], axis=1)

    first_x = [shards] + [x_shift(shards, d) for d in (1, -1, 2)]
    own = join(first_x + [shards], (0, 0, 0, 0, 1))
    inverse = y_all(inverse_factor)
    down1, up1, inverse, swapped = together(
        z_shift(own, 1), z_shift(own, -1), inverse, core_swap(adjoint))

    def x_others(*messages):
        part = join(messages, (4,) * len(messages)) if len(messages) > 1 else messages[0][-1:]
        return [part] + [x_shift(part, d) for d in (1, -1, 2)]

    masked = prepare(pos, taper, adjoint, swapped)
    down2, up2, masked, inverse_other, *near = together(
        z_shift(down1, 1), z_shift(up1, -1), masked, core_swap(inverse), *x_others(down1, up1))
    sums = product(
        pos, masked, [own, down1, up1, down2, up2], [(j, [(j, 0, 4)]) for j in range(5)])
    down3, up3, sums, *middle = together(
        z_shift(down2, 1), z_shift(up2, -1), sums, *x_others(down2, up2))
    sums = product(pos, masked, [down3, up3], [(5 + j, [(j, 0, 4)]) for j in range(2)], sums)
    sums_one = product(
        pos, masked, first_x + near + middle,
        [(0, [(i, 1, 1) for i in range(NX)])]
        + [(1 + j, [(NX * (1 + j // 2) + i, j % 2, 1) for i in range(NX)]) for j in range(4)])
    far_low, far_high, sums, sums_one, *third = together(
        z_shift(down3[:2], 1), z_shift(up3[2:], -1), sums, sums_one, *x_others(down3, up3))
    last = x_others(far_high)

    mine, *sent = product(
        pos, masked, [far_low, far_high], [(7, [(0, 0, 2), (1, 0, 2)])], sums, F32)
    r1, r2, r3 = [y_shift(part, d + 1) for d, part in enumerate(sent)]
    second_grad = incoming + ((mine + r1) + (r2 + r3))
    rounded = y_all(second_grad.astype(BF16))
    rounded_other = core_swap(rounded)

    where = tuple(
        ((i, 1),) + tuple((NX * (1 + j // 2) + i, j % 2) for j in range(7)) for i in range(NX))
    first, *rest = diagonal(pos, first_x + near + middle + third + last, where)
    rest = [y_first(part, d + 1) for d, part in enumerate(rest)]
    mine, *sent = product(
        pos, masked, third + last,
        [(5 + j, [(NX * (j // 2) + i, j % 2, 1) for i in range(NX)]) for j in range(3)],
        sums_one, BF16)
    r1, r2, r3 = [y_shift(part, d + 1).astype(F32) for d, part in enumerate(sent)]
    factors = factor(pos, inverse, inverse_other, [first] + rest)
    term = carried(rounded, rounded_other, *factors)
    return second_grad, (mine + r1) + (r2 + r3) - term


def solution(mesh):
    in_specs = (
        P("row", "col"),
        P(),
        P(("row", "col"), None),
        P(("row", "col"), None),
        P("col", "row"),
        P("row", None),
    )
    out_specs = (P("col", "row"), P("col", "row"))
    return jax.shard_map(local, mesh=mesh, in_specs=in_specs, out_specs=out_specs, check_vma=False)
```

```python
import functools

import jax
import jax.numpy as jnp
from jax import lax
from jax.experimental import pallas as pl
from jax.experimental.pallas import tpu as pltpu
from jax.sharding import PartitionSpec as P

BLK = 256
NX, NZ, NY = 4, 8, 4
SUB = 64
PAIR = 2 * SUB
HALF = 512
F32, BF16 = jnp.float32, jnp.bfloat16
VMEM = pl.BlockSpec(memory_space=pltpu.VMEM)
SMEM = pl.BlockSpec(memory_space=pltpu.SMEM)
ANY = pl.BlockSpec(memory_space=pl.ANY)
BIG = pltpu.CompilerParams(vmem_limit_bytes=24 * 2**20)
SMALL = pltpu.CompilerParams(vmem_limit_bytes=16 * 2**20)


def x_shift(value, dx):
    pairs = [(x * NZ + z, (x + dx) % NX * NZ + z) for x in range(NX) for z in range(NZ)]
    return lax.ppermute(value, "col", pairs)


def z_shift(value, dz):
    pairs = [(x * NZ + z, x * NZ + (z + dz) % NZ) for x in range(NX) for z in range(NZ)]
    return lax.ppermute(value, "col", pairs)


def y_shift(value, dy):
    pairs = [(y * 2 + k, (y + dy) % NY * 2 + k) for y in range(NY) for k in range(2)]
    return lax.ppermute(value, "row", pairs)


def y_first(value, y):
    return lax.ppermute(value, "row", [(k, y * 2 + k) for k in range(2)])


def y_all(value):
    return jnp.stack([value] + [y_shift(value, d) for d in range(1, NY)])


def core_swap(value):
    return lax.ppermute(value, "row", [(r, r ^ 1) for r in range(2 * NY)])


def together(*values):
    return lax.optimization_barrier(values)


def offset(n):
    return ((n + 1) // 2) * (1 - 2 * (n % 2))


def source(pos, i, j):
    return (pos[0] + offset(i) + NX) % NX, (pos[1] + offset(j) + NZ) % NZ


def pack_kernel(pos, two, one, own, give, held, sems):
    copies = [pltpu.make_async_copy(ref, held.at[n], sems.at[n]) for n, ref in enumerate((two, one))]
    for copy in copies:
        copy.start()
    first = pos[3] == 0
    for n, copy in enumerate(copies):
        copy.wait()
        for q in range(NY):
            at = slice(q * 128, q * 128 + 128)
            left = held[n, :, q * 256:q * 256 + 128]
            right = held[n, :, q * 256 + 128:q * 256 + 256]
            own[n, :, at] = jnp.where(first, left, right)
            give[n, :, at] = jnp.where(first, right, left)


def pack(pos, two, one):
    return pl.pallas_call(
        pack_kernel,
        out_shape=(jax.ShapeDtypeStruct((2, SUB, HALF), BF16),) * 2,
        in_specs=[SMEM, ANY, ANY],
        out_specs=(VMEM, VMEM),
        scratch_shapes=[pltpu.VMEM((2, SUB, 2 * HALF), BF16), pltpu.SemaphoreType.DMA((2,))],
        compiler_params=SMALL,
        name="pack_columns",
    )(pos, two, one)


def join_kernel(picks, *refs):
    for n, pick in enumerate(picks):
        refs[-1][n] = refs[n][...] if pick is None else refs[n][pick]


def join(parts, picks):
    return pl.pallas_call(
        functools.partial(join_kernel, picks),
        out_shape=jax.ShapeDtypeStruct((len(parts), PAIR, HALF), BF16),
        in_specs=[VMEM] * len(parts),
        out_specs=VMEM,
        compiler_params=SMALL,
        name="join_parts",
    )(*parts)


def prepare_kernel(pos, taper, mine, other, for_two, for_one, rows):
    lane = lax.broadcasted_iota(jnp.int32, (SUB, 2 * BLK), 1)
    first_col = (pos[0] * NZ + pos[1]) * 2

    def put(at, i, j):
        x, z = source(pos, i, j)
        row = pl.multiple_of((x * NZ + z) * SUB, SUB)
        for h, ref in enumerate((mine, other)):
            core = pos[3] if h == 0 else 1 - pos[3]
            tile = (pos[2] * 2 + core) * 8 + x * 2 + z // 4
            left = taper[tile, first_col].astype(F32)
            right = taper[tile, first_col + 1].astype(F32)
            keep = jnp.where(lane < BLK, left, right)
            rows[at + h * SUB:at + h * SUB + SUB, :] = (
                ref[pl.ds(row, SUB), :].astype(F32) * keep).astype(BF16)

    def block_two(j, carry):
        for i in range(NX):
            put(i * PAIR, i, j)
        for_two[j] = rows[:512].T
        return carry

    def block_one(c, carry):
        for i in range(NX):
            for s in range(2):
                put((2 * i + s) * PAIR, i, jnp.where(c == 0, 7 * s, 2 * c - 1 + s))
        for_one[c] = rows[...].T
        return carry

    lax.fori_loop(0, NZ, block_two, 0)
    lax.fori_loop(0, NZ // 2, block_one, 0)


def prepare(pos, taper, mine, other):
    return pl.pallas_call(
        prepare_kernel,
        out_shape=(
            jax.ShapeDtypeStruct((NZ, 512, 512), BF16),
            jax.ShapeDtypeStruct((NZ // 2, 512, 1024), BF16),
        ),
        in_specs=[SMEM, SMEM, VMEM, VMEM],
        out_specs=(VMEM, VMEM),
        scratch_shapes=[pltpu.VMEM((1024, 512), BF16)],
        compiler_params=SMALL,
        name="prepare_adjoint",
    )(pos, taper, mine, other)


def product_kernel(count, items, first, last, pos, adjoint, *refs):
    panels, refs = refs[:count], list(refs[count:])
    before = None if first else refs.pop(0)
    outs = [refs.pop(0) for _ in range(NY)] if last else None
    total, held, sems = refs
    for n, (_, parts) in enumerate(items):
        to = 0
        for index, start, size in parts:
            pltpu.make_async_copy(
                panels[index].at[pl.ds(start, size)], held.at[n, pl.ds(to, size)], sems.at[n]).start()
            to += size
    if first:
        total[...] = jnp.zeros_like(total)
    else:
        total[...] = before[...]
    begin = items[0][0]

    def step(n, carry):
        pltpu.make_async_copy(held.at[n], held.at[n], sems.at[n]).wait()
        total[...] += jnp.dot(
            adjoint[begin + n], held[n].reshape(-1, HALF), preferred_element_type=F32)
        return carry

    lax.fori_loop(0, len(items), step, 0)
    if last:
        for d, out in enumerate(outs):
            column = pl.multiple_of((pos[2] + d) % NY * 128, 128)
            out[...] = (-2.0 * total[:, pl.ds(column, 128)]).astype(out.dtype)


def product(pos, adjoint, panels, items, before=None, kind=None):
    last = kind is not None
    column = jax.ShapeDtypeStruct((512, 128), F32)
    scratch = [pltpu.VMEM((512, HALF), F32)] if last else []
    scratch += [
        pltpu.VMEM((len(items), adjoint.shape[2] // PAIR, PAIR, HALF), BF16),
        pltpu.SemaphoreType.DMA((len(items),)),
    ]
    extra = [] if before is None else [before]
    kernel = functools.partial(product_kernel, len(panels), tuple(items), before is None, last)
    return pl.pallas_call(
        kernel,
        out_shape=(column,) + (jax.ShapeDtypeStruct((512, 128), kind),) * 3
        if last else jax.ShapeDtypeStruct((512, HALF), F32),
        in_specs=[SMEM, VMEM] + [ANY] * len(panels) + [VMEM] * len(extra),
        out_specs=(VMEM,) * 4 if last else VMEM,
        scratch_shapes=scratch,
        compiler_params=SMALL,
        name="masked_product",
    )(pos, adjoint, *panels, *extra)


def diagonal_kernel(where, pos, *refs):
    panels, outs, held, sem = refs[:-6], refs[-6:-2], refs[-2], refs[-1]
    half = jnp.where(pos[3] == 0, 0, SUB)

    @pl.when(pos[2] == 0)
    def _():
        for i in range(NX):
            x = source(pos, i, 0)[0]

            @pl.when(x < 2)
            def _(i=i, x=x):
                for j in range(NZ):
                    index, at = where[i][j]
                    z = source(pos, i, j)[1]
                    pltpu.make_async_copy(
                        panels[index].at[at, pl.ds(half, SUB), :], held.at[x * NZ + z], sem.at[0]
                    ).start()

        pltpu.make_async_copy(held, held, sem.at[0]).wait()
        for d, out in enumerate(outs):
            out[...] = held[:, :, d * 128:(d + 1) * 128].reshape(2 * NZ * SUB, 128)


def diagonal(pos, panels, where):
    return pl.pallas_call(
        functools.partial(diagonal_kernel, where),
        out_shape=(jax.ShapeDtypeStruct((1024, 128), BF16),) * 4,
        in_specs=[SMEM] + [ANY] * len(panels),
        out_specs=(VMEM,) * 4,
        scratch_shapes=[pltpu.VMEM((2 * NZ, SUB, HALF), BF16), pltpu.SemaphoreType.DMA((1,))],
        compiler_params=SMALL,
        name="diagonal_columns",
    )(pos, *panels)


def factor_kernel(pos, inverse, inverse_other, own, one, two, three, out, out_other):
    sent = (one[...] + two[...]) + three[...]
    columns = jnp.where(pos[2] == 0, own[...], sent)
    for left, result in ((inverse, out), (inverse_other, out_other)):
        value = jnp.dot(left[...].reshape(512, 1024), columns, preferred_element_type=F32)
        high = value.astype(BF16)
        low = (value - high.astype(F32)).astype(BF16)
        result[:, :, :128] = high.reshape(NY, 128, 128)
        result[:, :, 128:] = low.reshape(NY, 128, 128)


def factor(pos, inverse, inverse_other, parts):
    return pl.pallas_call(
        factor_kernel,
        out_shape=(jax.ShapeDtypeStruct((NY, 128, 256), BF16),) * 2,
        in_specs=[SMEM] + [VMEM] * 6,
        out_specs=(VMEM, VMEM),
        compiler_params=SMALL,
        name="inverse_times_diagonal",
    )(pos, inverse, inverse_other, *parts)


def carried_kernel(mine, other, factors, factors_other, out, total):
    total[...] = jnp.zeros_like(total)

    def block(d, carry):
        left = jnp.concatenate([mine[d], other[d]], axis=1)
        right = jnp.concatenate([factors[d], factors_other[d]], axis=0)
        total[...] += jnp.dot(left, right, preferred_element_type=F32)
        return carry

    lax.fori_loop(0, NY, block, 0)
    out[...] = total[:, :128] + total[:, 128:]


def carried(mine, other, factors, factors_other):
    return pl.pallas_call(
        carried_kernel,
        out_shape=jax.ShapeDtypeStruct((512, 128), F32),
        in_specs=[VMEM] * 4,
        out_specs=VMEM,
        scratch_shapes=[pltpu.VMEM((512, 256), F32)],
        compiler_params=SMALL,
        name="carried_term",
    )(mine, other, factors, factors_other)


def local(adjoint, taper, panel_two, panel_one, incoming, inverse_factor):
    row, col = lax.axis_index("row"), lax.axis_index("col")
    pos = jnp.stack([col // NZ, col % NZ, row // 2, row % 2]).astype(jnp.int32)

    own, give = pack(pos, panel_two, panel_one)
    taken = core_swap(give)
    shards = jnp.concatenate([own, taken], axis=1)

    two, one = shards[0], shards[1]

    def x_all(part):
        return [part] + [x_shift(part, d) for d in (1, -1, 2)]

    def of_one(*messages):
        return x_all(join(messages, (NX,) * len(messages)))

    *two, swapped = together(*x_all(two), core_swap(adjoint))
    own = join(two + [one], (None,) * 5)
    inverse = y_all(inverse_factor)
    down1, up1, inverse, *first_x = together(
        z_shift(own, 1), z_shift(own, -1), inverse, *x_all(one[None]))

    for_two, for_one = prepare(pos, taper, adjoint, swapped)
    down2, up2, for_two, for_one, inverse_other, *near = together(
        z_shift(down1, 1), z_shift(up1, -1), for_two, for_one, core_swap(inverse),
        *of_one(down1, up1))
    sums = product(
        pos, for_two, [own, down1, up1, down2, up2], [(j, [(j, 0, 4)]) for j in range(5)])
    down3, up3, sums, *middle = together(
        z_shift(down2, 1), z_shift(up2, -1), sums, *of_one(down2, up2))
    sums = product(pos, for_two, [down3, up3], [(5 + j, [(j, 0, 4)]) for j in range(2)], sums)
    sums_one = product(
        pos, for_one, near + middle,
        [(1 + c, [(NX * c + i, 0, 2) for i in range(NX)]) for c in range(2)])
    far_low, far_high, sums, sums_one, *third = together(
        z_shift(down3[:2], 1), z_shift(up3[2:], -1), sums, sums_one, *of_one(down3, up3))

    mine, *sent = product(
        pos, for_two, [far_low, far_high], [(7, [(0, 0, 2), (1, 0, 2)])], sums, F32)
    sums_one = product(pos, for_one, third, [(3, [(i, 0, 2) for i in range(NX)])], sums_one)
    r1, r2, r3, sums_one, *last = together(
        *[y_shift(part, d + 1) for d, part in enumerate(sent)], sums_one, *x_all(far_high[2:]))
    second_grad = incoming + ((mine + r1) + (r2 + r3))
    rounded = y_all(second_grad.astype(BF16))
    rounded_other = core_swap(rounded)

    where = tuple(
        ((i, 0),) + tuple((NX * (1 + j // 2) + i, j % 2) for j in range(7)) for i in range(NX))
    first, *rest = diagonal(pos, first_x + near + middle + third + last, where)
    rest = [y_first(part, d + 1) for d, part in enumerate(rest)]
    mine, *sent = product(
        pos, for_one, first_x + last,
        [(0, [(NX * s + i, 0, 1) for i in range(NX) for s in range(2)])], sums_one, BF16)
    r1, r2, r3 = [y_shift(part, d + 1).astype(F32) for d, part in enumerate(sent)]
    factors = factor(pos, inverse, inverse_other, [first] + rest)
    term = carried(rounded, rounded_other, *factors)
    return second_grad, (mine + r1) + (r2 + r3) - term


def solution(mesh):
    in_specs = (
        P("row", "col"),
        P(),
        P(("row", "col"), None),
        P(("row", "col"), None),
        P("col", "row"),
        P("row", None),
    )
    out_specs = (P("col", "row"), P("col", "row"))
    return jax.shard_map(local, mesh=mesh, in_specs=in_specs, out_specs=out_specs, check_vma=False)
```

```python
import functools

import jax
import jax.numpy as jnp
from jax import lax
from jax.experimental import pallas as pl
from jax.experimental.pallas import tpu as pltpu
from jax.sharding import PartitionSpec as P

BLK = 256
NX, NZ, NY = 4, 8, 4
SUB = 64
PAIR = 2 * SUB
HALF = 512
F32, BF16 = jnp.float32, jnp.bfloat16
VMEM = pl.BlockSpec(memory_space=pltpu.VMEM)
SMEM = pl.BlockSpec(memory_space=pltpu.SMEM)
ANY = pl.BlockSpec(memory_space=pl.ANY)
BIG = pltpu.CompilerParams(vmem_limit_bytes=24 * 2**20)
SMALL = pltpu.CompilerParams(vmem_limit_bytes=16 * 2**20)


def x_shift(value, dx):
    pairs = [(x * NZ + z, (x + dx) % NX * NZ + z) for x in range(NX) for z in range(NZ)]
    return lax.ppermute(value, "col", pairs)


def z_shift(value, dz):
    pairs = [(x * NZ + z, x * NZ + (z + dz) % NZ) for x in range(NX) for z in range(NZ)]
    return lax.ppermute(value, "col", pairs)


def y_shift(value, dy):
    pairs = [(y * 2 + k, (y + dy) % NY * 2 + k) for y in range(NY) for k in range(2)]
    return lax.ppermute(value, "row", pairs)


def y_first(value, y):
    return lax.ppermute(value, "row", [(k, y * 2 + k) for k in range(2)])


def core_swap(value):
    return lax.ppermute(value, "row", [(r, r ^ 1) for r in range(2 * NY)])


def together(*values):
    return lax.optimization_barrier(values)


def offset(n):
    return ((n + 1) // 2) * (1 - 2 * (n % 2))


def source(pos, i, j):
    return (pos[0] + offset(i) + NX) % NX, (pos[1] + offset(j) + NZ) % NZ


def pack_kernel(pos, two, one, own, give, held, sems):
    copies = [pltpu.make_async_copy(ref, held.at[n], sems.at[n]) for n, ref in enumerate((two, one))]
    for copy in copies:
        copy.start()
    first = pos[3] == 0
    for n, copy in enumerate(copies):
        copy.wait()
        for q in range(NY):
            at = slice(q * 128, q * 128 + 128)
            left = held[n, :, q * 256:q * 256 + 128]
            right = held[n, :, q * 256 + 128:q * 256 + 256]
            own[n, :, at] = jnp.where(first, left, right)
            give[n, :, at] = jnp.where(first, right, left)


def pack(pos, two, one):
    return pl.pallas_call(
        pack_kernel,
        out_shape=(jax.ShapeDtypeStruct((2, SUB, HALF), BF16),) * 2,
        in_specs=[SMEM, ANY, ANY],
        out_specs=(VMEM, VMEM),
        scratch_shapes=[pltpu.VMEM((2, SUB, 2 * HALF), BF16), pltpu.SemaphoreType.DMA((2,))],
        compiler_params=SMALL,
        name="pack_columns",
    )(pos, two, one)


def join_kernel(picks, *refs):
    for n, pick in enumerate(picks):
        refs[-1][n] = refs[n][...] if pick is None else refs[n][pick]


def join(parts, picks):
    return pl.pallas_call(
        functools.partial(join_kernel, picks),
        out_shape=jax.ShapeDtypeStruct((len(parts), PAIR, HALF), BF16),
        in_specs=[VMEM] * len(parts),
        out_specs=VMEM,
        compiler_params=SMALL,
        name="join_parts",
    )(*parts)


def prepare_kernel(pos, taper, mine, other, for_two, for_one, rows):
    lane = lax.broadcasted_iota(jnp.int32, (SUB, 2 * BLK), 1)
    first_col = (pos[0] * NZ + pos[1]) * 2

    def put(at, i, j):
        x, z = source(pos, i, j)
        row = pl.multiple_of((x * NZ + z) * SUB, SUB)
        for h, ref in enumerate((mine, other)):
            core = pos[3] if h == 0 else 1 - pos[3]
            tile = (pos[2] * 2 + core) * 8 + x * 2 + z // 4
            left = taper[tile, first_col].astype(F32)
            right = taper[tile, first_col + 1].astype(F32)
            keep = jnp.where(lane < BLK, left, right)
            rows[at + h * SUB:at + h * SUB + SUB, :] = (
                ref[pl.ds(row, SUB), :].astype(F32) * keep).astype(BF16)

    def block_two(j, carry):
        for i in range(NX):
            put(i * PAIR, i, j)
        for_two[j] = rows[:512].T
        return carry

    def block_one(c, carry):
        for i in range(NX):
            for s in range(2):
                put((2 * i + s) * PAIR, i, jnp.where(c == 0, 7 * s, 2 * c - 1 + s))
        for_one[c] = rows[...].T
        return carry

    lax.fori_loop(0, NZ, block_two, 0)
    lax.fori_loop(0, NZ // 2, block_one, 0)


def prepare(pos, taper, mine, other):
    return pl.pallas_call(
        prepare_kernel,
        out_shape=(
            jax.ShapeDtypeStruct((NZ, 512, 512), BF16),
            jax.ShapeDtypeStruct((NZ // 2, 512, 1024), BF16),
        ),
        in_specs=[SMEM, SMEM, VMEM, VMEM],
        out_specs=(VMEM, VMEM),
        scratch_shapes=[pltpu.VMEM((1024, 512), BF16)],
        compiler_params=SMALL,
        name="prepare_adjoint",
    )(pos, taper, mine, other)


def product_kernel(count, items, first, last, pos, adjoint, *refs):
    panels, refs = refs[:count], list(refs[count:])
    before = None if first else refs.pop(0)
    outs = [refs.pop(0) for _ in range(NY)] if last else None
    total, held, sems = refs
    for n, (_, parts) in enumerate(items):
        to = 0
        for index, start, size in parts:
            pltpu.make_async_copy(
                panels[index].at[pl.ds(start, size)], held.at[n, pl.ds(to, size)], sems.at[n]).start()
            to += size
    if first:
        total[...] = jnp.zeros_like(total)
    else:
        total[...] = before[...]
    begin = items[0][0]

    def step(n, carry):
        pltpu.make_async_copy(held.at[n], held.at[n], sems.at[n]).wait()
        total[...] += jnp.dot(
            adjoint[begin + n], held[n].reshape(-1, HALF), preferred_element_type=F32)
        return carry

    lax.fori_loop(0, len(items), step, 0)
    if last:
        for d, out in enumerate(outs):
            column = pl.multiple_of((pos[2] + d) % NY * 128, 128)
            out[...] = (-2.0 * total[:, pl.ds(column, 128)]).astype(out.dtype)


def product(pos, adjoint, panels, items, before=None, kind=None):
    last = kind is not None
    column = jax.ShapeDtypeStruct((512, 128), F32)
    scratch = [pltpu.VMEM((512, HALF), F32)] if last else []
    scratch += [
        pltpu.VMEM((len(items), adjoint.shape[2] // PAIR, PAIR, HALF), BF16),
        pltpu.SemaphoreType.DMA((len(items),)),
    ]
    extra = [] if before is None else [before]
    kernel = functools.partial(product_kernel, len(panels), tuple(items), before is None, last)
    return pl.pallas_call(
        kernel,
        out_shape=(column,) + (jax.ShapeDtypeStruct((512, 128), kind),) * 3
        if last else jax.ShapeDtypeStruct((512, HALF), F32),
        in_specs=[SMEM, VMEM] + [ANY] * len(panels) + [VMEM] * len(extra),
        out_specs=(VMEM,) * 4 if last else VMEM,
        scratch_shapes=scratch,
        compiler_params=SMALL,
        name="masked_product",
    )(pos, adjoint, *panels, *extra)


def diagonal_kernel(where, pos, *refs):
    panels, outs, held, sem = refs[:-6], refs[-6:-2], refs[-2], refs[-1]
    half = jnp.where(pos[3] == 0, 0, SUB)

    @pl.when(pos[2] == 0)
    def _():
        for i in range(NX):
            x = source(pos, i, 0)[0]

            @pl.when(x < 2)
            def _(i=i, x=x):
                for j in range(NZ):
                    index, at = where[i][j]
                    z = source(pos, i, j)[1]
                    pltpu.make_async_copy(
                        panels[index].at[at, pl.ds(half, SUB), :], held.at[x * NZ + z], sem.at[0]
                    ).start()

        pltpu.make_async_copy(held, held, sem.at[0]).wait()
        for d, out in enumerate(outs):
            out[...] = held[:, :, d * 128:(d + 1) * 128].reshape(2 * NZ * SUB, 128)


def diagonal(pos, panels, where):
    return pl.pallas_call(
        functools.partial(diagonal_kernel, where),
        out_shape=(jax.ShapeDtypeStruct((1024, 128), BF16),) * 4,
        in_specs=[SMEM] + [ANY] * len(panels),
        out_specs=(VMEM,) * 4,
        scratch_shapes=[pltpu.VMEM((2 * NZ, SUB, HALF), BF16), pltpu.SemaphoreType.DMA((1,))],
        compiler_params=SMALL,
        name="diagonal_columns",
    )(pos, *panels)


def factor_kernel(pos, inverse, inverse_other, own, one, two, three, out, out_other):
    sent = (one[...] + two[...]) + three[...]
    columns = jnp.where(pos[2] == 0, own[...], sent)
    for left, result in ((inverse, out), (inverse_other, out_other)):
        value = jnp.dot(left[...].reshape(512, 1024), columns, preferred_element_type=F32)
        high = value.astype(BF16)
        low = (value - high.astype(F32)).astype(BF16)
        result[:, :, :128] = high.reshape(NY, 128, 128)
        result[:, :, 128:] = low.reshape(NY, 128, 128)


def factor(pos, inverse, inverse_other, parts):
    return pl.pallas_call(
        factor_kernel,
        out_shape=(jax.ShapeDtypeStruct((NY, 128, 256), BF16),) * 2,
        in_specs=[SMEM] + [VMEM] * 6,
        out_specs=(VMEM, VMEM),
        compiler_params=SMALL,
        name="inverse_times_diagonal",
    )(pos, inverse, inverse_other, *parts)


def carried_kernel(mine, other, factors, factors_other, out, total):
    total[...] = jnp.zeros_like(total)

    def block(d, carry):
        left = jnp.concatenate([mine[d], other[d]], axis=1)
        right = jnp.concatenate([factors[d], factors_other[d]], axis=0)
        total[...] += jnp.dot(left, right, preferred_element_type=F32)
        return carry

    lax.fori_loop(0, NY, block, 0)
    out[...] = total[:, :128] + total[:, 128:]


def carried(mine, other, factors, factors_other):
    return pl.pallas_call(
        carried_kernel,
        out_shape=jax.ShapeDtypeStruct((512, 128), F32),
        in_specs=[VMEM] * 4,
        out_specs=VMEM,
        scratch_shapes=[pltpu.VMEM((512, 256), F32)],
        compiler_params=SMALL,
        name="carried_term",
    )(mine, other, factors, factors_other)


def local(adjoint, taper, panel_two, panel_one, incoming, inverse_factor):
    row, col = lax.axis_index("row"), lax.axis_index("col")
    pos = jnp.stack([col // NZ, col % NZ, row // 2, row % 2]).astype(jnp.int32)

    own, give = pack(pos, panel_two, panel_one)
    taken = core_swap(give)
    shards = jnp.concatenate([own, taken], axis=1)

    two, one = shards[0], shards[1]

    def x_all(part):
        return [part] + [x_shift(part, d) for d in (1, -1, 2)]

    def of_one(*messages):
        return x_all(join(messages, (NX,) * len(messages)))

    two, one, swapped = together(two, one, core_swap(adjoint))
    *two, inverse1, inverse3 = together(
        *x_all(two), y_shift(inverse_factor, 1), y_shift(inverse_factor, 3))
    own = join(two + [one], (None,) * 5)
    own, later = together(own, inverse_factor)
    inverse = jnp.stack([inverse_factor, inverse1, y_shift(later, 2), inverse3])
    down1, up1, inverse, *first_x = together(
        z_shift(own, 1), z_shift(own, -1), inverse, *x_all(one[None]))

    for_two, for_one = prepare(pos, taper, adjoint, swapped)
    down2, up2, for_two, for_one, *near = together(
        z_shift(down1, 1), z_shift(up1, -1), for_two, for_one, *of_one(down1, up1))
    inverse, down2, up2 = together(inverse, down2, up2)
    inverse_other = core_swap(inverse)
    sums = product(
        pos, for_two, [own, down1, up1, down2, up2], [(j, [(j, 0, 4)]) for j in range(5)])
    down3, up3, sums, *middle = together(
        z_shift(down2, 1), z_shift(up2, -1), sums, *of_one(down2, up2))
    sums = product(pos, for_two, [down3, up3], [(5 + j, [(j, 0, 4)]) for j in range(2)], sums)
    sums_one = product(
        pos, for_one, near + middle,
        [(1 + c, [(NX * c + i, 0, 2) for i in range(NX)]) for c in range(2)])
    third = of_one(down3, up3)
    far_low, far_high, sums, sums_one = together(
        z_shift(down3[:2], 1), z_shift(up3[2:], -1), sums, sums_one)

    mine, *sent = product(
        pos, for_two, [far_low, far_high], [(7, [(0, 0, 2), (1, 0, 2)])], sums, F32)
    last = x_all(far_high[2:])
    sums_one = product(pos, for_one, third, [(3, [(i, 0, 2) for i in range(NX)])], sums_one)
    where = tuple(
        ((i, 0),) + tuple((NX * (1 + j // 2) + i, j % 2) for j in range(7)) for i in range(NX))
    columns = diagonal(pos, first_x + near + middle + third + last, where)
    r1, r2, r3, sums_one, *columns = together(
        *[y_shift(part, d + 1) for d, part in enumerate(sent)], sums_one, *columns)
    second_grad = incoming + ((mine + r1) + (r2 + r3))
    rounded = second_grad.astype(BF16)

    sums_one = product(
        pos, for_one, first_x + last,
        [(0, [(NX * s + i, 0, 1) for i in range(NX) for s in range(2)])], sums_one, BF16)
    first, *rest = columns
    rest = [y_first(part, d + 1) for d, part in enumerate(rest)]
    s1, s2, s3, *rest = together(*[y_shift(rounded, d) for d in range(1, NY)], *rest, *sums_one)
    rest, (mine, *sent) = rest[:3], rest[3:]
    rounded = jnp.stack([rounded, s1, s2, s3])
    rounded_other = core_swap(rounded)
    r1, r2, r3 = [y_shift(part, d + 1).astype(F32) for d, part in enumerate(sent)]
    factors = factor(pos, inverse, inverse_other, [first] + rest)
    term = carried(rounded, rounded_other, *factors)
    return second_grad, (mine + r1) + (r2 + r3) - term


def solution(mesh):
    in_specs = (
        P("row", "col"),
        P(),
        P(("row", "col"), None),
        P(("row", "col"), None),
        P("col", "row"),
        P("row", None),
    )
    out_specs = (P("col", "row"), P("col", "row"))
    return jax.shard_map(local, mesh=mesh, in_specs=in_specs, out_specs=out_specs, check_vma=False)
```

```python
import functools

import jax
import jax.numpy as jnp
from jax import lax
from jax.experimental import pallas as pl
from jax.experimental.pallas import tpu as pltpu
from jax.sharding import PartitionSpec as P

BLK = 256
NX, NZ, NY = 4, 8, 4
SUB = 64
PAIR = 2 * SUB
HALF = 512
ROW = 16
ONE = PAIR // ROW + 1
TWO = NX * PAIR // ROW
F32, BF16 = jnp.float32, jnp.bfloat16
VMEM = pl.BlockSpec(memory_space=pltpu.VMEM)
SMEM = pl.BlockSpec(memory_space=pltpu.SMEM)
ANY = pl.BlockSpec(memory_space=pl.ANY)
BIG = pltpu.CompilerParams(vmem_limit_bytes=24 * 2**20)
SMALL = pltpu.CompilerParams(vmem_limit_bytes=16 * 2**20)


def x_shift(value, dx):
    pairs = [(x * NZ + z, (x + dx) % NX * NZ + z) for x in range(NX) for z in range(NZ)]
    return lax.ppermute(value, "col", pairs)


def z_shift(value, dz):
    pairs = [(x * NZ + z, x * NZ + (z + dz) % NZ) for x in range(NX) for z in range(NZ)]
    return lax.ppermute(value, "col", pairs)


def y_shift(value, dy):
    pairs = [(y * 2 + k, (y + dy) % NY * 2 + k) for y in range(NY) for k in range(2)]
    return lax.ppermute(value, "row", pairs)


def y_first(value, y):
    return lax.ppermute(value, "row", [(k, y * 2 + k) for k in range(2)])


def core_swap(value):
    return lax.ppermute(value, "row", [(r, r ^ 1) for r in range(2 * NY)])


def together(*values):
    return lax.optimization_barrier(values)


def offset(n):
    return ((n + 1) // 2) * (1 - 2 * (n % 2))


def source(pos, i, j):
    return (pos[0] + offset(i) + NX) % NX, (pos[1] + offset(j) + NZ) % NZ


def pack_kernel(pos, two, one, own, give, held, sems):
    copies = [pltpu.make_async_copy(ref, held.at[n], sems.at[n]) for n, ref in enumerate((two, one))]
    for copy in copies:
        copy.start()
    first = pos[3] == 0
    for n, copy in enumerate(copies):
        copy.wait()
        for q in range(NY):
            at = slice(q * 128, q * 128 + 128)
            left = held[n, :, q * 256:q * 256 + 128]
            right = held[n, :, q * 256 + 128:q * 256 + 256]
            own[n, :, at] = jnp.where(first, left, right)
            give[n, :, at] = jnp.where(first, right, left)


def pack(pos, two, one):
    return pl.pallas_call(
        pack_kernel,
        out_shape=(jax.ShapeDtypeStruct((2, SUB, HALF), BF16),) * 2,
        in_specs=[SMEM, ANY, ANY],
        out_specs=(VMEM, VMEM),
        scratch_shapes=[pltpu.VMEM((2, SUB, 2 * HALF), BF16), pltpu.SemaphoreType.DMA((2,))],
        compiler_params=SMALL,
        name="pack_columns",
    )(pos, two, one)


def top_kernel(pos, own, taken, *outs):
    first = pos[3] == 0
    for y, out in enumerate(outs):
        at = slice(y * 128, y * 128 + 128)
        out[...] = jnp.where(first, own[1, :, at], taken[1, :, at])


def top(pos, own, taken):
    return pl.pallas_call(
        top_kernel,
        out_shape=(jax.ShapeDtypeStruct((SUB, 128), BF16),) * NY,
        in_specs=[SMEM, VMEM, VMEM],
        out_specs=(VMEM,) * NY,
        compiler_params=SMALL,
        name="diagonal_blocks",
    )(pos, own, taken)


def message_kernel(pos, two, down, up, far, one, own, b1, b2, b3, out, part):
    for n, ref in enumerate((two, down, up, far)):
        out[n * 8:n * 8 + 8] = ref[...].reshape(8, ROW, HALF)
    rows = one[...].reshape(8, ROW, HALF)
    out[TWO:TWO + 8] = rows
    part[0, :8] = rows
    sent = (b1[...] + b2[...]) + b3[...]
    columns = jnp.where(pos[2] == 0, own[...], sent)
    for q in range(NY):
        at = slice(q * 128, q * 128 + 128)
        out[TWO + 8, :, at] = columns[q * ROW:(q + 1) * ROW]
        part[0, 8, :, at] = columns[q * ROW:(q + 1) * ROW]


def message(pos, twos, one, blocks):
    return pl.pallas_call(
        message_kernel,
        out_shape=(
            jax.ShapeDtypeStruct((TWO + ONE, ROW, HALF), BF16),
            jax.ShapeDtypeStruct((1, ONE, ROW, HALF), BF16),
        ),
        in_specs=[SMEM] + [VMEM] * 9,
        out_specs=(VMEM, VMEM),
        compiler_params=SMALL,
        name="ring_message",
    )(pos, *twos, one, *blocks)


def join_kernel(*refs):
    for n, ref in enumerate(refs[:-1]):
        refs[-1][n] = ref[TWO:]


def join(*messages):
    return pl.pallas_call(
        join_kernel,
        out_shape=jax.ShapeDtypeStruct((len(messages), ONE, ROW, HALF), BF16),
        in_specs=[VMEM] * len(messages),
        out_specs=VMEM,
        compiler_params=SMALL,
        name="join_parts",
    )(*messages)


def prepare_kernel(pos, taper, mine, other, for_two, for_one, rows):
    lane = lax.broadcasted_iota(jnp.int32, (SUB, 2 * BLK), 1)
    first_col = (pos[0] * NZ + pos[1]) * 2

    def put(at, i, j):
        x, z = source(pos, i, j)
        row = pl.multiple_of((x * NZ + z) * SUB, SUB)
        for h, ref in enumerate((mine, other)):
            core = pos[3] if h == 0 else 1 - pos[3]
            tile = (pos[2] * 2 + core) * 8 + x * 2 + z // 4
            left = taper[tile, first_col].astype(F32)
            right = taper[tile, first_col + 1].astype(F32)
            keep = jnp.where(lane < BLK, left, right)
            rows[at + h * SUB:at + h * SUB + SUB, :] = (
                ref[pl.ds(row, SUB), :].astype(F32) * keep).astype(BF16)

    def block_two(j, carry):
        for i in range(NX):
            put(i * PAIR, i, j)
        for_two[j] = rows[:512].T
        return carry

    def block_one(c, carry):
        for i in range(NX):
            for s in range(2):
                put((2 * i + s) * PAIR, i, jnp.where(c == 0, 7 * s, 2 * c - 1 + s))
        for_one[c] = rows[...].T
        return carry

    lax.fori_loop(0, NZ, block_two, 0)
    lax.fori_loop(0, NZ // 2, block_one, 0)


def prepare(pos, taper, mine, other):
    return pl.pallas_call(
        prepare_kernel,
        out_shape=(
            jax.ShapeDtypeStruct((NZ, 512, 512), BF16),
            jax.ShapeDtypeStruct((NZ // 2, 512, 1024), BF16),
        ),
        in_specs=[SMEM, SMEM, VMEM, VMEM],
        out_specs=(VMEM, VMEM),
        scratch_shapes=[pltpu.VMEM((1024, 512), BF16)],
        compiler_params=SMALL,
        name="prepare_adjoint",
    )(pos, taper, mine, other)


def product_kernel(count, items, first, last, pos, adjoint, *refs):
    panels, refs = refs[:count], list(refs[count:])
    before = None if first else refs.pop(0)
    outs = [refs.pop(0) for _ in range(NY)] if last else None
    total, held, sems = refs
    for n, (_, parts) in enumerate(items):
        to = 0
        for index, start, size in parts:
            panel = panels[index].at[pl.ds(start, size)]
            if len(held.shape) == 5:
                panel = panel.at[:, pl.ds(0, PAIR // ROW)]
            pltpu.make_async_copy(panel, held.at[n, pl.ds(to, size)], sems.at[n]).start()
            to += size
    if first:
        total[...] = jnp.zeros_like(total)
    else:
        total[...] = before[...]
    begin = items[0][0]

    def step(n, carry):
        pltpu.make_async_copy(held.at[n], held.at[n], sems.at[n]).wait()
        total[...] += jnp.dot(
            adjoint[begin + n], held[n].reshape(-1, HALF), preferred_element_type=F32)
        return carry

    lax.fori_loop(0, len(items), step, 0)
    if last:
        for d, out in enumerate(outs):
            column = pl.multiple_of((pos[2] + d) % NY * 128, 128)
            out[...] = (-2.0 * total[:, pl.ds(column, 128)]).astype(out.dtype)


def product(pos, adjoint, panels, items, before=None, kind=None):
    last = kind is not None
    shape = (TWO,) if panels[0].ndim == 3 else (2 * NX, PAIR // ROW)
    column = jax.ShapeDtypeStruct((512, 128), F32)
    scratch = [pltpu.VMEM((512, HALF), F32)] if last else []
    scratch += [
        pltpu.VMEM((len(items),) + shape + (ROW, HALF), BF16),
        pltpu.SemaphoreType.DMA((len(items),)),
    ]
    extra = [] if before is None else [before]
    kernel = functools.partial(product_kernel, len(panels), tuple(items), before is None, last)
    return pl.pallas_call(
        kernel,
        out_shape=(column,) + (jax.ShapeDtypeStruct((512, 128), kind),) * 3
        if last else jax.ShapeDtypeStruct((512, HALF), F32),
        in_specs=[SMEM, VMEM] + [ANY] * len(panels) + [VMEM] * len(extra),
        out_specs=(VMEM,) * 4 if last else VMEM,
        scratch_shapes=scratch,
        compiler_params=SMALL,
        name="masked_product",
    )(pos, adjoint, *panels, *extra)


def factor_kernel(where, pos, inverse, inverse_other, *refs):
    panels, (out, out_other, held, diagonal, sem) = refs[:-5], refs[-5:]
    for i in range(NX):
        x = source(pos, i, 0)[0]

        @pl.when(x < 2)
        def _(i=i, x=x):
            for j in range(NZ):
                index, at = where[i][j]
                z = source(pos, i, j)[1]
                pltpu.make_async_copy(panels[index].at[at, ONE - 1], held.at[x * NZ + z], sem.at[0]).start()

    pltpu.make_async_copy(held, held, sem.at[0]).wait()
    for q in range(NY):
        diagonal[:, q] = held[:, :, q * 128:(q + 1) * 128]
    columns = diagonal[...].reshape(2 * NZ * SUB, 128)
    for left, result in ((inverse, out), (inverse_other, out_other)):
        value = jnp.dot(left[...].reshape(512, 1024), columns, preferred_element_type=F32)
        high = value.astype(BF16)
        low = (value - high.astype(F32)).astype(BF16)
        result[:, :, :128] = high.reshape(NY, 128, 128)
        result[:, :, 128:] = low.reshape(NY, 128, 128)


def factor(pos, inverse, inverse_other, panels, where):
    return pl.pallas_call(
        functools.partial(factor_kernel, where),
        out_shape=(jax.ShapeDtypeStruct((NY, 128, 256), BF16),) * 2,
        in_specs=[SMEM, VMEM, VMEM] + [ANY] * len(panels),
        out_specs=(VMEM, VMEM),
        scratch_shapes=[
            pltpu.VMEM((2 * NZ, ROW, HALF), BF16),
            pltpu.VMEM((2 * NZ, NY, ROW, 128), BF16),
            pltpu.SemaphoreType.DMA((1,)),
        ],
        compiler_params=SMALL,
        name="inverse_times_diagonal",
    )(pos, inverse, inverse_other, *panels)


def carried_kernel(mine, other, factors, factors_other, out, total):
    total[...] = jnp.zeros_like(total)

    def block(d, carry):
        left = jnp.concatenate([mine[d], other[d]], axis=1)
        right = jnp.concatenate([factors[d], factors_other[d]], axis=0)
        total[...] += jnp.dot(left, right, preferred_element_type=F32)
        return carry

    lax.fori_loop(0, NY, block, 0)
    out[...] = total[:, :128] + total[:, 128:]


def carried(mine, other, factors, factors_other):
    return pl.pallas_call(
        carried_kernel,
        out_shape=jax.ShapeDtypeStruct((512, 128), F32),
        in_specs=[VMEM] * 4,
        out_specs=VMEM,
        scratch_shapes=[pltpu.VMEM((512, 256), F32)],
        compiler_params=SMALL,
        name="carried_term",
    )(mine, other, factors, factors_other)


def local(adjoint, taper, panel_two, panel_one, incoming, inverse_factor):
    row, col = lax.axis_index("row"), lax.axis_index("col")
    pos = jnp.stack([col // NZ, col % NZ, row // 2, row % 2]).astype(jnp.int32)

    own, give = pack(pos, panel_two, panel_one)
    taken = core_swap(give)
    shards = jnp.concatenate([own, taken], axis=1)
    block, *blocks = top(pos, own, taken)
    two, one = shards[0], shards[1]

    def x_all(part):
        return [part] + [x_shift(part, d) for d in (1, -1, 2)]

    two, one, swapped = together(two, one, core_swap(adjoint))
    *two, inverse1, inverse3 = together(
        *x_all(two), y_shift(inverse_factor, 1), y_shift(inverse_factor, 3))
    blocks = [y_first(part, d + 1) for d, part in enumerate(blocks)]
    own, part = message(pos, two, one, [block] + blocks)
    own, part, later = together(own, part, inverse_factor)
    inverse = jnp.stack([inverse_factor, inverse1, y_shift(later, 2), inverse3])
    down1, up1, inverse, *first_x = together(
        z_shift(own, 1), z_shift(own, -1), inverse, *x_all(part))

    for_two, for_one = prepare(pos, taper, adjoint, swapped)
    down2, up2, for_two, for_one, *near = together(
        z_shift(down1, 1), z_shift(up1, -1), for_two, for_one, *x_all(join(down1, up1)))
    inverse, down2, up2 = together(inverse, down2, up2)
    inverse_other = core_swap(inverse)
    sums = product(
        pos, for_two, [own, down1, up1, down2, up2], [(j, [(j, 0, TWO)]) for j in range(5)])
    down3, up3, sums, *middle = together(
        z_shift(down2, 1), z_shift(up2, -1), sums, *x_all(join(down2, up2)))
    sums = product(pos, for_two, [down3, up3], [(5 + j, [(j, 0, TWO)]) for j in range(2)], sums)
    sums_one = product(
        pos, for_one, near + middle,
        [(1 + c, [(NX * c + i, 0, 2) for i in range(NX)]) for c in range(2)])
    third = x_all(join(down3, up3))
    far_low, far_high, sums, sums_one = together(
        z_shift(down3[:TWO // 2], 1), z_shift(up3[TWO // 2:], -1), sums, sums_one)

    mine, *sent = product(
        pos, for_two, [far_low, far_high], [(7, [(0, 0, TWO // 2), (1, 0, TWO // 2)])], sums, F32)
    last = x_all(far_high[None, TWO // 2:])
    sums_one = product(pos, for_one, third, [(3, [(i, 0, 2) for i in range(NX)])], sums_one)
    r1, r2, r3, sums_one, *last = together(
        *[y_shift(part, d + 1) for d, part in enumerate(sent)], sums_one, *last)
    second_grad = incoming + ((mine + r1) + (r2 + r3))
    rounded = second_grad.astype(BF16)

    sums_one = product(
        pos, for_one, first_x + last,
        [(0, [(NX * s + i, 0, 1) for i in range(NX) for s in range(2)])], sums_one, BF16)
    where = tuple(
        ((i, 0),) + tuple((NX * (1 + j // 2) + i, j % 2) for j in range(7)) for i in range(NX))
    factors = factor(pos, inverse, inverse_other, first_x + near + middle + third + last, where)
    s1, s2, s3, mine, *sent = together(*[y_shift(rounded, d) for d in range(1, NY)], *sums_one)
    rounded = jnp.stack([rounded, s1, s2, s3])
    rounded_other = core_swap(rounded)
    r1, r2, r3 = [y_shift(part, d + 1).astype(F32) for d, part in enumerate(sent)]
    term = carried(rounded, rounded_other, *factors)
    return second_grad, (mine + r1) + (r2 + r3) - term


def solution(mesh):
    in_specs = (
        P("row", "col"),
        P(),
        P(("row", "col"), None),
        P(("row", "col"), None),
        P("col", "row"),
        P("row", None),
    )
    out_specs = (P("col", "row"), P("col", "row"))
    return jax.shard_map(local, mesh=mesh, in_specs=in_specs, out_specs=out_specs, check_vma=False)
```

```python
import functools

import jax
import jax.numpy as jnp
from jax import lax
from jax.experimental import pallas as pl
from jax.experimental.pallas import tpu as pltpu
from jax.sharding import PartitionSpec as P

BLK = 256
NX, NZ, NY = 4, 8, 4
SUB = 64
PAIR = 2 * SUB
HALF = 512
ROW = 16
ONE = PAIR // ROW + 1
TWO = NX * PAIR // ROW
F32, BF16 = jnp.float32, jnp.bfloat16
VMEM = pl.BlockSpec(memory_space=pltpu.VMEM)
SMEM = pl.BlockSpec(memory_space=pltpu.SMEM)
ANY = pl.BlockSpec(memory_space=pl.ANY)
BIG = pltpu.CompilerParams(vmem_limit_bytes=24 * 2**20)
SMALL = pltpu.CompilerParams(vmem_limit_bytes=16 * 2**20)


def x_shift(value, dx):
    pairs = [(x * NZ + z, (x + dx) % NX * NZ + z) for x in range(NX) for z in range(NZ)]
    return lax.ppermute(value, "col", pairs)


def z_shift(value, dz):
    pairs = [(x * NZ + z, x * NZ + (z + dz) % NZ) for x in range(NX) for z in range(NZ)]
    return lax.ppermute(value, "col", pairs)


def y_shift(value, dy):
    pairs = [(y * 2 + k, (y + dy) % NY * 2 + k) for y in range(NY) for k in range(2)]
    return lax.ppermute(value, "row", pairs)


def y_first(value, y):
    return lax.ppermute(value, "row", [(k, y * 2 + k) for k in range(2)])


def core_swap(value):
    return lax.ppermute(value, "row", [(r, r ^ 1) for r in range(2 * NY)])


def together(*values):
    return lax.optimization_barrier(values)


def offset(n):
    return ((n + 1) // 2) * (1 - 2 * (n % 2))


def source(pos, i, j):
    return (pos[0] + offset(i) + NX) % NX, (pos[1] + offset(j) + NZ) % NZ


def pack_kernel(pos, two, one, own, give, held, sems):
    copies = [pltpu.make_async_copy(ref, held.at[n], sems.at[n]) for n, ref in enumerate((two, one))]
    for copy in copies:
        copy.start()
    first = pos[3] == 0
    for n, copy in enumerate(copies):
        copy.wait()
        for q in range(NY):
            at = slice(q * 128, q * 128 + 128)
            left = held[n, :, q * 256:q * 256 + 128]
            right = held[n, :, q * 256 + 128:q * 256 + 256]
            own[n, :, at] = jnp.where(first, left, right)
            give[n, :, at] = jnp.where(first, right, left)


def pack(pos, two, one):
    return pl.pallas_call(
        pack_kernel,
        out_shape=(jax.ShapeDtypeStruct((2, SUB, HALF), BF16),) * 2,
        in_specs=[SMEM, ANY, ANY],
        out_specs=(VMEM, VMEM),
        scratch_shapes=[pltpu.VMEM((2, SUB, 2 * HALF), BF16), pltpu.SemaphoreType.DMA((2,))],
        compiler_params=SMALL,
        name="pack_columns",
    )(pos, two, one)


def top_kernel(pos, own, taken, *outs):
    first = pos[3] == 0
    for y, out in enumerate(outs):
        at = slice(y * 128, y * 128 + 128)
        out[...] = jnp.where(first, own[1, :, at], taken[1, :, at])


def top(pos, own, taken):
    return pl.pallas_call(
        top_kernel,
        out_shape=(jax.ShapeDtypeStruct((SUB, 128), BF16),) * NY,
        in_specs=[SMEM, VMEM, VMEM],
        out_specs=(VMEM,) * NY,
        compiler_params=SMALL,
        name="diagonal_blocks",
    )(pos, own, taken)


def message_kernel(pos, two, down, up, far, one, own, b1, b2, b3, out):
    for n, ref in enumerate((two, down, up, far)):
        out[n * 8:n * 8 + 8] = ref[...].reshape(8, ROW, HALF)
    rows = one[...].reshape(8, ROW, HALF)
    out[TWO:TWO + 8] = rows
    sent = (b1[...] + b2[...]) + b3[...]
    columns = jnp.where(pos[2] == 0, own[...], sent)
    for q in range(NY):
        at = slice(q * 128, q * 128 + 128)
        out[TWO + 8, :, at] = columns[q * ROW:(q + 1) * ROW]


def message(pos, twos, one, blocks):
    return pl.pallas_call(
        message_kernel,
        out_shape=jax.ShapeDtypeStruct((TWO + ONE, ROW, HALF), BF16),
        in_specs=[SMEM] + [VMEM] * 9,
        out_specs=VMEM,
        compiler_params=SMALL,
        name="ring_message",
    )(pos, *twos, one, *blocks)


def join_kernel(*refs):
    for n, ref in enumerate(refs[:-1]):
        refs[-1][n] = ref[ref.shape[0] - ONE:]


def join(*messages):
    return pl.pallas_call(
        join_kernel,
        out_shape=jax.ShapeDtypeStruct((len(messages), ONE, ROW, HALF), BF16),
        in_specs=[VMEM] * len(messages),
        out_specs=VMEM,
        compiler_params=SMALL,
        name="join_parts",
    )(*messages)


def prepare_kernel(pos, taper, mine, other, for_two, for_one, rows):
    lane = lax.broadcasted_iota(jnp.int32, (SUB, 2 * BLK), 1)
    first_col = (pos[0] * NZ + pos[1]) * 2

    def put(at, i, j):
        x, z = source(pos, i, j)
        row = pl.multiple_of((x * NZ + z) * SUB, SUB)
        for h, ref in enumerate((mine, other)):
            core = pos[3] if h == 0 else 1 - pos[3]
            tile = (pos[2] * 2 + core) * 8 + x * 2 + z // 4
            left = taper[tile, first_col].astype(F32)
            right = taper[tile, first_col + 1].astype(F32)
            keep = jnp.where(lane < BLK, left, right)
            rows[at + h * SUB:at + h * SUB + SUB, :] = (
                ref[pl.ds(row, SUB), :].astype(F32) * keep).astype(BF16)

    def block_two(j, carry):
        for i in range(NX):
            put(i * PAIR, i, j)
        for_two[j] = rows[:512].T
        return carry

    def block_one(c, carry):
        for i in range(NX):
            for s in range(2):
                put((2 * i + s) * PAIR, i, jnp.where(c == 0, 7 * s, 2 * c - 1 + s))
        for_one[c] = rows[...].T
        return carry

    lax.fori_loop(0, NZ, block_two, 0)
    lax.fori_loop(0, NZ // 2, block_one, 0)


def prepare(pos, taper, mine, other):
    return pl.pallas_call(
        prepare_kernel,
        out_shape=(
            jax.ShapeDtypeStruct((NZ, 512, 512), BF16),
            jax.ShapeDtypeStruct((NZ // 2, 512, 1024), BF16),
        ),
        in_specs=[SMEM, SMEM, VMEM, VMEM],
        out_specs=(VMEM, VMEM),
        scratch_shapes=[pltpu.VMEM((1024, 512), BF16)],
        compiler_params=SMALL,
        name="prepare_adjoint",
    )(pos, taper, mine, other)


def product_kernel(count, items, first, last, pos, adjoint, *refs):
    panels, refs = refs[:count], list(refs[count:])
    before = None if first else refs.pop(0)
    outs = [refs.pop(0) for _ in range(NY)] if last else None
    total, held, sems = refs
    for n, (_, parts) in enumerate(items):
        to = 0
        for index, start, size in parts:
            panel = panels[index].at[pl.ds(start, size)]
            if len(held.shape) == 5:
                panel = panel.at[:, pl.ds(0, PAIR // ROW)]
            pltpu.make_async_copy(panel, held.at[n, pl.ds(to, size)], sems.at[n]).start()
            to += size
    if first:
        total[...] = jnp.zeros_like(total)
    else:
        total[...] = before[...]
    begin = items[0][0]

    def step(n, carry):
        pltpu.make_async_copy(held.at[n], held.at[n], sems.at[n]).wait()
        total[...] += jnp.dot(
            adjoint[begin + n], held[n].reshape(-1, HALF), preferred_element_type=F32)
        return carry

    lax.fori_loop(0, len(items), step, 0)
    if last:
        for d, out in enumerate(outs):
            column = pl.multiple_of((pos[2] + d) % NY * 128, 128)
            out[...] = (-2.0 * total[:, pl.ds(column, 128)]).astype(out.dtype)


def product(pos, adjoint, panels, items, before=None, kind=None):
    last = kind is not None
    shape = (TWO,) if panels[0].ndim == 3 else (2 * NX, PAIR // ROW)
    column = jax.ShapeDtypeStruct((512, 128), F32)
    scratch = [pltpu.VMEM((512, HALF), F32)] if last else []
    scratch += [
        pltpu.VMEM((len(items),) + shape + (ROW, HALF), BF16),
        pltpu.SemaphoreType.DMA((len(items),)),
    ]
    extra = [] if before is None else [before]
    kernel = functools.partial(product_kernel, len(panels), tuple(items), before is None, last)
    return pl.pallas_call(
        kernel,
        out_shape=(column,) + (jax.ShapeDtypeStruct((512, 128), kind),) * 3
        if last else jax.ShapeDtypeStruct((512, HALF), F32),
        in_specs=[SMEM, VMEM] + [ANY] * len(panels) + [VMEM] * len(extra),
        out_specs=(VMEM,) * 4 if last else VMEM,
        scratch_shapes=scratch,
        compiler_params=SMALL,
        name="masked_product",
    )(pos, adjoint, *panels, *extra)


def factor_kernel(where, pos, inverse, inverse_other, *refs):
    panels, (out, out_other, held, diagonal, sem) = refs[:-5], refs[-5:]
    for i in range(NX):
        x = source(pos, i, 0)[0]

        @pl.when(x < 2)
        def _(i=i, x=x):
            for j in range(NZ):
                index, at = where[i][j]
                z = source(pos, i, j)[1]
                pltpu.make_async_copy(panels[index].at[at, ONE - 1], held.at[x * NZ + z], sem.at[0]).start()

    pltpu.make_async_copy(held, held, sem.at[0]).wait()
    for q in range(NY):
        diagonal[:, q] = held[:, :, q * 128:(q + 1) * 128]
    columns = diagonal[...].reshape(2 * NZ * SUB, 128)
    for left, result in ((inverse, out), (inverse_other, out_other)):
        value = jnp.dot(left[...].reshape(512, 1024), columns, preferred_element_type=F32)
        high = value.astype(BF16)
        low = (value - high.astype(F32)).astype(BF16)
        result[:, :, :128] = high.reshape(NY, 128, 128)
        result[:, :, 128:] = low.reshape(NY, 128, 128)


def factor(pos, inverse, inverse_other, panels, where):
    return pl.pallas_call(
        functools.partial(factor_kernel, where),
        out_shape=(jax.ShapeDtypeStruct((NY, 128, 256), BF16),) * 2,
        in_specs=[SMEM, VMEM, VMEM] + [ANY] * len(panels),
        out_specs=(VMEM, VMEM),
        scratch_shapes=[
            pltpu.VMEM((2 * NZ, ROW, HALF), BF16),
            pltpu.VMEM((2 * NZ, NY, ROW, 128), BF16),
            pltpu.SemaphoreType.DMA((1,)),
        ],
        compiler_params=SMALL,
        name="inverse_times_diagonal",
    )(pos, inverse, inverse_other, *panels)


def carried_kernel(mine, other, factors, factors_other, out, total):
    total[...] = jnp.zeros_like(total)

    def block(d, carry):
        left = jnp.concatenate([mine[d], other[d]], axis=1)
        right = jnp.concatenate([factors[d], factors_other[d]], axis=0)
        total[...] += jnp.dot(left, right, preferred_element_type=F32)
        return carry

    lax.fori_loop(0, NY, block, 0)
    out[...] = total[:, :128] + total[:, 128:]


def carried(mine, other, factors, factors_other):
    return pl.pallas_call(
        carried_kernel,
        out_shape=jax.ShapeDtypeStruct((512, 128), F32),
        in_specs=[VMEM] * 4,
        out_specs=VMEM,
        scratch_shapes=[pltpu.VMEM((512, 256), F32)],
        compiler_params=SMALL,
        name="carried_term",
    )(mine, other, factors, factors_other)


def local(adjoint, taper, panel_two, panel_one, incoming, inverse_factor):
    row, col = lax.axis_index("row"), lax.axis_index("col")
    pos = jnp.stack([col // NZ, col % NZ, row // 2, row % 2]).astype(jnp.int32)

    own, give = pack(pos, panel_two, panel_one)
    taken = core_swap(give)
    shards = jnp.concatenate([own, taken], axis=1)
    block, *blocks = top(pos, own, taken)
    two, one = shards[0], shards[1]

    def x_all(part):
        return [part] + [x_shift(part, d) for d in (1, -1, 2)]

    two, one, swapped = together(two, one, core_swap(adjoint))
    twos = together(*x_all(two))
    blocks = [y_first(part, d + 1) for d, part in enumerate(blocks)]
    own, later = together(message(pos, twos, one, [block] + blocks), inverse_factor)
    inverse = jnp.stack([later] + [y_shift(later, d) for d in range(1, NY)])
    down1, up1, inverse = together(z_shift(own, 1), z_shift(own, -1), inverse)

    for_two, for_one = prepare(pos, taper, adjoint, swapped)
    down2, up2, for_two, for_one, *near = together(
        z_shift(down1, 1), z_shift(up1, -1), for_two, for_one, *x_all(join(down1, up1)))
    inverse, down2, up2 = together(inverse, down2, up2)
    inverse_other = core_swap(inverse)
    sums = product(
        pos, for_two, [own, down1, up1, down2, up2], [(j, [(j, 0, TWO)]) for j in range(5)])
    sums_one = product(pos, for_one, near, [(1, [(i, 0, 2) for i in range(NX)])])
    down3, up3, sums, sums_one, *middle = together(
        z_shift(down2, 1), z_shift(up2, -1), sums, sums_one, *x_all(join(down2, up2)))
    sums = product(pos, for_two, [down3, up3], [(5 + j, [(j, 0, TWO)]) for j in range(2)], sums)
    sums_one = product(pos, for_one, middle, [(2, [(i, 0, 2) for i in range(NX)])], sums_one)
    third = x_all(join(down3, up3))
    far_low, far_high, sums, sums_one = together(
        z_shift(down3[:TWO // 2], 1), z_shift(up3[TWO // 2:], -1), sums, sums_one)

    mine, *sent = product(
        pos, for_two, [far_low, far_high], [(7, [(0, 0, TWO // 2), (1, 0, TWO // 2)])], sums, F32)
    last = x_all(join(own, far_high))
    sums_one = product(pos, for_one, third, [(3, [(i, 0, 2) for i in range(NX)])], sums_one)
    r1, r2, r3, sums_one = together(*[y_shift(part, d + 1) for d, part in enumerate(sent)], sums_one)
    second_grad = incoming + ((mine + r1) + (r2 + r3))
    rounded = second_grad.astype(BF16)

    sums_one = product(pos, for_one, last, [(0, [(i, 0, 2) for i in range(NX)])], sums_one, BF16)
    where = tuple(
        ((3 * NX + i, 0),) + tuple((NX * (j // 2) + i, j % 2) for j in range(6)) + ((3 * NX + i, 1),)
        for i in range(NX))
    factors = factor(pos, inverse, inverse_other, near + middle + third + last, where)
    s1, s2, s3, mine, *sent = together(*[y_shift(rounded, d) for d in range(1, NY)], *sums_one)
    rounded = jnp.stack([rounded, s1, s2, s3])
    rounded_other = core_swap(rounded)
    r1, r2, r3 = [y_shift(part, d + 1).astype(F32) for d, part in enumerate(sent)]
    term = carried(rounded, rounded_other, *factors)
    return second_grad, (mine + r1) + (r2 + r3) - term


def solution(mesh):
    in_specs = (
        P("row", "col"),
        P(),
        P(("row", "col"), None),
        P(("row", "col"), None),
        P("col", "row"),
        P("row", None),
    )
    out_specs = (P("col", "row"), P("col", "row"))
    return jax.shard_map(local, mesh=mesh, in_specs=in_specs, out_specs=out_specs, check_vma=False)
```

```python
import functools

import jax
import jax.numpy as jnp
from jax import lax
from jax.experimental import pallas as pl
from jax.experimental.pallas import tpu as pltpu
from jax.sharding import PartitionSpec as P

BLK = 256
NX, NZ, NY = 4, 8, 4
SUB = 64
PAIR = 2 * SUB
HALF = 512
ROW = 16
ONE = PAIR // ROW + 1
TWO = NX * PAIR // ROW
F32, BF16 = jnp.float32, jnp.bfloat16
VMEM = pl.BlockSpec(memory_space=pltpu.VMEM)
SMEM = pl.BlockSpec(memory_space=pltpu.SMEM)
ANY = pl.BlockSpec(memory_space=pl.ANY)
BIG = pltpu.CompilerParams(vmem_limit_bytes=24 * 2**20)
SMALL = pltpu.CompilerParams(vmem_limit_bytes=16 * 2**20)


def x_shift(value, dx):
    pairs = [(x * NZ + z, (x + dx) % NX * NZ + z) for x in range(NX) for z in range(NZ)]
    return lax.ppermute(value, "col", pairs)


def z_shift(value, dz):
    pairs = [(x * NZ + z, x * NZ + (z + dz) % NZ) for x in range(NX) for z in range(NZ)]
    return lax.ppermute(value, "col", pairs)


def y_shift(value, dy):
    pairs = [(y * 2 + k, (y + dy) % NY * 2 + k) for y in range(NY) for k in range(2)]
    return lax.ppermute(value, "row", pairs)


def y_first(value, y):
    return lax.ppermute(value, "row", [(k, y * 2 + k) for k in range(2)])


def core_swap(value):
    return lax.ppermute(value, "row", [(r, r ^ 1) for r in range(2 * NY)])


def together(*values):
    return lax.optimization_barrier(values)


def offset(n):
    return ((n + 1) // 2) * (1 - 2 * (n % 2))


def source(pos, i, j):
    return (pos[0] + offset(i) + NX) % NX, (pos[1] + offset(j) + NZ) % NZ


def pack_kernel(pos, two, one, own, give, held, sems):
    copies = [pltpu.make_async_copy(ref, held.at[n], sems.at[n]) for n, ref in enumerate((two, one))]
    for copy in copies:
        copy.start()
    first = pos[3] == 0
    for n, copy in enumerate(copies):
        copy.wait()
        for q in range(NY):
            at = slice(q * 128, q * 128 + 128)
            left = held[n, :, q * 256:q * 256 + 128]
            right = held[n, :, q * 256 + 128:q * 256 + 256]
            own[n, :, at] = jnp.where(first, left, right)
            give[n, :, at] = jnp.where(first, right, left)


def pack(pos, two, one):
    return pl.pallas_call(
        pack_kernel,
        out_shape=(jax.ShapeDtypeStruct((2, SUB, HALF), BF16),) * 2,
        in_specs=[SMEM, ANY, ANY],
        out_specs=(VMEM, VMEM),
        scratch_shapes=[pltpu.VMEM((2, SUB, 2 * HALF), BF16), pltpu.SemaphoreType.DMA((2,))],
        compiler_params=SMALL,
        name="pack_columns",
    )(pos, two, one)


def top_kernel(pos, own, taken, *outs):
    first = pos[3] == 0
    for y, out in enumerate(outs):
        at = slice(y * 128, y * 128 + 128)
        out[...] = jnp.where(first, own[1, :, at], taken[1, :, at])


def top(pos, own, taken):
    return pl.pallas_call(
        top_kernel,
        out_shape=(jax.ShapeDtypeStruct((SUB, 128), BF16),) * NY,
        in_specs=[SMEM, VMEM, VMEM],
        out_specs=(VMEM,) * NY,
        compiler_params=SMALL,
        name="diagonal_blocks",
    )(pos, own, taken)


def message_kernel(pos, two, down, up, far, one, own, b1, b2, b3, out, part):
    for n, ref in enumerate((two, down, up, far)):
        out[n * 8:n * 8 + 8] = ref[...].reshape(8, ROW, HALF)
    rows = one[...].reshape(8, ROW, HALF)
    out[TWO:TWO + 8] = rows
    part[0, :8] = rows
    sent = (b1[...] + b2[...]) + b3[...]
    columns = jnp.where(pos[2] == 0, own[...], sent)
    for q in range(NY):
        at = slice(q * 128, q * 128 + 128)
        out[TWO + 8, :, at] = columns[q * ROW:(q + 1) * ROW]
        part[0, 8, :, at] = columns[q * ROW:(q + 1) * ROW]


def message(pos, twos, one, blocks):
    return pl.pallas_call(
        message_kernel,
        out_shape=(
            jax.ShapeDtypeStruct((TWO + ONE, ROW, HALF), BF16),
            jax.ShapeDtypeStruct((1, ONE, ROW, HALF), BF16),
        ),
        in_specs=[SMEM] + [VMEM] * 9,
        out_specs=(VMEM, VMEM),
        compiler_params=SMALL,
        name="ring_message",
    )(pos, *twos, one, *blocks)


def join_kernel(*refs):
    for n, ref in enumerate(refs[:-1]):
        refs[-1][n] = ref[ref.shape[0] - ONE:]


def join(*messages):
    return pl.pallas_call(
        join_kernel,
        out_shape=jax.ShapeDtypeStruct((len(messages), ONE, ROW, HALF), BF16),
        in_specs=[VMEM] * len(messages),
        out_specs=VMEM,
        compiler_params=SMALL,
        name="join_parts",
    )(*messages)


def prepare_kernel(pos, taper, mine, other, for_two, for_one, rows):
    lane = lax.broadcasted_iota(jnp.int32, (SUB, 2 * BLK), 1)
    first_col = (pos[0] * NZ + pos[1]) * 2

    def put(at, i, j):
        x, z = source(pos, i, j)
        row = pl.multiple_of((x * NZ + z) * SUB, SUB)
        for h, ref in enumerate((mine, other)):
            core = pos[3] if h == 0 else 1 - pos[3]
            tile = (pos[2] * 2 + core) * 8 + x * 2 + z // 4
            left = taper[tile, first_col].astype(F32)
            right = taper[tile, first_col + 1].astype(F32)
            keep = jnp.where(lane < BLK, left, right)
            rows[at + h * SUB:at + h * SUB + SUB, :] = (
                ref[pl.ds(row, SUB), :].astype(F32) * keep).astype(BF16)

    def block_two(j, carry):
        for i in range(NX):
            put(i * PAIR, i, j)
        for_two[j] = rows[:512].T
        return carry

    def block_one(c, carry):
        for i in range(NX):
            for s in range(2):
                put((2 * i + s) * PAIR, i, jnp.where(c == 0, 7 * s, 2 * c - 1 + s))
        for_one[c] = rows[...].T
        return carry

    lax.fori_loop(0, NZ, block_two, 0)
    lax.fori_loop(0, NZ // 2, block_one, 0)


def prepare(pos, taper, mine, other):
    return pl.pallas_call(
        prepare_kernel,
        out_shape=(
            jax.ShapeDtypeStruct((NZ, 512, 512), BF16),
            jax.ShapeDtypeStruct((NZ // 2, 512, 1024), BF16),
        ),
        in_specs=[SMEM, SMEM, VMEM, VMEM],
        out_specs=(VMEM, VMEM),
        scratch_shapes=[pltpu.VMEM((1024, 512), BF16)],
        compiler_params=SMALL,
        name="prepare_adjoint",
    )(pos, taper, mine, other)


def product_kernel(count, items, first, last, pos, adjoint, *refs):
    panels, refs = refs[:count], list(refs[count:])
    before = None if first else refs.pop(0)
    outs = [refs.pop(0) for _ in range(NY)] if last else None
    total, held, sems = refs
    for n, (_, parts) in enumerate(items):
        to = 0
        for index, start, size in parts:
            panel = panels[index].at[pl.ds(start, size)]
            if len(held.shape) == 5:
                panel = panel.at[:, pl.ds(0, PAIR // ROW)]
            pltpu.make_async_copy(panel, held.at[n, pl.ds(to, size)], sems.at[n]).start()
            to += size
    if first:
        total[...] = jnp.zeros_like(total)
    else:
        total[...] = before[...]
    begin = items[0][0]

    def step(n, carry):
        pltpu.make_async_copy(held.at[n], held.at[n], sems.at[n]).wait()
        total[...] += jnp.dot(
            adjoint[begin + n], held[n].reshape(-1, HALF), preferred_element_type=F32)
        return carry

    lax.fori_loop(0, len(items), step, 0)
    if last:
        for d, out in enumerate(outs):
            column = pl.multiple_of((pos[2] + d) % NY * 128, 128)
            out[...] = (-2.0 * total[:, pl.ds(column, 128)]).astype(out.dtype)


def product(pos, adjoint, panels, items, before=None, kind=None):
    last = kind is not None
    shape = (TWO,) if panels[0].ndim == 3 else (2 * NX, PAIR // ROW)
    column = jax.ShapeDtypeStruct((512, 128), F32)
    scratch = [pltpu.VMEM((512, HALF), F32)] if last else []
    scratch += [
        pltpu.VMEM((len(items),) + shape + (ROW, HALF), BF16),
        pltpu.SemaphoreType.DMA((len(items),)),
    ]
    extra = [] if before is None else [before]
    kernel = functools.partial(product_kernel, len(panels), tuple(items), before is None, last)
    return pl.pallas_call(
        kernel,
        out_shape=(column,) + (jax.ShapeDtypeStruct((512, 128), kind),) * 3
        if last else jax.ShapeDtypeStruct((512, HALF), F32),
        in_specs=[SMEM, VMEM] + [ANY] * len(panels) + [VMEM] * len(extra),
        out_specs=(VMEM,) * 4 if last else VMEM,
        scratch_shapes=scratch,
        compiler_params=SMALL,
        name="masked_product",
    )(pos, adjoint, *panels, *extra)


def factor_kernel(where, pos, inverse, inverse_other, *refs):
    panels, (out, out_other, held, diagonal, sem) = refs[:-5], refs[-5:]
    for i in range(NX):
        x = source(pos, i, 0)[0]

        @pl.when(x < 2)
        def _(i=i, x=x):
            for j in range(NZ):
                index, at = where[i][j]
                z = source(pos, i, j)[1]
                pltpu.make_async_copy(panels[index].at[at, ONE - 1], held.at[x * NZ + z], sem.at[0]).start()

    pltpu.make_async_copy(held, held, sem.at[0]).wait()
    for q in range(NY):
        diagonal[:, q] = held[:, :, q * 128:(q + 1) * 128]
    columns = diagonal[...].reshape(2 * NZ * SUB, 128)
    for left, result in ((inverse, out), (inverse_other, out_other)):
        value = jnp.dot(left[...].reshape(512, 1024), columns, preferred_element_type=F32)
        high = value.astype(BF16)
        low = (value - high.astype(F32)).astype(BF16)
        result[:, :, :128] = high.reshape(NY, 128, 128)
        result[:, :, 128:] = low.reshape(NY, 128, 128)


def factor(pos, inverse, inverse_other, panels, where):
    return pl.pallas_call(
        functools.partial(factor_kernel, where),
        out_shape=(jax.ShapeDtypeStruct((NY, 128, 256), BF16),) * 2,
        in_specs=[SMEM, VMEM, VMEM] + [ANY] * len(panels),
        out_specs=(VMEM, VMEM),
        scratch_shapes=[
            pltpu.VMEM((2 * NZ, ROW, HALF), BF16),
            pltpu.VMEM((2 * NZ, NY, ROW, 128), BF16),
            pltpu.SemaphoreType.DMA((1,)),
        ],
        compiler_params=SMALL,
        name="inverse_times_diagonal",
    )(pos, inverse, inverse_other, *panels)


def carried_kernel(mine, other, factors, factors_other, out, total):
    total[...] = jnp.zeros_like(total)

    def block(d, carry):
        left = jnp.concatenate([mine[d], other[d]], axis=1)
        right = jnp.concatenate([factors[d], factors_other[d]], axis=0)
        total[...] += jnp.dot(left, right, preferred_element_type=F32)
        return carry

    lax.fori_loop(0, NY, block, 0)
    out[...] = total[:, :128] + total[:, 128:]


def carried(mine, other, factors, factors_other):
    return pl.pallas_call(
        carried_kernel,
        out_shape=jax.ShapeDtypeStruct((512, 128), F32),
        in_specs=[VMEM] * 4,
        out_specs=VMEM,
        scratch_shapes=[pltpu.VMEM((512, 256), F32)],
        compiler_params=SMALL,
        name="carried_term",
    )(mine, other, factors, factors_other)


def local(adjoint, taper, panel_two, panel_one, incoming, inverse_factor):
    row, col = lax.axis_index("row"), lax.axis_index("col")
    pos = jnp.stack([col // NZ, col % NZ, row // 2, row % 2]).astype(jnp.int32)

    own, give = pack(pos, panel_two, panel_one)
    taken = core_swap(give)
    shards = jnp.concatenate([own, taken], axis=1)
    block, *blocks = top(pos, own, taken)
    two, one = shards[0], shards[1]

    def x_all(part):
        return [part] + [x_shift(part, d) for d in (1, -1, 2)]

    two, one, swapped = together(two, one, core_swap(adjoint))
    *two, inverse1, inverse3 = together(
        *x_all(two), y_shift(inverse_factor, 1), y_shift(inverse_factor, 3))
    blocks = [y_first(part, d + 1) for d, part in enumerate(blocks)]
    own, part = message(pos, two, one, [block] + blocks)
    own, part, later = together(own, part, inverse_factor)
    inverse = jnp.stack([inverse_factor, inverse1, y_shift(later, 2), inverse3])
    down1, up1, inverse, *first_x = together(
        z_shift(own, 1), z_shift(own, -1), inverse, *x_all(part))

    for_two, for_one = prepare(pos, taper, adjoint, swapped)
    down2, up2, for_two, for_one, *near = together(
        z_shift(down1, 1), z_shift(up1, -1), for_two, for_one, *x_all(join(down1, up1)))
    inverse, down2, up2 = together(inverse, down2, up2)
    inverse_other = core_swap(inverse)
    sums = product(
        pos, for_two, [own, down1, up1, down2, up2], [(j, [(j, 0, TWO)]) for j in range(5)])
    down3, up3, sums, *middle = together(
        z_shift(down2, 1), z_shift(up2, -1), sums, *x_all(join(down2, up2)))
    sums = product(pos, for_two, [down3, up3], [(5 + j, [(j, 0, TWO)]) for j in range(2)], sums)
    sums_one = product(
        pos, for_one, near + middle,
        [(1 + c, [(NX * c + i, 0, 2) for i in range(NX)]) for c in range(2)])
    far_low, far_high, sums, sums_one = together(
        z_shift(down3[:TWO // 2], 1), z_shift(up3[TWO // 2:], -1), sums, sums_one)

    mine, *sent = product(
        pos, for_two, [far_low, far_high], [(7, [(0, 0, TWO // 2), (1, 0, TWO // 2)])], sums, F32)
    sent = [y_shift(part, d + 1) for d, part in enumerate(sent)]
    third = x_all(join(down3, up3, far_high))
    r1, r2, r3 = together(*sent)
    second_grad = incoming + ((mine + r1) + (r2 + r3))
    rounded = second_grad.astype(BF16)

    sums_one = product(pos, for_one, third, [(3, [(i, 0, 2) for i in range(NX)])], sums_one)
    sums_one = product(
        pos, for_one, first_x + third,
        [(0, [(NX * s + i, 2 * s, 1) for i in range(NX) for s in range(2)])], sums_one, BF16)
    where = tuple(
        ((i, 0),) + tuple((NX * (1 + j // 2) + i, j % 2) for j in range(6)) + ((3 * NX + i, 2),)
        for i in range(NX))
    factors = factor(pos, inverse, inverse_other, first_x + near + middle + third, where)
    s1, s2, s3, mine, *sent = together(*[y_shift(rounded, d) for d in range(1, NY)], *sums_one)
    rounded = jnp.stack([rounded, s1, s2, s3])
    rounded_other = core_swap(rounded)
    r1, r2, r3 = [y_shift(part, d + 1).astype(F32) for d, part in enumerate(sent)]
    term = carried(rounded, rounded_other, *factors)
    return second_grad, (mine + r1) + (r2 + r3) - term


def solution(mesh):
    in_specs = (
        P("row", "col"),
        P(),
        P(("row", "col"), None),
        P(("row", "col"), None),
        P("col", "row"),
        P("row", None),
    )
    out_specs = (P("col", "row"), P("col", "row"))
    return jax.shard_map(local, mesh=mesh, in_specs=in_specs, out_specs=out_specs, check_vma=False)
```

```python
import functools

import jax
import jax.numpy as jnp
from jax import lax
from jax.experimental import pallas as pl
from jax.experimental.pallas import tpu as pltpu
from jax.sharding import PartitionSpec as P

BLK = 256
NX, NZ, NY = 4, 8, 4
SUB = 64
PAIR = 2 * SUB
HALF = 512
ROW = 16
ONE = PAIR // ROW + 1
TWO = NX * PAIR // ROW
F32, BF16 = jnp.float32, jnp.bfloat16
VMEM = pl.BlockSpec(memory_space=pltpu.VMEM)
SMEM = pl.BlockSpec(memory_space=pltpu.SMEM)
ANY = pl.BlockSpec(memory_space=pl.ANY)
BIG = pltpu.CompilerParams(vmem_limit_bytes=24 * 2**20)
SMALL = pltpu.CompilerParams(vmem_limit_bytes=16 * 2**20)


def x_shift(value, dx):
    pairs = [(x * NZ + z, (x + dx) % NX * NZ + z) for x in range(NX) for z in range(NZ)]
    return lax.ppermute(value, "col", pairs)


def z_shift(value, dz):
    pairs = [(x * NZ + z, x * NZ + (z + dz) % NZ) for x in range(NX) for z in range(NZ)]
    return lax.ppermute(value, "col", pairs)


def y_shift(value, dy):
    pairs = [(y * 2 + k, (y + dy) % NY * 2 + k) for y in range(NY) for k in range(2)]
    return lax.ppermute(value, "row", pairs)


def y_first(value, y):
    return lax.ppermute(value, "row", [(k, y * 2 + k) for k in range(2)])


def core_swap(value):
    return lax.ppermute(value, "row", [(r, r ^ 1) for r in range(2 * NY)])


def together(*values):
    return lax.optimization_barrier(values)


def offset(n):
    return ((n + 1) // 2) * (1 - 2 * (n % 2))


def source(pos, i, j):
    return (pos[0] + offset(i) + NX) % NX, (pos[1] + offset(j) + NZ) % NZ


def pack_kernel(pos, two, one, own, give, held, sems):
    copies = [pltpu.make_async_copy(ref, held.at[n], sems.at[n]) for n, ref in enumerate((two, one))]
    for copy in copies:
        copy.start()
    first = pos[3] == 0
    for n, copy in enumerate(copies):
        copy.wait()
        for q in range(NY):
            at = slice(q * 128, q * 128 + 128)
            left = held[n, :, q * 256:q * 256 + 128]
            right = held[n, :, q * 256 + 128:q * 256 + 256]
            own[n, :, at] = jnp.where(first, left, right)
            give[n, :, at] = jnp.where(first, right, left)


def pack(pos, two, one):
    return pl.pallas_call(
        pack_kernel,
        out_shape=(jax.ShapeDtypeStruct((2, SUB, HALF), BF16),) * 2,
        in_specs=[SMEM, ANY, ANY],
        out_specs=(VMEM, VMEM),
        scratch_shapes=[pltpu.VMEM((2, SUB, 2 * HALF), BF16), pltpu.SemaphoreType.DMA((2,))],
        compiler_params=SMALL,
        name="pack_columns",
    )(pos, two, one)


def top_kernel(pos, own, taken, *outs):
    first = pos[3] == 0
    for y, out in enumerate(outs):
        at = slice(y * 128, y * 128 + 128)
        out[...] = jnp.where(first, own[1, :, at], taken[1, :, at])


def top(pos, own, taken):
    return pl.pallas_call(
        top_kernel,
        out_shape=(jax.ShapeDtypeStruct((SUB, 128), BF16),) * NY,
        in_specs=[SMEM, VMEM, VMEM],
        out_specs=(VMEM,) * NY,
        compiler_params=SMALL,
        name="diagonal_blocks",
    )(pos, own, taken)


def message_kernel(pos, two, down, up, far, one, own, b1, b2, b3, out, part):
    for n, ref in enumerate((two, down, up, far)):
        out[n * 8:n * 8 + 8] = ref[...].reshape(8, ROW, HALF)
    rows = one[...].reshape(8, ROW, HALF)
    out[TWO:TWO + 8] = rows
    part[0, :8] = rows
    sent = (b1[...] + b2[...]) + b3[...]
    columns = jnp.where(pos[2] == 0, own[...], sent)
    for q in range(NY):
        at = slice(q * 128, q * 128 + 128)
        out[TWO + 8, :, at] = columns[q * ROW:(q + 1) * ROW]
        part[0, 8, :, at] = columns[q * ROW:(q + 1) * ROW]


def message(pos, twos, one, blocks):
    return pl.pallas_call(
        message_kernel,
        out_shape=(
            jax.ShapeDtypeStruct((TWO + ONE, ROW, HALF), BF16),
            jax.ShapeDtypeStruct((1, ONE, ROW, HALF), BF16),
        ),
        in_specs=[SMEM] + [VMEM] * 9,
        out_specs=(VMEM, VMEM),
        compiler_params=SMALL,
        name="ring_message",
    )(pos, *twos, one, *blocks)


def join_kernel(*refs):
    for n, ref in enumerate(refs[:-1]):
        refs[-1][n] = ref[ref.shape[0] - ONE:]


def join(*messages):
    return pl.pallas_call(
        join_kernel,
        out_shape=jax.ShapeDtypeStruct((len(messages), ONE, ROW, HALF), BF16),
        in_specs=[VMEM] * len(messages),
        out_specs=VMEM,
        compiler_params=SMALL,
        name="join_parts",
    )(*messages)


def prepare_kernel(pos, taper, mine, other, for_two, for_one, rows):
    lane = lax.broadcasted_iota(jnp.int32, (SUB, 2 * BLK), 1)
    first_col = (pos[0] * NZ + pos[1]) * 2

    def put(at, i, j):
        x, z = source(pos, i, j)
        row = pl.multiple_of((x * NZ + z) * SUB, SUB)
        for h, ref in enumerate((mine, other)):
            core = pos[3] if h == 0 else 1 - pos[3]
            tile = (pos[2] * 2 + core) * 8 + x * 2 + z // 4
            left = taper[tile, first_col].astype(F32)
            right = taper[tile, first_col + 1].astype(F32)
            keep = jnp.where(lane < BLK, left, right)
            rows[at + h * SUB:at + h * SUB + SUB, :] = (
                ref[pl.ds(row, SUB), :].astype(F32) * keep).astype(BF16)

    def block_two(j, carry):
        for i in range(NX):
            put(i * PAIR, i, j)
        for_two[j] = rows[:512].T
        return carry

    def block_one(c, carry):
        for i in range(NX):
            for s in range(2):
                put((2 * i + s) * PAIR, i, jnp.where(c == 0, 7 * s, 2 * c - 1 + s))
        for_one[c] = rows[...].T
        return carry

    lax.fori_loop(0, NZ, block_two, 0)
    lax.fori_loop(0, NZ // 2, block_one, 0)


def prepare(pos, taper, mine, other):
    return pl.pallas_call(
        prepare_kernel,
        out_shape=(
            jax.ShapeDtypeStruct((NZ, 512, 512), BF16),
            jax.ShapeDtypeStruct((NZ // 2, 512, 1024), BF16),
        ),
        in_specs=[SMEM, SMEM, VMEM, VMEM],
        out_specs=(VMEM, VMEM),
        scratch_shapes=[pltpu.VMEM((1024, 512), BF16)],
        compiler_params=SMALL,
        name="prepare_adjoint",
    )(pos, taper, mine, other)


def product_kernel(count, items, first, last, pos, adjoint, *refs):
    panels, refs = refs[:count], list(refs[count:])
    before = None if first else refs.pop(0)
    outs = [refs.pop(0) for _ in range(NY)] if last else None
    total, held, sems = refs
    for n, (_, parts) in enumerate(items):
        to = 0
        for index, start, size in parts:
            panel = panels[index].at[pl.ds(start, size)]
            if len(held.shape) == 5:
                panel = panel.at[:, pl.ds(0, PAIR // ROW)]
            pltpu.make_async_copy(panel, held.at[n, pl.ds(to, size)], sems.at[n]).start()
            to += size
    if first:
        total[...] = jnp.zeros_like(total)
    else:
        total[...] = before[...]
    begin = items[0][0]

    def step(n, carry):
        pltpu.make_async_copy(held.at[n], held.at[n], sems.at[n]).wait()
        total[...] += jnp.dot(
            adjoint[begin + n], held[n].reshape(-1, HALF), preferred_element_type=F32)
        return carry

    lax.fori_loop(0, len(items), step, 0)
    if last:
        for d, out in enumerate(outs):
            column = pl.multiple_of((pos[2] + d) % NY * 128, 128)
            out[...] = (-2.0 * total[:, pl.ds(column, 128)]).astype(out.dtype)


def product(pos, adjoint, panels, items, before=None, kind=None):
    last = kind is not None
    shape = (TWO,) if panels[0].ndim == 3 else (2 * NX, PAIR // ROW)
    column = jax.ShapeDtypeStruct((512, 128), F32)
    scratch = [pltpu.VMEM((512, HALF), F32)] if last else []
    scratch += [
        pltpu.VMEM((len(items),) + shape + (ROW, HALF), BF16),
        pltpu.SemaphoreType.DMA((len(items),)),
    ]
    extra = [] if before is None else [before]
    kernel = functools.partial(product_kernel, len(panels), tuple(items), before is None, last)
    return pl.pallas_call(
        kernel,
        out_shape=(column,) + (jax.ShapeDtypeStruct((512, 128), kind),) * 3
        if last else jax.ShapeDtypeStruct((512, HALF), F32),
        in_specs=[SMEM, VMEM] + [ANY] * len(panels) + [VMEM] * len(extra),
        out_specs=(VMEM,) * 4 if last else VMEM,
        scratch_shapes=scratch,
        compiler_params=SMALL,
        name="masked_product",
    )(pos, adjoint, *panels, *extra)


def factor_kernel(where, pos, inverse, inverse_other, *refs):
    panels, (out, out_other, held, diagonal, sem) = refs[:-5], refs[-5:]
    for i in range(NX):
        x = source(pos, i, 0)[0]

        @pl.when(x < 2)
        def _(i=i, x=x):
            for j in range(NZ):
                index, at = where[i][j]
                z = source(pos, i, j)[1]
                pltpu.make_async_copy(panels[index].at[at, ONE - 1], held.at[x * NZ + z], sem.at[0]).start()

    pltpu.make_async_copy(held, held, sem.at[0]).wait()
    for q in range(NY):
        diagonal[:, q] = held[:, :, q * 128:(q + 1) * 128]
    columns = diagonal[...].reshape(2 * NZ * SUB, 128)
    for left, result in ((inverse, out), (inverse_other, out_other)):
        value = jnp.dot(left[...].reshape(512, 1024), columns, preferred_element_type=F32)
        high = value.astype(BF16)
        low = (value - high.astype(F32)).astype(BF16)
        result[:, :, :128] = high.reshape(NY, 128, 128)
        result[:, :, 128:] = low.reshape(NY, 128, 128)


def factor(pos, inverse, inverse_other, panels, where):
    return pl.pallas_call(
        functools.partial(factor_kernel, where),
        out_shape=(jax.ShapeDtypeStruct((NY, 128, 256), BF16),) * 2,
        in_specs=[SMEM, VMEM, VMEM] + [ANY] * len(panels),
        out_specs=(VMEM, VMEM),
        scratch_shapes=[
            pltpu.VMEM((2 * NZ, ROW, HALF), BF16),
            pltpu.VMEM((2 * NZ, NY, ROW, 128), BF16),
            pltpu.SemaphoreType.DMA((1,)),
        ],
        compiler_params=SMALL,
        name="inverse_times_diagonal",
    )(pos, inverse, inverse_other, *panels)


def carried_kernel(mine, other, factors, factors_other, out, total):
    total[...] = jnp.zeros_like(total)

    def block(d, carry):
        left = jnp.concatenate([mine[d], other[d]], axis=1)
        right = jnp.concatenate([factors[d], factors_other[d]], axis=0)
        total[...] += jnp.dot(left, right, preferred_element_type=F32)
        return carry

    lax.fori_loop(0, NY, block, 0)
    out[...] = total[:, :128] + total[:, 128:]


def carried(mine, other, factors, factors_other):
    return pl.pallas_call(
        carried_kernel,
        out_shape=jax.ShapeDtypeStruct((512, 128), F32),
        in_specs=[VMEM] * 4,
        out_specs=VMEM,
        scratch_shapes=[pltpu.VMEM((512, 256), F32)],
        compiler_params=SMALL,
        name="carried_term",
    )(mine, other, factors, factors_other)


def local(adjoint, taper, panel_two, panel_one, incoming, inverse_factor):
    row, col = lax.axis_index("row"), lax.axis_index("col")
    pos = jnp.stack([col // NZ, col % NZ, row // 2, row % 2]).astype(jnp.int32)

    own, give = pack(pos, panel_two, panel_one)
    taken = core_swap(give)
    shards = jnp.concatenate([own, taken], axis=1)
    block, *blocks = top(pos, own, taken)
    two, one = shards[0], shards[1]

    def x_all(part):
        return [part] + [x_shift(part, d) for d in (1, -1, 2)]

    two, one, swapped = together(two, one, core_swap(adjoint))
    *two, inverse1, inverse3 = together(
        *x_all(two), y_shift(inverse_factor, 1), y_shift(inverse_factor, 3))
    blocks = [y_first(part, d + 1) for d, part in enumerate(blocks)]
    own, part = message(pos, two, one, [block] + blocks)
    own, part, later = together(own, part, inverse_factor)
    inverse = jnp.stack([inverse_factor, inverse1, y_shift(later, 2), inverse3])
    down1, up1, inverse, *first_x = together(
        z_shift(own, 1), z_shift(own, -1), inverse, *x_all(part))

    for_two, for_one = prepare(pos, taper, adjoint, swapped)
    down2, up2, for_two, for_one, *near = together(
        z_shift(down1, 1), z_shift(up1, -1), for_two, for_one, *x_all(join(down1, up1)))
    inverse, down2, up2 = together(inverse, down2, up2)
    inverse_other = core_swap(inverse)
    sums = product(
        pos, for_two, [own, down1, up1, down2, up2], [(j, [(j, 0, TWO)]) for j in range(5)])
    down3, up3, sums, *middle = together(
        z_shift(down2, 1), z_shift(up2, -1), sums, *x_all(join(down2, up2)))
    sums = product(pos, for_two, [down3, up3], [(5 + j, [(j, 0, TWO)]) for j in range(2)], sums)
    sums_one = product(
        pos, for_one, near + middle,
        [(1 + c, [(NX * c + i, 0, 2) for i in range(NX)]) for c in range(2)])
    third = join(down3, up3)
    third = [third, x_shift(third, 1), x_shift(third, -1)]
    far_low, far_high, sums, sums_one, *third = together(
        z_shift(down3[:TWO // 2], 1), z_shift(up3[TWO // 2:], -1), sums, sums_one, *third)

    mine, *sent = product(
        pos, for_two, [far_low, far_high], [(7, [(0, 0, TWO // 2), (1, 0, TWO // 2)])], sums, F32)
    last = far_high[None, TWO // 2:]
    last = [last, x_shift(last, 1), x_shift(last, -1)]
    third.append(x_shift(join(down3, up3, far_high), 2))
    r1, r2, r3 = together(*[y_shift(part, d + 1) for d, part in enumerate(sent)])
    second_grad = incoming + ((mine + r1) + (r2 + r3))
    rounded = second_grad.astype(BF16)

    sums_one = product(pos, for_one, third, [(3, [(i, 0, 2) for i in range(NX)])], sums_one)
    parts = []
    for i in range(NX):
        parts += [(i, 0, 1), (NX + 1 + i, 0, 1) if i < 3 else (NX, 2, 1)]
    sums_one = product(pos, for_one, first_x + third[3:] + last, [(0, parts)], sums_one, BF16)
    where = tuple(
        ((i, 0),) + tuple((NX * (1 + j // 2) + i, j % 2) for j in range(6))
        + ((4 * NX + i, 0) if i < 3 else (4 * NX - 1, 2),)
        for i in range(NX))
    factors = factor(pos, inverse, inverse_other, first_x + near + middle + third + last, where)
    s1, s2, s3, mine, *sent = together(*[y_shift(rounded, d) for d in range(1, NY)], *sums_one)
    rounded = jnp.stack([rounded, s1, s2, s3])
    rounded_other = core_swap(rounded)
    r1, r2, r3 = [y_shift(part, d + 1).astype(F32) for d, part in enumerate(sent)]
    term = carried(rounded, rounded_other, *factors)
    return second_grad, (mine + r1) + (r2 + r3) - term


def solution(mesh):
    in_specs = (
        P("row", "col"),
        P(),
        P(("row", "col"), None),
        P(("row", "col"), None),
        P("col", "row"),
        P("row", None),
    )
    out_specs = (P("col", "row"), P("col", "row"))
    return jax.shard_map(local, mesh=mesh, in_specs=in_specs, out_specs=out_specs, check_vma=False)
```

```python
import functools

import jax
import jax.numpy as jnp
from jax import lax
from jax.experimental import pallas as pl
from jax.experimental.pallas import tpu as pltpu
from jax.sharding import PartitionSpec as P

BLK = 256
NX, NZ, NY = 4, 8, 4
SUB = 64
PAIR = 2 * SUB
HALF = 512
ROW = 16
ONE = PAIR // ROW + 1
TWO = NX * PAIR // ROW
F32, BF16 = jnp.float32, jnp.bfloat16
VMEM = pl.BlockSpec(memory_space=pltpu.VMEM)
SMEM = pl.BlockSpec(memory_space=pltpu.SMEM)
ANY = pl.BlockSpec(memory_space=pl.ANY)
BIG = pltpu.CompilerParams(vmem_limit_bytes=24 * 2**20)
SMALL = pltpu.CompilerParams(vmem_limit_bytes=16 * 2**20)


def x_shift(value, dx):
    pairs = [(x * NZ + z, (x + dx) % NX * NZ + z) for x in range(NX) for z in range(NZ)]
    return lax.ppermute(value, "col", pairs)


def z_shift(value, dz):
    pairs = [(x * NZ + z, x * NZ + (z + dz) % NZ) for x in range(NX) for z in range(NZ)]
    return lax.ppermute(value, "col", pairs)


def y_shift(value, dy):
    pairs = [(y * 2 + k, (y + dy) % NY * 2 + k) for y in range(NY) for k in range(2)]
    return lax.ppermute(value, "row", pairs)


def y_first(value, y):
    return lax.ppermute(value, "row", [(k, y * 2 + k) for k in range(2)])


def core_swap(value):
    return lax.ppermute(value, "row", [(r, r ^ 1) for r in range(2 * NY)])


def together(*values):
    return lax.optimization_barrier(values)


def offset(n):
    return ((n + 1) // 2) * (1 - 2 * (n % 2))


def source(pos, i, j):
    return (pos[0] + offset(i) + NX) % NX, (pos[1] + offset(j) + NZ) % NZ


def pack_kernel(pos, two, one, own, give, held, sems):
    copies = [pltpu.make_async_copy(ref, held.at[n], sems.at[n]) for n, ref in enumerate((two, one))]
    for copy in copies:
        copy.start()
    first = pos[3] == 0
    for n, copy in enumerate(copies):
        copy.wait()
        for q in range(NY):
            at = slice(q * 128, q * 128 + 128)
            left = held[n, :, q * 256:q * 256 + 128]
            right = held[n, :, q * 256 + 128:q * 256 + 256]
            own[n, :, at] = jnp.where(first, left, right)
            give[n, :, at] = jnp.where(first, right, left)


def pack(pos, two, one):
    return pl.pallas_call(
        pack_kernel,
        out_shape=(jax.ShapeDtypeStruct((2, SUB, HALF), BF16),) * 2,
        in_specs=[SMEM, ANY, ANY],
        out_specs=(VMEM, VMEM),
        scratch_shapes=[pltpu.VMEM((2, SUB, 2 * HALF), BF16), pltpu.SemaphoreType.DMA((2,))],
        compiler_params=SMALL,
        name="pack_columns",
    )(pos, two, one)


def top_kernel(pos, own, taken, *outs):
    first = pos[3] == 0
    for y, out in enumerate(outs):
        at = slice(y * 128, y * 128 + 128)
        out[...] = jnp.where(first, own[1, :, at], taken[1, :, at])


def top(pos, own, taken):
    return pl.pallas_call(
        top_kernel,
        out_shape=(jax.ShapeDtypeStruct((SUB, 128), BF16),) * NY,
        in_specs=[SMEM, VMEM, VMEM],
        out_specs=(VMEM,) * NY,
        compiler_params=SMALL,
        name="diagonal_blocks",
    )(pos, own, taken)


def message_kernel(pos, two, down, up, far, one, own, b1, b2, b3, out, part):
    for n, ref in enumerate((two, down, up, far)):
        out[n * 8:n * 8 + 8] = ref[...].reshape(8, ROW, HALF)
    rows = one[...].reshape(8, ROW, HALF)
    out[TWO:TWO + 8] = rows
    part[0, :8] = rows
    sent = (b1[...] + b2[...]) + b3[...]
    columns = jnp.where(pos[2] == 0, own[...], sent)
    for q in range(NY):
        at = slice(q * 128, q * 128 + 128)
        out[TWO + 8, :, at] = columns[q * ROW:(q + 1) * ROW]
        part[0, 8, :, at] = columns[q * ROW:(q + 1) * ROW]


def message(pos, twos, one, blocks):
    return pl.pallas_call(
        message_kernel,
        out_shape=(
            jax.ShapeDtypeStruct((TWO + ONE, ROW, HALF), BF16),
            jax.ShapeDtypeStruct((1, ONE, ROW, HALF), BF16),
        ),
        in_specs=[SMEM] + [VMEM] * 9,
        out_specs=(VMEM, VMEM),
        compiler_params=SMALL,
        name="ring_message",
    )(pos, *twos, one, *blocks)


def join_kernel(*refs):
    for n, ref in enumerate(refs[:-1]):
        refs[-1][n] = ref[ref.shape[0] - ONE:]


def join(*messages):
    return pl.pallas_call(
        join_kernel,
        out_shape=jax.ShapeDtypeStruct((len(messages), ONE, ROW, HALF), BF16),
        in_specs=[VMEM] * len(messages),
        out_specs=VMEM,
        compiler_params=SMALL,
        name="join_parts",
    )(*messages)


def prepare_kernel(pos, taper, mine, other, for_two, for_one, rows):
    lane = lax.broadcasted_iota(jnp.int32, (SUB, 2 * BLK), 1)
    first_col = (pos[0] * NZ + pos[1]) * 2

    def put(at, i, j):
        x, z = source(pos, i, j)
        row = pl.multiple_of((x * NZ + z) * SUB, SUB)
        for h, ref in enumerate((mine, other)):
            core = pos[3] if h == 0 else 1 - pos[3]
            tile = (pos[2] * 2 + core) * 8 + x * 2 + z // 4
            left = taper[tile, first_col].astype(F32)
            right = taper[tile, first_col + 1].astype(F32)
            keep = jnp.where(lane < BLK, left, right)
            rows[at + h * SUB:at + h * SUB + SUB, :] = (
                ref[pl.ds(row, SUB), :].astype(F32) * keep).astype(BF16)

    def block_two(j, carry):
        for i in range(NX):
            put(i * PAIR, i, j)
        for_two[j] = rows[:512].T
        return carry

    def block_one(c, carry):
        for i in range(NX):
            for s in range(2):
                put((2 * i + s) * PAIR, i, jnp.where(c == 0, 7 * s, 2 * c - 1 + s))
        for_one[c] = rows[...].T
        return carry

    lax.fori_loop(0, NZ, block_two, 0)
    lax.fori_loop(0, NZ // 2, block_one, 0)


def prepare(pos, taper, mine, other):
    return pl.pallas_call(
        prepare_kernel,
        out_shape=(
            jax.ShapeDtypeStruct((NZ, 512, 512), BF16),
            jax.ShapeDtypeStruct((NZ // 2, 512, 1024), BF16),
        ),
        in_specs=[SMEM, SMEM, VMEM, VMEM],
        out_specs=(VMEM, VMEM),
        scratch_shapes=[pltpu.VMEM((1024, 512), BF16)],
        compiler_params=SMALL,
        name="prepare_adjoint",
    )(pos, taper, mine, other)


def product_kernel(count, items, first, last, pos, adjoint, *refs):
    panels, refs = refs[:count], list(refs[count:])
    before = None if first else refs.pop(0)
    outs = [refs.pop(0) for _ in range(NY)] if last else None
    total, held, sems = refs
    for n, (_, parts) in enumerate(items):
        to = 0
        for index, start, size in parts:
            panel = panels[index].at[pl.ds(start, size)]
            if len(held.shape) == 5:
                panel = panel.at[:, pl.ds(0, PAIR // ROW)]
            pltpu.make_async_copy(panel, held.at[n, pl.ds(to, size)], sems.at[n]).start()
            to += size
    if first:
        total[...] = jnp.zeros_like(total)
    else:
        total[...] = before[...]
    begin = items[0][0]

    def step(n, carry):
        pltpu.make_async_copy(held.at[n], held.at[n], sems.at[n]).wait()
        total[...] += jnp.dot(
            adjoint[begin + n], held[n].reshape(-1, HALF), preferred_element_type=F32)
        return carry

    lax.fori_loop(0, len(items), step, 0)
    if last:
        for d, out in enumerate(outs):
            column = pl.multiple_of((pos[2] + d) % NY * 128, 128)
            out[...] = (-2.0 * total[:, pl.ds(column, 128)]).astype(out.dtype)


def product(pos, adjoint, panels, items, before=None, kind=None):
    last = kind is not None
    shape = (TWO,) if panels[0].ndim == 3 else (2 * NX, PAIR // ROW)
    column = jax.ShapeDtypeStruct((512, 128), F32)
    scratch = [pltpu.VMEM((512, HALF), F32)] if last else []
    scratch += [
        pltpu.VMEM((len(items),) + shape + (ROW, HALF), BF16),
        pltpu.SemaphoreType.DMA((len(items),)),
    ]
    extra = [] if before is None else [before]
    kernel = functools.partial(product_kernel, len(panels), tuple(items), before is None, last)
    return pl.pallas_call(
        kernel,
        out_shape=(column,) + (jax.ShapeDtypeStruct((512, 128), kind),) * 3
        if last else jax.ShapeDtypeStruct((512, HALF), F32),
        in_specs=[SMEM, VMEM] + [ANY] * len(panels) + [VMEM] * len(extra),
        out_specs=(VMEM,) * 4 if last else VMEM,
        scratch_shapes=scratch,
        compiler_params=SMALL,
        name="masked_product",
    )(pos, adjoint, *panels, *extra)


def factor_kernel(where, pos, inverse, inverse_other, *refs):
    panels, (out, out_other, held, diagonal, sem) = refs[:-5], refs[-5:]
    for i in range(NX):
        x = source(pos, i, 0)[0]

        @pl.when(x < 2)
        def _(i=i, x=x):
            for j in range(NZ):
                index, at = where[i][j]
                z = source(pos, i, j)[1]
                pltpu.make_async_copy(panels[index].at[at, ONE - 1], held.at[x * NZ + z], sem.at[0]).start()

    pltpu.make_async_copy(held, held, sem.at[0]).wait()
    for q in range(NY):
        diagonal[:, q] = held[:, :, q * 128:(q + 1) * 128]
    columns = diagonal[...].reshape(2 * NZ * SUB, 128)
    for left, result in ((inverse, out), (inverse_other, out_other)):
        value = jnp.dot(left[...].reshape(512, 1024), columns, preferred_element_type=F32)
        high = value.astype(BF16)
        low = (value - high.astype(F32)).astype(BF16)
        result[:, :, :128] = high.reshape(NY, 128, 128)
        result[:, :, 128:] = low.reshape(NY, 128, 128)


def factor(pos, inverse, inverse_other, panels, where):
    return pl.pallas_call(
        functools.partial(factor_kernel, where),
        out_shape=(jax.ShapeDtypeStruct((NY, 128, 256), BF16),) * 2,
        in_specs=[SMEM, VMEM, VMEM] + [ANY] * len(panels),
        out_specs=(VMEM, VMEM),
        scratch_shapes=[
            pltpu.VMEM((2 * NZ, ROW, HALF), BF16),
            pltpu.VMEM((2 * NZ, NY, ROW, 128), BF16),
            pltpu.SemaphoreType.DMA((1,)),
        ],
        compiler_params=SMALL,
        name="inverse_times_diagonal",
    )(pos, inverse, inverse_other, *panels)


def carried_kernel(mine, other, factors, factors_other, out, total):
    total[...] = jnp.zeros_like(total)

    def block(d, carry):
        left = jnp.concatenate([mine[d], other[d]], axis=1)
        right = jnp.concatenate([factors[d], factors_other[d]], axis=0)
        total[...] += jnp.dot(left, right, preferred_element_type=F32)
        return carry

    lax.fori_loop(0, NY, block, 0)
    out[...] = total[:, :128] + total[:, 128:]


def carried(mine, other, factors, factors_other):
    return pl.pallas_call(
        carried_kernel,
        out_shape=jax.ShapeDtypeStruct((512, 128), F32),
        in_specs=[VMEM] * 4,
        out_specs=VMEM,
        scratch_shapes=[pltpu.VMEM((512, 256), F32)],
        compiler_params=SMALL,
        name="carried_term",
    )(mine, other, factors, factors_other)


def local(adjoint, taper, panel_two, panel_one, incoming, inverse_factor):
    row, col = lax.axis_index("row"), lax.axis_index("col")
    pos = jnp.stack([col // NZ, col % NZ, row // 2, row % 2]).astype(jnp.int32)

    own, give = pack(pos, panel_two, panel_one)
    taken = core_swap(give)
    shards = jnp.concatenate([own, taken], axis=1)
    block, *blocks = top(pos, own, taken)
    two, one = shards[0], shards[1]

    def x_all(part):
        return [part] + [x_shift(part, d) for d in (1, -1, 2)]

    two, one, swapped = together(two, one, core_swap(adjoint))
    *two, inverse1, inverse3 = together(
        *x_all(two), y_shift(inverse_factor, 1), y_shift(inverse_factor, 3))
    blocks = [y_first(part, d + 1) for d, part in enumerate(blocks)]
    own, part = message(pos, two, one, [block] + blocks)
    own, part, later = together(own, part, inverse_factor)
    inverse = jnp.stack([inverse_factor, inverse1, y_shift(later, 2), inverse3])
    down1, up1, inverse, *first_x = together(
        z_shift(own, 1), z_shift(own, -1), inverse, *x_all(part))

    for_two, for_one = prepare(pos, taper, adjoint, swapped)
    down2, up2, for_two, for_one, *near = together(
        z_shift(down1, 1), z_shift(up1, -1), for_two, for_one, *x_all(join(down1, up1)))
    inverse, down2, up2 = together(inverse, down2, up2)
    inverse_other = core_swap(inverse)
    sums = product(
        pos, for_two, [own, down1, up1, down2, up2], [(j, [(j, 0, TWO)]) for j in range(5)])
    down3, up3, sums, *middle = together(
        z_shift(down2, 1), z_shift(up2, -1), sums, *x_all(join(down2, up2)))
    sums = product(pos, for_two, [down3, up3], [(5 + j, [(j, 0, TWO)]) for j in range(2)], sums)
    sums_one = product(
        pos, for_one, near + middle,
        [(1 + c, [(NX * c + i, 0, 2) for i in range(NX)]) for c in range(2)])
    third = join(down3, up3)
    third = [third, x_shift(third, 1), x_shift(third, -1)]
    far_low, far_high, sums, sums_one, *third = together(
        z_shift(down3[:TWO // 2], 1), z_shift(up3[TWO // 2:], -1), sums, sums_one, *third)

    mine, *sent = product(
        pos, for_two, [far_low, far_high], [(7, [(0, 0, TWO // 2), (1, 0, TWO // 2)])], sums, F32)
    last = far_high[None, TWO // 2:]
    last = [last, x_shift(last, 1), x_shift(last, -1)]
    r1, r2, r3 = [y_shift(part, d + 1) for d, part in enumerate(sent)]
    r1, *last, distant = together(r1, *last, join(down3, up3, far_high))
    third.append(x_shift(distant, 2))
    r1, r2, r3, inverse_other = together(r1, r2, r3, inverse_other)
    second_grad = incoming + ((mine + r1) + (r2 + r3))
    rounded = second_grad.astype(BF16)

    sums_one = product(pos, for_one, third, [(3, [(i, 0, 2) for i in range(NX)])], sums_one)
    parts = []
    for i in range(NX):
        parts += [(i, 0, 1), (NX + 1 + i, 0, 1) if i < 3 else (NX, 2, 1)]
    sums_one = product(pos, for_one, first_x + third[3:] + last, [(0, parts)], sums_one, BF16)
    where = tuple(
        ((i, 0),) + tuple((NX * (1 + j // 2) + i, j % 2) for j in range(6))
        + ((4 * NX + i, 0) if i < 3 else (4 * NX - 1, 2),)
        for i in range(NX))
    factors = factor(pos, inverse, inverse_other, first_x + near + middle + third + last, where)
    s1, s2, s3, mine, *sent = together(*[y_shift(rounded, d) for d in range(1, NY)], *sums_one)
    rounded = jnp.stack([rounded, s1, s2, s3])
    rounded_other = core_swap(rounded)
    r1, r2, r3 = [y_shift(part, d + 1).astype(F32) for d, part in enumerate(sent)]
    term = carried(rounded, rounded_other, *factors)
    return second_grad, (mine + r1) + (r2 + r3) - term


def solution(mesh):
    in_specs = (
        P("row", "col"),
        P(),
        P(("row", "col"), None),
        P(("row", "col"), None),
        P("col", "row"),
        P("row", None),
    )
    out_specs = (P("col", "row"), P("col", "row"))
    return jax.shard_map(local, mesh=mesh, in_specs=in_specs, out_specs=out_specs, check_vma=False)
```

```python
import functools

import jax
import jax.numpy as jnp
from jax import lax
from jax.experimental import pallas as pl
from jax.experimental.pallas import tpu as pltpu
from jax.sharding import PartitionSpec as P

BLK = 256
NX, NZ, NY = 4, 8, 4
SUB = 64
PAIR = 2 * SUB
HALF = 512
ROW = 16
ONE = PAIR // ROW + 1
TWO = NX * PAIR // ROW
F32, BF16 = jnp.float32, jnp.bfloat16
VMEM = pl.BlockSpec(memory_space=pltpu.VMEM)
SMEM = pl.BlockSpec(memory_space=pltpu.SMEM)
ANY = pl.BlockSpec(memory_space=pl.ANY)
BIG = pltpu.CompilerParams(vmem_limit_bytes=24 * 2**20)
SMALL = pltpu.CompilerParams(vmem_limit_bytes=16 * 2**20)


def x_shift(value, dx):
    pairs = [(x * NZ + z, (x + dx) % NX * NZ + z) for x in range(NX) for z in range(NZ)]
    return lax.ppermute(value, "col", pairs)


def z_shift(value, dz):
    pairs = [(x * NZ + z, x * NZ + (z + dz) % NZ) for x in range(NX) for z in range(NZ)]
    return lax.ppermute(value, "col", pairs)


def y_shift(value, dy):
    pairs = [(y * 2 + k, (y + dy) % NY * 2 + k) for y in range(NY) for k in range(2)]
    return lax.ppermute(value, "row", pairs)


def y_first(value, y):
    return lax.ppermute(value, "row", [(k, y * 2 + k) for k in range(2)])


def core_swap(value):
    return lax.ppermute(value, "row", [(r, r ^ 1) for r in range(2 * NY)])


def together(*values):
    return lax.optimization_barrier(values)


def offset(n):
    return ((n + 1) // 2) * (1 - 2 * (n % 2))


def source(pos, i, j):
    return (pos[0] + offset(i) + NX) % NX, (pos[1] + offset(j) + NZ) % NZ


def pack_kernel(pos, two, one, own, give, held, sems):
    copies = [pltpu.make_async_copy(ref, held.at[n], sems.at[n]) for n, ref in enumerate((two, one))]
    for copy in copies:
        copy.start()
    first = pos[3] == 0
    for n, copy in enumerate(copies):
        copy.wait()
        for q in range(NY):
            at = slice(q * 128, q * 128 + 128)
            left = held[n, :, q * 256:q * 256 + 128]
            right = held[n, :, q * 256 + 128:q * 256 + 256]
            own[n, :, at] = jnp.where(first, left, right)
            give[n, :, at] = jnp.where(first, right, left)


def pack(pos, two, one):
    return pl.pallas_call(
        pack_kernel,
        out_shape=(jax.ShapeDtypeStruct((2, SUB, HALF), BF16),) * 2,
        in_specs=[SMEM, ANY, ANY],
        out_specs=(VMEM, VMEM),
        scratch_shapes=[pltpu.VMEM((2, SUB, 2 * HALF), BF16), pltpu.SemaphoreType.DMA((2,))],
        compiler_params=SMALL,
        name="pack_columns",
    )(pos, two, one)


def top_kernel(pos, own, taken, *outs):
    first = pos[3] == 0
    for y, out in enumerate(outs):
        at = slice(y * 128, y * 128 + 128)
        out[...] = jnp.where(first, own[1, :, at], taken[1, :, at])


def top(pos, own, taken):
    return pl.pallas_call(
        top_kernel,
        out_shape=(jax.ShapeDtypeStruct((SUB, 128), BF16),) * NY,
        in_specs=[SMEM, VMEM, VMEM],
        out_specs=(VMEM,) * NY,
        compiler_params=SMALL,
        name="diagonal_blocks",
    )(pos, own, taken)


def message_kernel(pos, two, down, up, far, one, own, b1, b2, b3, out, part):
    for n, ref in enumerate((two, down, up, far)):
        out[n * 8:n * 8 + 8] = ref[...].reshape(8, ROW, HALF)
    rows = one[...].reshape(8, ROW, HALF)
    out[TWO:TWO + 8] = rows
    part[0, :8] = rows
    sent = (b1[...] + b2[...]) + b3[...]
    columns = jnp.where(pos[2] == 0, own[...], sent)
    for q in range(NY):
        at = slice(q * 128, q * 128 + 128)
        out[TWO + 8, :, at] = columns[q * ROW:(q + 1) * ROW]
        part[0, 8, :, at] = columns[q * ROW:(q + 1) * ROW]


def message(pos, twos, one, blocks):
    return pl.pallas_call(
        message_kernel,
        out_shape=(
            jax.ShapeDtypeStruct((TWO + ONE, ROW, HALF), BF16),
            jax.ShapeDtypeStruct((1, ONE, ROW, HALF), BF16),
        ),
        in_specs=[SMEM] + [VMEM] * 9,
        out_specs=(VMEM, VMEM),
        compiler_params=SMALL,
        name="ring_message",
    )(pos, *twos, one, *blocks)


def join_kernel(*refs):
    for n, ref in enumerate(refs[:-1]):
        refs[-1][n] = ref[TWO:]


def join(*messages):
    return pl.pallas_call(
        join_kernel,
        out_shape=jax.ShapeDtypeStruct((len(messages), ONE, ROW, HALF), BF16),
        in_specs=[VMEM] * len(messages),
        out_specs=VMEM,
        compiler_params=SMALL,
        name="join_parts",
    )(*messages)


def prepare_kernel(pos, taper, mine, other, for_two, for_one, rows):
    lane = lax.broadcasted_iota(jnp.int32, (SUB, 2 * BLK), 1)
    first_col = (pos[0] * NZ + pos[1]) * 2

    def put(at, i, j):
        x, z = source(pos, i, j)
        row = pl.multiple_of((x * NZ + z) * SUB, SUB)
        for h, ref in enumerate((mine, other)):
            core = pos[3] if h == 0 else 1 - pos[3]
            tile = (pos[2] * 2 + core) * 8 + x * 2 + z // 4
            left = taper[tile, first_col].astype(F32)
            right = taper[tile, first_col + 1].astype(F32)
            keep = jnp.where(lane < BLK, left, right)
            rows[at + h * SUB:at + h * SUB + SUB, :] = (
                ref[pl.ds(row, SUB), :].astype(F32) * keep).astype(BF16)

    def block_two(j, carry):
        for i in range(NX):
            put(i * PAIR, i, j)
        for_two[j] = rows[:512].T
        return carry

    def block_one(c, carry):
        for i in range(NX):
            for s in range(2):
                put((2 * i + s) * PAIR, i, jnp.where(c == 0, 7 * s, 2 * c - 1 + s))
        for_one[c] = rows[...].T
        return carry

    lax.fori_loop(0, NZ, block_two, 0)
    lax.fori_loop(0, NZ // 2, block_one, 0)


def prepare(pos, taper, mine, other):
    return pl.pallas_call(
        prepare_kernel,
        out_shape=(
            jax.ShapeDtypeStruct((NZ, 512, 512), BF16),
            jax.ShapeDtypeStruct((NZ // 2, 512, 1024), BF16),
        ),
        in_specs=[SMEM, SMEM, VMEM, VMEM],
        out_specs=(VMEM, VMEM),
        scratch_shapes=[pltpu.VMEM((1024, 512), BF16)],
        compiler_params=SMALL,
        name="prepare_adjoint",
    )(pos, taper, mine, other)


def product_kernel(count, items, first, last, pos, adjoint, *refs):
    panels, refs = refs[:count], list(refs[count:])
    before = None if first else refs.pop(0)
    outs = [refs.pop(0) for _ in range(NY)] if last else None
    total, held, sems = refs
    for n, (_, parts) in enumerate(items):
        to = 0
        for index, start, size in parts:
            panel = panels[index].at[pl.ds(start, size)]
            if len(held.shape) == 5:
                panel = panel.at[:, pl.ds(0, PAIR // ROW)]
            pltpu.make_async_copy(panel, held.at[n, pl.ds(to, size)], sems.at[n]).start()
            to += size
    if first:
        total[...] = jnp.zeros_like(total)
    else:
        total[...] = before[...]
    begin = items[0][0]

    def step(n, carry):
        pltpu.make_async_copy(held.at[n], held.at[n], sems.at[n]).wait()
        total[...] += jnp.dot(
            adjoint[begin + n], held[n].reshape(-1, HALF), preferred_element_type=F32)
        return carry

    lax.fori_loop(0, len(items), step, 0)
    if last:
        for d, out in enumerate(outs):
            column = pl.multiple_of((pos[2] + d) % NY * 128, 128)
            out[...] = (-2.0 * total[:, pl.ds(column, 128)]).astype(out.dtype)


def product(pos, adjoint, panels, items, before=None, kind=None):
    last = kind is not None
    shape = (TWO,) if panels[0].ndim == 3 else (2 * NX, PAIR // ROW)
    column = jax.ShapeDtypeStruct((512, 128), F32)
    scratch = [pltpu.VMEM((512, HALF), F32)] if last else []
    scratch += [
        pltpu.VMEM((len(items),) + shape + (ROW, HALF), BF16),
        pltpu.SemaphoreType.DMA((len(items),)),
    ]
    extra = [] if before is None else [before]
    kernel = functools.partial(product_kernel, len(panels), tuple(items), before is None, last)
    return pl.pallas_call(
        kernel,
        out_shape=(column,) + (jax.ShapeDtypeStruct((512, 128), kind),) * 3
        if last else jax.ShapeDtypeStruct((512, HALF), F32),
        in_specs=[SMEM, VMEM] + [ANY] * len(panels) + [VMEM] * len(extra),
        out_specs=(VMEM,) * 4 if last else VMEM,
        scratch_shapes=scratch,
        compiler_params=SMALL,
        name="masked_product",
    )(pos, adjoint, *panels, *extra)


def factor_kernel(where, pos, inverse, inverse_other, *refs):
    panels, (out, out_other, held, diagonal, sem) = refs[:-5], refs[-5:]
    for i in range(NX):
        x = source(pos, i, 0)[0]

        @pl.when(x < 2)
        def _(i=i, x=x):
            for j in range(NZ):
                index, at = where[i][j]
                z = source(pos, i, j)[1]
                pltpu.make_async_copy(panels[index].at[at, ONE - 1], held.at[x * NZ + z], sem.at[0]).start()

    pltpu.make_async_copy(held, held, sem.at[0]).wait()
    for q in range(NY):
        diagonal[:, q] = held[:, :, q * 128:(q + 1) * 128]
    columns = diagonal[...].reshape(2 * NZ * SUB, 128)
    for left, result in ((inverse, out), (inverse_other, out_other)):
        value = jnp.dot(left[...].reshape(512, 1024), columns, preferred_element_type=F32)
        high = value.astype(BF16)
        low = (value - high.astype(F32)).astype(BF16)
        result[:, :, :128] = high.reshape(NY, 128, 128)
        result[:, :, 128:] = low.reshape(NY, 128, 128)


def factor(pos, inverse, inverse_other, panels, where):
    return pl.pallas_call(
        functools.partial(factor_kernel, where),
        out_shape=(jax.ShapeDtypeStruct((NY, 128, 256), BF16),) * 2,
        in_specs=[SMEM, VMEM, VMEM] + [ANY] * len(panels),
        out_specs=(VMEM, VMEM),
        scratch_shapes=[
            pltpu.VMEM((2 * NZ, ROW, HALF), BF16),
            pltpu.VMEM((2 * NZ, NY, ROW, 128), BF16),
            pltpu.SemaphoreType.DMA((1,)),
        ],
        compiler_params=SMALL,
        name="inverse_times_diagonal",
    )(pos, inverse, inverse_other, *panels)


def carried_kernel(mine, other, factors, factors_other, out, total):
    total[...] = jnp.zeros_like(total)

    def block(d, carry):
        left = jnp.concatenate([mine[d], other[d]], axis=1)
        right = jnp.concatenate([factors[d], factors_other[d]], axis=0)
        total[...] += jnp.dot(left, right, preferred_element_type=F32)
        return carry

    lax.fori_loop(0, NY, block, 0)
    out[...] = total[:, :128] + total[:, 128:]


def carried(mine, other, factors, factors_other):
    return pl.pallas_call(
        carried_kernel,
        out_shape=jax.ShapeDtypeStruct((512, 128), F32),
        in_specs=[VMEM] * 4,
        out_specs=VMEM,
        scratch_shapes=[pltpu.VMEM((512, 256), F32)],
        compiler_params=SMALL,
        name="carried_term",
    )(mine, other, factors, factors_other)


def local(adjoint, taper, panel_two, panel_one, incoming, inverse_factor):
    row, col = lax.axis_index("row"), lax.axis_index("col")
    pos = jnp.stack([col // NZ, col % NZ, row // 2, row % 2]).astype(jnp.int32)

    own, give = pack(pos, panel_two, panel_one)
    taken = core_swap(give)
    shards = jnp.concatenate([own, taken], axis=1)
    block, *blocks = top(pos, own, taken)
    two, one = shards[0], shards[1]

    def x_all(part):
        return [part] + [x_shift(part, d) for d in (1, -1, 2)]

    two, one, swapped = together(two, one, core_swap(adjoint))
    *two, inverse1, inverse3 = together(
        *x_all(two), y_shift(inverse_factor, 1), y_shift(inverse_factor, 3))
    blocks = [y_first(part, d + 1) for d, part in enumerate(blocks)]
    own, part = message(pos, two, one, [block] + blocks)
    own, part, later = together(own, part, inverse_factor)
    inverse = jnp.stack([inverse_factor, inverse1, y_shift(later, 2), inverse3])
    down1, up1, inverse, *first_x = together(
        z_shift(own, 1), z_shift(own, -1), inverse, *x_all(part))

    for_two, for_one = prepare(pos, taper, adjoint, swapped)
    down2, up2, for_two, for_one, *near = together(
        z_shift(down1, 1), z_shift(up1, -1), for_two, for_one, *x_all(join(down1, up1)))
    inverse, down2, up2 = together(inverse, down2, up2)
    inverse_other = core_swap(inverse)
    sums = product(
        pos, for_two, [own, down1, up1, down2, up2], [(j, [(j, 0, TWO)]) for j in range(5)])
    down3, up3, sums, *middle = together(
        z_shift(down2, 1), z_shift(up2, -1), sums, *x_all(join(down2, up2)))
    sums = product(pos, for_two, [down3, up3], [(5 + j, [(j, 0, TWO)]) for j in range(2)], sums)
    sums_one = product(
        pos, for_one, near + middle,
        [(1 + c, [(NX * c + i, 0, 2) for i in range(NX)]) for c in range(2)])
    third = x_all(join(down3, up3))
    far_low, far_high, sums, sums_one = together(
        z_shift(down3[:TWO // 2], 1), z_shift(up3[TWO // 2:], -1), sums, sums_one)

    mine, *sent = product(
        pos, for_two, [far_low, far_high], [(7, [(0, 0, TWO // 2), (1, 0, TWO // 2)])], sums, F32)
    last = x_all(far_high[None, TWO // 2:])
    r1, r2, r3, *last = together(
        *[y_shift(part, d + 1) for d, part in enumerate(sent)], *last, *third)
    last, third = last[:NX], last[NX:]
    second_grad = incoming + ((mine + r1) + (r2 + r3))
    rounded = second_grad.astype(BF16)

    sums_one = product(pos, for_one, third, [(3, [(i, 0, 2) for i in range(NX)])], sums_one)
    sums_one = product(
        pos, for_one, first_x + last,
        [(0, [(NX * s + i, 0, 1) for i in range(NX) for s in range(2)])], sums_one, BF16)
    where = tuple(
        ((i, 0),) + tuple((NX * (1 + j // 2) + i, j % 2) for j in range(7)) for i in range(NX))
    factors = factor(pos, inverse, inverse_other, first_x + near + middle + third + last, where)
    s1, s2, s3, mine, *sent = together(*[y_shift(rounded, d) for d in range(1, NY)], *sums_one)
    rounded = jnp.stack([rounded, s1, s2, s3])
    rounded_other = core_swap(rounded)
    r1, r2, r3 = [y_shift(part, d + 1).astype(F32) for d, part in enumerate(sent)]
    term = carried(rounded, rounded_other, *factors)
    return second_grad, (mine + r1) + (r2 + r3) - term


def solution(mesh):
    in_specs = (
        P("row", "col"),
        P(),
        P(("row", "col"), None),
        P(("row", "col"), None),
        P("col", "row"),
        P("row", None),
    )
    out_specs = (P("col", "row"), P("col", "row"))
    return jax.shard_map(local, mesh=mesh, in_specs=in_specs, out_specs=out_specs, check_vma=False)
```
